32 devices in a mesh: ctx: 8 (over z, y), fsdp: 4 (over x, core).
Axes of the slice: x: 2, y: 2, z: 4, core: 2. Of those that a mesh axis runs over, the one named last changes fastest.
Arguments:
- tokens: bfloat16 [4, 4096, 768], P('fsdp', 'ctx'), may hold values from -6 to 6
- cotangent: bfloat16 [4, 4096, 768], P('fsdp', 'ctx'), may hold values from -6 to 6
- pair_table: int32 [4, 8, 2], P('fsdp', 'ctx'), may hold values from 0 to 15, as said below
- seq_ids: int32 [4, 16], P('fsdp'), may hold values from 0 to 1, as said below
- first_gain: bfloat16 [768], P('fsdp'), may hold values from 0.5 to 1.5
- first_shift: bfloat16 [768], P('fsdp'), may hold values from -0.59765625 to 0.59765625
- project_weight: bfloat16 [768, 2304], P(None, 'fsdp'), may hold values from -0.21875 to 0.21875
- project_bias: bfloat16 [2304], P('fsdp'), may hold values from -0.059814453 to 0.059814453
- feature_query: bfloat16 [12, 64, 64], P('fsdp'), may hold values from -1.5 to 1.5
- feature_key: bfloat16 [12, 64, 64], P('fsdp'), may hold values from -1.5 to 1.5
- output_weight: bfloat16 [768, 768], P('fsdp'), may hold values from -9 to 9
- output_bias: bfloat16 [768], P('fsdp'), may hold values from -0.59765625 to 0.59765625
- second_gain: bfloat16 [768], P('fsdp'), may hold values from 0.5 to 1.5
- second_shift: bfloat16 [768], P('fsdp'), may hold values from -0.59765625 to 0.59765625
- expand_weight: bfloat16 [768, 3072], P(None, 'fsdp'), may hold values from -0.21875 to 0.21875
- expand_bias: bfloat16 [3072], P('fsdp'), may hold values from -0.59765625 to 0.59765625
- reduce_weight: bfloat16 [3072, 768], P('fsdp'), may hold values from -0.109375 to 0.109375
- reduce_bias: bfloat16 [768], P('fsdp'), may hold values from -0.59765625 to 0.59765625
Outputs:
- layer_output: float32 [4, 4096, 768], P('fsdp', 'ctx')
- input_grad: float32 [4, 4096, 768], P('fsdp', 'ctx')
- grad_first_gain: float32 [768], P('fsdp')
- grad_first_shift: float32 [768], P('fsdp')
- grad_project_weight: float32 [768, 2304], P(None, 'fsdp')
- grad_project_bias: float32 [2304], P('fsdp')
- grad_feature_query: float32 [12, 64, 64], P('fsdp')
- grad_feature_key: float32 [12, 64, 64], P('fsdp')
- grad_output_weight: float32 [768, 768], P('fsdp')
- grad_output_bias: float32 [768], P('fsdp')
- grad_second_gain: float32 [768], P('fsdp')
- grad_second_shift: float32 [768], P('fsdp')
- grad_expand_weight: float32 [768, 3072], P(None, 'fsdp')
- grad_expand_bias: float32 [3072], P('fsdp')
- grad_reduce_weight: float32 [3072, 768], P('fsdp')
- grad_reduce_bias: float32 [768], P('fsdp')
The draws below stay inside these ranges and needn't reach their ends.
Inputs may be any that keep to these rules, and one draw needn't show every extreme that they name: `pair_table`: at ctx index c of a group, slots 0 and 1 hold blocks c and 15 - c in either order. `seq_ids`: each group's blocks hold 2 sequences, ids 0 then 1 in block order; sequence 0 has 4 to 12 blocks.
All inputs are finite; a program needn't handle non-finite values.
Results may differ from the reference program's by a relative error of at most 0.019.
Values may be sent and summed in bfloat16 or wider, within the bound.
No kernel may reach another device: no remote copies, remote signals or barrier semaphores. Data moves between devices by JAX's collectives and lax.ppermute only.
A program may use at most 256 MiB of HBM per device.

```python
import jax
import jax.numpy as jnp
from jax import lax

D = 768
H = 12
HD = 64
FF = 3072
BLOCKS = 16
ROWS = 4096
GROUPS = 4


def draw_pair_table(key, part):
    half = BLOCKS // 2
    flips = jax.random.randint(key, (GROUPS, half), 0, 2)
    place = jnp.arange(half, dtype=jnp.int32)[None, :] + jnp.zeros((GROUPS, half), jnp.int32)
    low_one = place
    high_one = BLOCKS - 1 - place
    first_a = jnp.where(flips == 1, high_one, low_one)
    second_a = jnp.where(flips == 1, low_one, high_one)
    return jnp.stack([first_a, second_a], axis=-1).astype(jnp.int32)


def draw_seq_ids(key, part):
    cuts = jax.random.randint(key, (GROUPS, 1), BLOCKS // 4, 3 * BLOCKS // 4 + 1)
    order = jnp.arange(BLOCKS, dtype=jnp.int32)[None, :]
    return (order >= cuts).astype(jnp.int32)


def level_of(stream_key, dims, pieces, low, top_value):
    level, own = 1.0, jax.random.fold_in(stream_key, 6)
    for dim, shards_of in pieces:
        steps = jnp.exp(jax.random.uniform(jax.random.fold_in(own, dim), (shards_of,), jnp.float32, low / len(pieces), top_value / len(pieces)))
        level = level * jnp.repeat(steps, dims[dim] // shards_of).reshape([-1 if axis == dim else 1 for axis in range(len(dims))])
    return level


def noise(stream_key, extent, deviation, limit, pieces=(), kind=jnp.bfloat16):
    drawn = deviation * jax.random.normal(stream_key, extent, jnp.float32)
    if pieces:
        drawn = drawn * level_of(stream_key, extent, pieces, -0.22, 0.18)
    return jnp.clip(drawn, -limit, limit).astype(kind)


def setup_inputs(seed: int = 0) -> dict:
    streams_of = jax.random.split(jax.random.key(seed), 19)
    return {
        "tokens": noise(streams_of[0], (GROUPS, ROWS, D), 1.0, 6.0, ((0, 4), (1, 8))),
        "cotangent": noise(streams_of[1], (GROUPS, ROWS, D), 1.0, 6.0, ((0, 4), (1, 8))),
        "pair_table": draw_pair_table(jax.random.fold_in(streams_of[18], 71), 0),
        "seq_ids": draw_seq_ids(jax.random.fold_in(streams_of[18], 71), 0),
        "first_gain": jnp.clip(1.0 + 0.1 * jax.random.normal(streams_of[4], (D,), jnp.float32), 0.5, 1.5).astype(jnp.bfloat16),
        "first_shift": noise(streams_of[5], (D,), 0.1, 0.59765625, ((0, 4),)),
        "project_weight": noise(streams_of[6], (D, 3 * D), D ** -0.5, 0.21875, ((1, 4),)),
        "project_bias": noise(streams_of[7], (3 * D,), 0.01, 0.059814453, ((0, 4),)),
        "feature_query": noise(streams_of[8], (H, HD, HD), (HD // 4) ** -0.5, 1.5, ((0, 4),)),
        "feature_key": noise(streams_of[9], (H, HD, HD), (HD // 4) ** -0.5, 1.5, ((0, 4),)),
        "output_weight": noise(streams_of[10], (D, D), 1.5, 9.0, ((0, 4),)),
        "output_bias": noise(streams_of[11], (D,), 0.1, 0.59765625, ((0, 4),)),
        "second_gain": jnp.clip(1.0 + 0.1 * jax.random.normal(streams_of[12], (D,), jnp.float32), 0.5, 1.5).astype(jnp.bfloat16),
        "second_shift": noise(streams_of[13], (D,), 0.1, 0.59765625, ((0, 4),)),
        "expand_weight": noise(streams_of[14], (D, FF), D ** -0.5, 0.21875, ((1, 4),)),
        "expand_bias": noise(streams_of[15], (FF,), 0.1, 0.59765625, ((0, 4),)),
        "reduce_weight": noise(streams_of[16], (FF, D), FF ** -0.5, 0.109375, ((0, 4),)),
        "reduce_bias": noise(streams_of[17], (D,), 0.1, 0.59765625, ((0, 4),)),
    }


EPS = 1e-05
HIGH = lax.Precision.HIGHEST

@jax.custom_vjp
def low(v):
    return lax.optimization_barrier(v.astype(jnp.bfloat16)).astype(jnp.float32)

@jax.custom_vjp
def low_back(v):
    return v

def low_keep(v):
    return (low(v), None)

def low_pass(kept, grad):
    return (grad,)

def back_keep(v):
    return (v, None)

def back_low(kept, grad):
    return (low(grad),)
low.defvjp(low_keep, low_pass)
low_back.defvjp(back_keep, back_low)

def layer_norm(rows_in, gains, shift):
    center = rows_in - lax.optimization_barrier(jnp.mean(rows_in, axis=-1, keepdims=True))
    spread = lax.optimization_barrier(jnp.mean(center * center, axis=-1, keepdims=True))
    return center * lax.rsqrt(spread + EPS) * gains + shift

def features(logits):
    return jnp.concatenate([jax.nn.softmax(logits, axis=-1), jax.nn.softmax(-logits, axis=-1)], axis=-1)

def key_states(block_rows, params):
    first_gain, first_shift, project_weight, project_bias, feature_query, feature_key, output_weight, output_bias, second_gain, second_shift, expand_weight, expand_bias, reduce_weight, reduce_bias = params
    width = block_rows.shape[1]
    heads = feature_key.shape[0]
    head_dim = width // heads
    rounded = low(layer_norm(block_rows, first_gain, first_shift))
    kv_rows = jnp.dot(rounded, project_weight[:, width:], precision=HIGH) + project_bias[width:]
    key_rows = low(low_back(kv_rows[:, :width])).reshape(-1, heads, head_dim)
    value_rows = low(low_back(kv_rows[:, width:])).reshape(-1, heads, head_dim)
    key_logits = low_back(jnp.einsum('bhd,hde->bhe', key_rows, feature_key, precision=HIGH))
    key_feats = low(low_back(features(key_logits)))
    states = low_back(jnp.einsum('bhf,bhd->hfd', key_feats, value_rows, precision=HIGH))
    norms = lax.optimization_barrier(jnp.sum(key_feats, axis=0))
    return (states, norms)

def block_output(block_rows, state_in, norm_in, params):
    first_gain, first_shift, project_weight, project_bias, feature_query, feature_key, output_weight, output_bias, second_gain, second_shift, expand_weight, expand_bias, reduce_weight, reduce_bias = params
    rows_n, width = block_rows.shape
    heads = feature_query.shape[0]
    head_dim = width // heads
    rounded = low(layer_norm(block_rows, first_gain, first_shift))
    query_rows = jnp.dot(rounded, project_weight[:, :width], precision=HIGH) + project_bias[:width]
    queries = low(low_back(query_rows)).reshape(rows_n, heads, head_dim)
    query_logits = low_back(jnp.einsum('bhd,hde->bhe', queries, feature_query, precision=HIGH))
    query_feats = low(low_back(features(query_logits)))
    numer = low_back(jnp.einsum('bhf,hfd->bhd', query_feats, low(state_in), precision=HIGH))
    denom = low_back(jnp.einsum('bhf,hf->bh', query_feats, low(norm_in), precision=HIGH))
    mixed = low(low_back((numer / denom[..., None]).reshape(rows_n, width)))
    attended = low_back(jnp.dot(mixed, output_weight, precision=HIGH) + output_bias)
    middle = block_rows + attended
    normed_two = low(layer_norm(middle, second_gain, second_shift))
    hidden = low_back(jnp.dot(normed_two, expand_weight, precision=HIGH) + expand_bias)
    active = low(low_back(jax.nn.gelu(hidden, approximate=True)))
    return middle + low_back(jnp.dot(active, reduce_weight, precision=HIGH) + reduce_bias)

def group_forward(block_rows, params, carry_mult):

    def states_of(rows_in):
        return key_states(rows_in, params)
    states, norms = lax.map(jax.checkpoint(states_of), block_rows)

    def accumulate(carry, item):
        run_state, run_norm = carry
        mult, state, norm = item
        run_state = mult * run_state + state
        run_norm = mult * run_norm + norm
        return ((run_state, run_norm), (run_state, run_norm))
    start = (jnp.zeros(states.shape[1:], jnp.float32), jnp.zeros(norms.shape[1:], jnp.float32))
    _, (incl_states, incl_norms) = lax.scan(accumulate, start, (carry_mult, states, norms))

    def output_of(item):
        return block_output(item[0], item[1], item[2], params)
    return lax.map(jax.checkpoint(output_of), (block_rows, incl_states, incl_norms))

def reference(tokens, cotangent, pair_table, seq_ids, first_gain, first_shift, project_weight, project_bias, feature_query, feature_key, output_weight, output_bias, second_gain, second_shift, expand_weight, expand_bias, reduce_weight, reduce_bias):
    params = tuple((param.astype(jnp.float32) for param in (first_gain, first_shift, project_weight, project_bias, feature_query, feature_key, output_weight, output_bias, second_gain, second_shift, expand_weight, expand_bias, reduce_weight, reduce_bias)))
    groups, rows, width = tokens.shape
    blocks = seq_ids.shape[1]
    block_len = rows // blocks
    nctx = pair_table.shape[1]
    lanes_all = blocks // nctx
    half_lanes = lanes_all // 2

    def one_group(totals, item):
        rows_in, cot_in, table, ids = item
        order = jnp.arange(blocks, dtype=jnp.int32)
        lane = (order // nctx).astype(jnp.int32)
        within = (order % nctx).astype(jnp.int32)
        owner = jnp.where(lane < half_lanes, within, nctx - 1 - within).astype(jnp.int32)
        pair = jnp.where(lane < half_lanes, lane, lanes_all - 1 - lane).astype(jnp.int32)
        second_slot = (table[owner, 2 * pair + 1] == order).astype(jnp.int32)
        store = (lanes_all * owner + 2 * pair + second_slot).astype(jnp.int32)
        block_rows = rows_in.astype(jnp.float32).reshape(blocks, block_len, width)[store]
        block_cot = cot_in.astype(jnp.float32).reshape(blocks, block_len, width)[store]
        starts = jnp.concatenate([jnp.ones((1,), jnp.float32), (ids[1:] != ids[:-1]).astype(jnp.float32)])
        carry_mult = 1.0 - starts

        def forward(block_in, params_in):
            return group_forward(block_in, params_in, carry_mult)
        outputs, pullback = jax.vjp(forward, block_rows, params)
        grad_rows, grad_params = pullback(block_cot)
        back_index = table.reshape(-1).astype(jnp.int32)
        out_store = outputs[back_index].reshape(rows, width)
        grad_store = grad_rows[back_index].reshape(rows, width)
        totals = tuple((total + grad for total, grad in zip(totals, grad_params)))
        return (totals, (out_store, grad_store))
    zeros = tuple((jnp.zeros(param.shape, jnp.float32) for param in params))
    totals, (outs, grads) = lax.scan(one_group, zeros, (tokens, cotangent, pair_table, seq_ids))
    return (outs, grads, totals[0], totals[1], totals[2], totals[3], totals[4], totals[5], totals[6], totals[7], totals[8], totals[9], totals[10], totals[11], totals[12], totals[13])
```

```python
import functools

import jax
import jax.numpy as jnp
from jax import lax
from jax.experimental import pallas as pl
from jax.experimental.pallas import tpu as pltpu
from jax.sharding import PartitionSpec as P

EPS = 1e-05
F32 = jnp.float32
BF16 = jnp.bfloat16
AUG = 80
KEEP = 72
NN = (((1,), (0,)), ((), ()))
NT = (((1,), (1,)), ((), ()))
TN = (((0,), (0,)), ((), ()))
CORE = [(i, i ^ 1) for i in range(4)]
CROSS = [(i, i ^ 2) for i in range(4)]
VMEM = pl.BlockSpec(memory_space=pltpu.VMEM)
SMEM = pl.BlockSpec(memory_space=pltpu.SMEM)


def mm(a, b, dims):
    return lax.dot_general(a, b, dims, preferred_element_type=F32)


def call(kernel, outs, kinds, args, flops, name, scratch=(), aliases=None):
    size = sum(a.size * a.dtype.itemsize for a in args)
    size += sum(o.size * o.dtype.itemsize for o in outs)
    return pl.pallas_call(
        kernel,
        out_shape=outs,
        in_specs=[SMEM if k == "s" else VMEM for k in kinds],
        out_specs=[VMEM] * len(outs),
        scratch_shapes=list(scratch),
        input_output_aliases=aliases or {},
        compiler_params=pltpu.CompilerParams(vmem_limit_bytes=40 << 20),
        cost_estimate=pl.CostEstimate(flops=flops, bytes_accessed=size, transcendentals=0),
        name=name,
    )(*args)


def shaped(shape, dtype=F32):
    return jax.ShapeDtypeStruct(shape, dtype)


def norm_parts(v):
    center = v - jnp.mean(v, axis=-1, keepdims=True)
    scale = lax.rsqrt(jnp.mean(center * center, axis=-1, keepdims=True) + EPS)
    return center * scale, scale


def norm_back(gy, normal, scale, gain):
    a = gy * gain
    return (
        a - jnp.mean(a, axis=-1, keepdims=True)
        - normal * jnp.mean(a * normal, axis=-1, keepdims=True)
    ) * scale


def aug_rows(top, row):
    index = lax.broadcasted_iota(jnp.int32, (AUG - top.shape[0], top.shape[1]), 0)
    tail = jnp.where(index == 0, row, 0.0).astype(BF16)
    return jnp.concatenate([top, tail], axis=0)


def spread_states(total_ref, out_ref, parts, rows_per):
    for part in range(parts):
        out_ref[part] = total_ref[:, part * rows_per : (part + 1) * rows_per, :].astype(BF16)


def collect_states(in_ref, total_ref, parts, rows_per):
    for part in range(parts):
        total_ref[:, part * rows_per : (part + 1) * rows_per, :] = in_ref[part].astype(F32)


def project_kernel(meta, x_ref, p_ref, w0, w1, w2, w3, pb_ref, qkv_ref):
    normal, _ = norm_parts(x_ref[...].astype(F32))
    n = (normal * p_ref[0:1] + p_ref[1:2]).astype(BF16)
    cols = w0.shape[1]
    for j, w in enumerate((w0, w1, w2, w3)):
        out = mm(n, w[...], NN) + pb_ref[j : j + 1]
        start = pl.multiple_of(meta[j] * cols, 64)
        qkv_ref[pl.ds(start, cols), :] = out.astype(BF16).T


def phi(rows_ref, base, map_ref, h):
    rows = rows_ref[pl.ds(pl.multiple_of(base + h * 64, 64), 64), :]
    logits = mm(map_ref[h], rows, TN)
    up = jnp.exp(logits - jnp.max(logits, axis=0, keepdims=True))
    down = jnp.exp(jnp.min(logits, axis=0, keepdims=True) - logits)
    p1 = up / jnp.sum(up, axis=0, keepdims=True)
    p2 = down / jnp.sum(down, axis=0, keepdims=True)
    return p1.astype(BF16), p2.astype(BF16)


def key_kernel(heads, slots, parts, meta, qkv_ref, map_ref, fk_ref, s_ref, total):
    width = heads * 64
    cols = qkv_ref.shape[1] // slots
    rows_per = s_ref.shape[2]
    total[...] = jnp.zeros_like(total)

    def head(h, carry):
        p1, p2 = phi(qkv_ref, width, map_ref, h)
        at = pl.multiple_of(h * 128, 128)
        fk_ref[pl.ds(at, 64), :] = p1
        fk_ref[pl.ds(pl.multiple_of(at + 64, 64), 64), :] = p2
        v = qkv_ref[pl.ds(pl.multiple_of(2 * width + h * 64, 64), 64), :]
        va = aug_rows(v, 1.0)
        fk = jnp.concatenate([p1, p2], axis=0)
        for s in range(slots):
            part = slice(s * cols, (s + 1) * cols)
            state = mm(va[:, part], fk[:, part], NT)
            total[s ^ meta[4], pl.ds(pl.multiple_of(h * KEEP, 8), KEEP), :] = state[:KEEP]
        return carry

    lax.fori_loop(0, heads, head, 0)
    spread_states(total, s_ref, parts, rows_per)


def query_kernel(heads, qkv_ref, map_ref, fq_ref):
    def head(h, carry):
        p1, p2 = phi(qkv_ref, 0, map_ref, h)
        at = pl.multiple_of(h * 128, 128)
        fq_ref[pl.ds(at, 64), :] = p1
        fq_ref[pl.ds(pl.multiple_of(at + 64, 64), 64), :] = p2
        return carry

    lax.fori_loop(0, heads, head, 0)


def scan_kernel(nctx, backward, keep, in_ref, out_ref):
    blocks = 2 * nctx
    order = [(b, 0) if b < nctx else (blocks - 1 - b, 1) for b in range(blocks)]
    acc = jnp.zeros(in_ref.shape[2:], F32)
    for b in reversed(range(blocks)) if backward else range(blocks):
        c, lane = order[b]
        acc = acc * keep[b] + in_ref[c, lane].astype(F32)
        out_ref[c, lane] = acc.astype(BF16)


def fill_output(meta, wo_refs, wo):
    rows = wo_refs[0].shape[0]
    for j, ref in enumerate(wo_refs):
        wo[pl.ds(pl.multiple_of(meta[j] * rows, 64), rows), :] = ref[...]


def attend_kernel(
    heads, slots, parts, meta, c_ref, fq_ref, x_ref, w0, w1, w2, w3, p_ref,
    mixed_ref, den_ref, middle_ref, n2_ref, n2t_ref, total, wo,
):
    cols = fq_ref.shape[1] // slots
    collect_states(c_ref, total, parts, c_ref.shape[2])
    fill_output(meta, (w0, w1, w2, w3), wo)

    def head(h, carry):
        fq = fq_ref[pl.ds(pl.multiple_of(h * 128, 128), 128), :]
        for s in range(slots):
            part = slice(s * cols, (s + 1) * cols)
            c = total[s ^ meta[4], pl.ds(pl.multiple_of(h * KEEP, 8), AUG), :].astype(BF16)
            both = mm(c, fq[:, part], NN)
            den = both[64:65]
            mixed_ref[pl.ds(pl.multiple_of(h * 64, 64), 64), part] = (both[:64] / den).astype(BF16)
            den_ref[pl.ds(pl.multiple_of(h * 8, 8), 8), part] = jnp.broadcast_to(den, (8, cols))
        return carry

    lax.fori_loop(0, heads, head, 0)
    middle = x_ref[...].astype(F32) + mm(mixed_ref[...], wo[...], TN) + p_ref[4:5]
    middle_ref[...] = middle
    normal, _ = norm_parts(middle)
    n2 = (normal * p_ref[2:3] + p_ref[3:4]).astype(BF16)
    n2_ref[...] = n2
    n2t_ref[...] = n2.T


def mlp_kernel(
    tile, n2_ref, n2t_ref, cot_ref, base_ref, back_ref, eb_ref, wea, wra, web, wrb,
    out_ref, dn_ref, gea, gra, geb, grb, gb_ref,
):
    out_ref[...] = base_ref[...]
    dn_ref[...] = back_ref[...]
    for j, (we, wr, ge, gr) in enumerate(((wea, wra, gea, gra), (web, wrb, geb, grb))):

        def step(t, carry):
            at = pl.ds(pl.multiple_of(t * tile, tile), tile)
            w_in = we[:, at]
            w_out = wr[at, :]
            cot = cot_ref[...]
            hidden = mm(n2_ref[...], w_in, NN) + eb_ref[j : j + 1, at]
            square = hidden * hidden
            inner = 0.7978845608028654 * hidden * (1.0 + 0.044715 * square)
            tanh = jnp.tanh(inner)
            half = 0.5 * (1.0 + tanh)
            active = (hidden * half).astype(BF16)
            slope = half + 0.5 * hidden * (1.0 - tanh * tanh) * (
                0.7978845608028654 * (1.0 + 0.134145 * square)
            )
            r_active = mm(cot, w_out, NT).astype(BF16).astype(F32)
            r_hidden32 = (r_active * slope).astype(BF16)
            out_ref[...] += mm(active, w_out, NN)
            dn_ref[...] += mm(r_hidden32, w_in, NT)
            gr[at, :] = mm(active, cot, TN).astype(BF16)
            ge[:, at] = mm(n2t_ref[...], r_hidden32, NN).astype(BF16)
            gb_ref[8 * j : 8 * j + 8, at] = jnp.broadcast_to(
                jnp.sum(r_hidden32.astype(F32), axis=0, keepdims=True), (8, tile)
            )
            return carry

        lax.fori_loop(0, we.shape[1] // tile, step, 0)


def middle_kernel(
    heads, slots, parts, meta, dn_ref, middle_ref, cot_ref, p_ref, mixed_ref, den_ref, fq_ref,
    w0, w1, w2, w3, gm_ref, ratt_ref, raug_ref, g_ref, small_ref, total, wo, rmix,
):
    cols = fq_ref.shape[1] // slots
    fill_output(meta, (w0, w1, w2, w3), wo)
    normal, scale = norm_parts(middle_ref[...])
    gy = dn_ref[...]
    cot = cot_ref[...].astype(F32)
    g_middle = cot + norm_back(gy, normal, scale, p_ref[2:3])
    gm_ref[...] = g_middle
    r_att = g_middle.astype(BF16)
    ratt_ref[...] = r_att
    small_ref[...] = jnp.concatenate(
        [
            jnp.sum(gy * normal, axis=0, keepdims=True),
            jnp.sum(gy, axis=0, keepdims=True),
            jnp.sum(r_att.astype(F32), axis=0, keepdims=True),
            jnp.sum(cot, axis=0, keepdims=True),
            jnp.zeros((4, gy.shape[1]), F32),
        ],
        axis=0,
    )
    rmix[...] = mm(wo[...], r_att, NT).astype(BF16)
    total[...] = jnp.zeros_like(total)

    def head(h, carry):
        rows = pl.ds(pl.multiple_of(h * 64, 64), 64)
        rm = rmix[rows, :].astype(F32)
        inverse = 1.0 / den_ref[pl.ds(pl.multiple_of(h * 8, 8), 8), :][0:1]
        rn = (rm * inverse).astype(BF16)
        rd = -jnp.sum(rm * mixed_ref[rows, :].astype(F32), axis=0, keepdims=True) * inverse
        ra = aug_rows(rn, rd)
        raug_ref[pl.ds(pl.multiple_of(h * AUG, 16), AUG), :] = ra
        fq = fq_ref[pl.ds(pl.multiple_of(h * 128, 128), 128), :]
        for s in range(slots):
            part = slice(s * cols, (s + 1) * cols)
            state = mm(ra[:, part], fq[:, part], NT)
            total[s ^ meta[4], pl.ds(pl.multiple_of(h * KEEP, 8), KEEP), :] = state[:KEEP]
        return carry

    lax.fori_loop(0, heads, head, 0)
    spread_states(total, g_ref, parts, g_ref.shape[2])


def logits_back(p_both, g_both):
    p1, p2 = p_both[:64].astype(F32), p_both[64:].astype(F32)
    g1, g2 = g_both[:64], g_both[64:]
    s1 = jnp.sum(p1 * g1, axis=0, keepdims=True)
    s2 = jnp.sum(p2 * g2, axis=0, keepdims=True)
    return (p1 * (g1 - s1) - p2 * (g2 - s2)).astype(BF16)


def query_back_kernel(
    heads, slots, parts, meta, c_ref, raug_ref, fq_ref, qkv_ref, map_ref, mixed_ref, ratt_ref,
    rq_ref, gmap_ref, g0, g1, g2, g3, total,
):
    cols = fq_ref.shape[1] // slots
    collect_states(c_ref, total, parts, c_ref.shape[2])

    def head(h, carry):
        ra = raug_ref[pl.ds(pl.multiple_of(h * AUG, 16), AUG), :]
        fq = fq_ref[pl.ds(pl.multiple_of(h * 128, 128), 128), :]
        pieces = []
        for s in range(slots):
            part = slice(s * cols, (s + 1) * cols)
            c = total[s ^ meta[4], pl.ds(pl.multiple_of(h * KEEP, 8), AUG), :].astype(BF16)
            pieces.append(mm(c, ra[:, part], TN))
        r_fq = jnp.concatenate(pieces, axis=1).astype(BF16).astype(F32)
        r_l = logits_back(fq, r_fq)
        rows = pl.ds(pl.multiple_of(h * 64, 64), 64)
        rq_ref[rows, :] = mm(map_ref[h], r_l, NN).astype(BF16)
        gmap_ref[h] = mm(qkv_ref[rows, :], r_l, NT)
        return carry

    lax.fori_loop(0, heads, head, 0)
    rows = g0.shape[0]
    for j, g in enumerate((g0, g1, g2, g3)):
        mixed = mixed_ref[pl.ds(pl.multiple_of(meta[j] * rows, 64), rows), :]
        g[...] = mm(mixed, ratt_ref[...], NN).astype(BF16)


def key_back_kernel(
    heads, slots, parts, meta, d_ref, fk_ref, qkv_ref, map_ref, rq_ref, x_ref, p_ref,
    rp_ref, gmap_ref, g0, g1, g2, g3, gpb_ref, total,
):
    width = heads * 64
    cols = fk_ref.shape[1] // slots
    collect_states(d_ref, total, parts, d_ref.shape[2])
    rp_ref[0:width, :] = rq_ref[...]

    def head(h, carry):
        fk = fk_ref[pl.ds(pl.multiple_of(h * 128, 128), 128), :]
        v = qkv_ref[pl.ds(pl.multiple_of(2 * width + h * 64, 64), 64), :]
        va = aug_rows(v, 1.0)
        pieces = []
        for s in range(slots):
            part = slice(s * cols, (s + 1) * cols)
            d = total[s ^ meta[4], pl.ds(pl.multiple_of(h * KEEP, 8), AUG), :].astype(BF16)
            pieces.append(mm(d, va[:, part], TN))
            rv = mm(d[:64], fk[:, part], NN).astype(BF16)
            rp_ref[pl.ds(pl.multiple_of(2 * width + h * 64, 64), 64), part] = rv
        r_fk = jnp.concatenate(pieces, axis=1).astype(BF16).astype(F32)
        r_l = logits_back(fk, r_fk)
        rows = pl.ds(pl.multiple_of(width + h * 64, 64), 64)
        rp_ref[rows, :] = mm(map_ref[h], r_l, NN).astype(BF16)
        gmap_ref[h] = mm(qkv_ref[rows, :], r_l, NT)
        return carry

    lax.fori_loop(0, heads, head, 0)
    normal, _ = norm_parts(x_ref[...].astype(F32))
    nt = (normal * p_ref[0:1] + p_ref[1:2]).astype(BF16).T
    span = g0.shape[1]
    ones = jnp.ones((8, x_ref.shape[0]), BF16)
    for j, g in enumerate((g0, g1, g2, g3)):
        rp = rp_ref[pl.ds(pl.multiple_of(meta[j] * span, 64), span), :]
        g[...] = mm(nt, rp, NT).astype(BF16)
        gpb_ref[8 * j : 8 * j + 8, :] = mm(ones, rp, NT)


def input_kernel(meta, rp_ref, x_ref, p_ref, gm_ref, w0, w1, w2, w3, dx_ref, small_ref):
    span = w0.shape[1]
    back = None
    for j, w in enumerate((w0, w1, w2, w3)):
        rp = rp_ref[pl.ds(pl.multiple_of(meta[j] * span, 64), span), :]
        part = mm(w[...], rp, NN)
        back = part if back is None else back + part
    gy = back.T
    normal, scale = norm_parts(x_ref[...].astype(F32))
    dx_ref[...] = gm_ref[...] + norm_back(gy, normal, scale, p_ref[0:1])
    small_ref[...] = jnp.concatenate(
        [
            jnp.sum(gy * normal, axis=0, keepdims=True),
            jnp.sum(gy, axis=0, keepdims=True),
            jnp.zeros((6, gy.shape[1]), F32),
        ],
        axis=0,
    )


def core_swap(a):
    return lax.ppermute(a, "fsdp", CORE)


def cross_swap(a):
    return lax.ppermute(a, "fsdp", CROSS)


def gather(shard):
    cross = cross_swap(shard)
    return [shard, core_swap(shard), cross, core_swap(cross)]


def add(a, b):
    return (a.astype(F32) + b.astype(F32)).astype(BF16)


def scatter_group(own, core, cross, far):
    far_in = core_swap(far)
    core_in = core_swap(core)
    cross_in = cross_swap(add(cross, far_in))
    return add(add(own, core_in), cross_in)


def sum_ctx(a, nctx, place):
    bits = nctx.bit_length() - 1
    cur = a
    for bit in range(bits):
        half = cur.shape[0] // 2
        mine = (place >> bit) & 1
        pairs = [(i, i ^ (1 << bit)) for i in range(nctx)]
        sent = lax.dynamic_slice_in_dim(cur, (1 - mine) * half, half, 0)
        kept = lax.dynamic_slice_in_dim(cur, mine * half, half, 0)
        cur = add(kept, lax.ppermute(sent, "ctx", pairs))
    for bit in reversed(range(bits)):
        mine = (place >> bit) & 1
        pairs = [(i, i ^ (1 << bit)) for i in range(nctx)]
        other = lax.ppermute(cur, "ctx", pairs)
        first = mine == 0
        cur = jnp.concatenate([jnp.where(first, cur, other), jnp.where(first, other, cur)], axis=0)
    return cur


def exchange(a):
    return lax.all_to_all(a, "ctx", 0, 0, tiled=True)


def straighten(parts, mine):
    a, b, c, d = parts
    odd = (mine & 1) == 1
    upper = (mine & 2) == 2
    a, b = jnp.where(odd, b, a), jnp.where(odd, a, b)
    c, d = jnp.where(odd, d, c), jnp.where(odd, c, d)
    return [
        jnp.where(upper, c, a), jnp.where(upper, d, b),
        jnp.where(upper, a, c), jnp.where(upper, b, d),
    ]


def body(
    tokens, cotangent, pair_table, seq_ids, first_gain, first_shift, project_weight, project_bias,
    feature_query, feature_key, output_weight, output_bias, second_gain, second_shift,
    expand_weight, expand_bias, reduce_weight, reduce_bias,
):
    x = tokens[0]
    cot = cotangent[0]
    rows_n, width = x.shape
    heads = width // feature_query.shape[1]
    own_heads = feature_query.shape[0]
    slots = pair_table.shape[2]
    nctx = lax.axis_size("ctx")
    place = lax.axis_index("ctx")
    mine = lax.axis_index("fsdp")
    span = project_weight.shape[1]
    hidden_own = expand_weight.shape[1]
    shard = width // 4
    wide = heads * 128

    vector = jnp.concatenate(
        [first_gain, first_shift, second_gain, second_shift, output_bias, reduce_bias,
         project_bias, expand_bias]
    )
    pack = jnp.concatenate(
        [feature_query.reshape(-1, 64), feature_key.reshape(-1, 64), vector.reshape(-1, 64)]
    )
    packs = gather(pack)
    projects = gather(project_weight)
    held = lax.optimization_barrier(
        (output_weight, expand_weight, reduce_weight, projects[2])
    )
    outputs = gather(held[0])
    expands = gather(held[1])
    held = lax.optimization_barrier((held[2], expands[2]))
    reduces = gather(held[0])

    map_rows = own_heads * 64
    vectors = [p[2 * map_rows :].reshape(-1) for p in packs]
    ordered = straighten(packs, mine)
    query_map = jnp.concatenate([p[:map_rows] for p in ordered]).reshape(heads, 64, 64)
    key_map = jnp.concatenate([p[map_rows : 2 * map_rows] for p in ordered]).reshape(heads, 64, 64)
    lines = jnp.stack([p[2 * map_rows :].reshape(-1)[: 6 * shard] for p in ordered])
    params = lines.reshape(4, 6, shard).transpose(1, 0, 2).reshape(6, width).astype(F32)
    params = jnp.concatenate([params, jnp.zeros((2, width), F32)])
    project_line = jnp.stack([v[6 * shard : 6 * shard + span] for v in vectors]).astype(F32)
    expand_line = jnp.stack([v[6 * shard + span :] for v in vectors]).astype(F32)

    positions = pair_table[0, 0]
    swap = (positions[0] > positions[1]).astype(jnp.int32)
    meta = jnp.stack([mine, mine ^ 1, mine ^ 2, mine ^ 3, swap]).astype(jnp.int32)
    ids = seq_ids[0]
    same = (ids[1:] == ids[:-1]).astype(F32)
    none = jnp.zeros((1,), F32)
    keep = jnp.concatenate([none, same])
    keep_next = jnp.concatenate([same, none])

    rows_per = -(-(heads * KEEP) // (nctx * 16)) * 16
    state_shape = shaped((nctx, slots, rows_per, 128), BF16)
    total = pltpu.VMEM((slots, nctx * rows_per, 128), F32)
    wo_scratch = pltpu.VMEM((width, width), BF16)
    dense = 2 * rows_n * width * width

    (qkv,) = call(
        project_kernel, [shaped((3 * width, rows_n), BF16)], "svvvvvvv",
        [meta, x, params, *projects, project_line], 3 * dense, "project",
    )
    fk, states = call(
        functools.partial(key_kernel, heads, slots, nctx),
        [shaped((wide, rows_n), BF16), state_shape], "svv", [meta, qkv, key_map], dense // 4, "keys",
        [total],
    )
    arrived = exchange(states)
    (fq,) = call(
        functools.partial(query_kernel, heads), [shaped((wide, rows_n), BF16)], "vv",
        [qkv, query_map], dense // 4, "queries",
    )
    (running,) = call(
        functools.partial(scan_kernel, nctx, False), [state_shape], "sv", [keep, arrived], 0, "scan",
    )
    carried = exchange(running)
    mixed, den, middle, n2, n2t = call(
        functools.partial(attend_kernel, heads, slots, nctx),
        [shaped((width, rows_n), BF16), shaped((heads * 8, rows_n)), shaped((rows_n, width)),
         shaped((rows_n, width), BF16), shaped((width, rows_n), BF16)],
        "svvvvvvvv", [meta, carried, fq, x, *outputs, params], dense * 2, "attend",
        [total, wo_scratch],
    )

    def mlp(base, back, a, b, name):
        lines = jnp.concatenate([expand_line[a : a + 1], expand_line[b : b + 1]])
        grad = shaped((width, hidden_own), BF16)
        grad_t = shaped((hidden_own, width), BF16)
        return call(
            functools.partial(mlp_kernel, 256),
            [shaped((rows_n, width)), shaped((rows_n, width)), grad, grad_t, grad, grad_t,
             shaped((16, hidden_own))],
            "vvvvvvvvvv",
            [n2, n2t, cot, base, back, lines, expands[a], reduces[a], expands[b], reduces[b]],
            12 * dense, name,
        )

    base = middle + params[5:6]
    out1, dn1, ge2, gr2, ge3, gr3, gb23 = mlp(base, jnp.zeros_like(base), 2, 3, "mlp_far")
    layer_out, dn2, ge0, gr0, ge1, gr1, gb01 = mlp(out1, dn1, 0, 1, "mlp_near")

    g_middle, r_att, raug, g_states, small_two = call(
        functools.partial(middle_kernel, heads, slots, nctx),
        [shaped((rows_n, width)), shaped((rows_n, width), BF16), shaped((heads * AUG, rows_n), BF16),
         state_shape, shaped((8, width))],
        "svvvvvvvvvvv", [meta, dn2, middle, cot, params, mixed, den, fq, *outputs], dense * 2, "middle",
        [total, wo_scratch, pltpu.VMEM((width, rows_n), BF16)],
    )
    g_arrived = exchange(g_states)
    rq, g_query_map, go0, go1, go2, go3 = call(
        functools.partial(query_back_kernel, heads, slots, nctx),
        [shaped((width, rows_n), BF16), shaped((heads, 64, 64))] + [shaped((shard, width), BF16)] * 4,
        "svvvvvvv", [meta, carried, raug, fq, qkv, query_map, mixed, r_att], dense * 2, "query_back",
        [total],
    )
    (g_running,) = call(
        functools.partial(scan_kernel, nctx, True), [state_shape], "sv", [keep_next, g_arrived], 0,
        "scan_back",
    )
    g_carried = exchange(g_running)
    rp, g_key_map, gp0, gp1, gp2, gp3, gpb = call(
        functools.partial(key_back_kernel, heads, slots, nctx),
        [shaped((3 * width, rows_n), BF16), shaped((heads, 64, 64))]
        + [shaped((width, span), BF16)] * 4 + [shaped((32, span))],
        "svvvvvvv", [meta, g_carried, fk, qkv, key_map, rq, x, params], dense * 4, "key_back",
        [total],
    )
    dx, small_one = call(
        input_kernel, [shaped((rows_n, width)), shaped((8, width))], "svvvvvvvv",
        [meta, rp, x, params, g_middle, *projects], dense * 3, "input",
    )

    g_expand = sum_ctx(scatter_group(ge0, ge1, ge2, ge3), nctx, place)
    g_reduce = sum_ctx(scatter_group(gr0, gr1, gr2, gr3), nctx, place)
    g_project = sum_ctx(scatter_group(gp0, gp1, gp2, gp3), nctx, place)

    lines = jnp.concatenate([small_one[:2], small_two[:4]]).reshape(6, 4, shard)
    lines = lines.transpose(1, 0, 2).reshape(4, 6 * shard)
    maps = jnp.concatenate(
        [g_query_map.reshape(4, -1), g_key_map.reshape(4, -1)], axis=1
    )
    tail = jnp.concatenate([lines, maps], axis=1)
    tail = straighten([tail[i] for i in range(4)], mine)
    bias_e = [gb01[0], gb01[8], gb23[0], gb23[8]]
    block_rows = 256
    blocks = []
    for j, go in enumerate((go0, go1, go2, go3)):
        flat = jnp.concatenate([tail[j], gpb[8 * j], bias_e[j]]).astype(BF16)
        room = (block_rows - shard) * width - flat.shape[0]
        flat = jnp.concatenate([flat, jnp.zeros((room,), BF16)]).reshape(-1, width)
        blocks.append(jnp.concatenate([go, flat]))
    rest = sum_ctx(scatter_group(*blocks), nctx, place)
    g_output = rest[:shard]
    flat = rest[shard:].reshape(-1).astype(F32)
    pieces = []
    at = 0
    for size in (shard,) * 6 + (own_heads * 4096,) * 2 + (span, hidden_own):
        pieces.append(flat[at : at + size])
        at += size
    g1, s1, g2, s2, bo, br, mq, mk, pb, eb = pieces
    return (
        layer_out[None], dx[None], g1, s1, g_project.astype(F32), pb,
        mq.reshape(own_heads, 64, 64), mk.reshape(own_heads, 64, 64), g_output.astype(F32), bo,
        g2, s2, g_expand.astype(F32), eb, g_reduce.astype(F32), br,
    )


def solution(mesh):
    row = P("fsdp", "ctx", None)
    vec = P("fsdp")
    maps = P("fsdp", None, None)
    in_specs = (
        row, row, row, P("fsdp", None), vec, vec, P(None, "fsdp"), vec, maps, maps,
        P("fsdp", None), vec, vec, vec, P(None, "fsdp"), vec, P("fsdp", None), vec,
    )
    out_specs = (
        row, row, vec, vec, P(None, "fsdp"), vec, maps, maps, P("fsdp", None), vec, vec, vec,
        P(None, "fsdp"), vec, P("fsdp", None), vec,
    )
    return jax.shard_map(body, mesh=mesh, in_specs=in_specs, out_specs=out_specs, check_vma=False)
```

```python
import functools

import jax
import jax.numpy as jnp
from jax import lax
from jax.experimental import pallas as pl
from jax.experimental.pallas import tpu as pltpu
from jax.sharding import PartitionSpec as P

EPS = 1e-05
F32 = jnp.float32
BF16 = jnp.bfloat16
AUG = 80
KEEP = 72
NN = (((1,), (0,)), ((), ()))
NT = (((1,), (1,)), ((), ()))
TN = (((0,), (0,)), ((), ()))
CORE = [(i, i ^ 1) for i in range(4)]
CROSS = [(i, i ^ 2) for i in range(4)]
VMEM = pl.BlockSpec(memory_space=pltpu.VMEM)
SMEM = pl.BlockSpec(memory_space=pltpu.SMEM)
FAR = pl.BlockSpec(memory_space=pltpu.HBM)
ANYWHERE = pl.BlockSpec(memory_space=pl.ANY)
SPECS = {"v": VMEM, "s": SMEM, "h": FAR, "a": ANYWHERE}


def mm(a, b, dims):
    return lax.dot_general(a, b, dims, preferred_element_type=F32)


class Staged:
    def __init__(self, far, near, sem, out):
        self.near, self.state = near, "out" if out else "in"
        self.copy = pltpu.make_async_copy(*((near, far) if out else (far, near)), sem)
        self.shape, self.dtype = near.shape, near.dtype
        if not out:
            self.copy.start()

    def ready(self):
        if self.state == "in":
            self.copy.wait()
            self.state = "ready"

    def flush(self):
        if self.state == "out":
            self.copy.start()
            self.state = "flushed"

    def finish(self):
        self.ready()
        self.flush()
        if self.state == "flushed":
            self.copy.wait()
            self.state = "done"

    def __getitem__(self, index):
        assert self.state in ("ready", "out", "flushed")
        return self.near[index]

    def __setitem__(self, index, value):
        assert self.state == "out"
        self.near[index] = value


def ready(*refs):
    for ref in refs:
        if isinstance(ref, Staged):
            ref.ready()


def flush(*refs):
    for ref in refs:
        if isinstance(ref, Staged):
            ref.flush()


def call(kernel, outs, kinds, args, name, scratch=(), out_kinds=None, limit=32):
    out_kinds = out_kinds or "v" * len(outs)
    both = kinds + out_kinds
    spans = [a[1:] if isinstance(a, tuple) else (0, a.shape[0]) for a in [*args, *outs]]
    args = [a[0] if isinstance(a, tuple) else a for a in args]
    staged = [
        pltpu.VMEM((size, *a.shape[1:]), a.dtype)
        for a, k, (_, size) in zip([*args, *outs], both, spans) if k in "ha"
    ]

    def run(*refs):
        count = len(both)
        extra = len(staged)
        near = refs[count : count + extra]
        sems = refs[count + extra] if extra else None
        rest = refs[count + extra + (1 if extra else 0) :]
        use, at = [], 0
        for i, kind in enumerate(both):
            if kind in "ha":
                start, size = spans[i]
                far = refs[i] if refs[i].shape[0] == size else refs[i].at[pl.ds(start, size)]
                use.append(Staged(far, near[at], sems.at[at], i >= len(kinds)))
                at += 1
            else:
                use.append(refs[i])
        kernel(*use, *rest)
        for ref in use:
            if isinstance(ref, Staged):
                ref.finish()

    sems = [pltpu.SemaphoreType.DMA((len(staged),))] if staged else []
    return pl.pallas_call(
        run,
        out_shape=[
            pltpu.HBM(o.shape, o.dtype) if k == "h" else o for o, k in zip(outs, out_kinds)
        ],
        in_specs=[SPECS[k] for k in kinds],
        out_specs=[SPECS[k] for k in out_kinds],
        scratch_shapes=[*staged, *sems, *scratch],
        compiler_params=pltpu.CompilerParams(vmem_limit_bytes=limit << 20),
        cost_estimate=pl.CostEstimate(flops=1, bytes_accessed=1, transcendentals=0),
        name=name,
    )(*[
        pltpu.with_memory_space_constraint(a, pltpu.HBM) if k == "h" else a
        for a, k in zip(args, kinds)
    ])


def shaped(shape, dtype=F32):
    return jax.ShapeDtypeStruct(shape, dtype)


def norm_parts(v):
    center = v - jnp.mean(v, axis=-1, keepdims=True)
    scale = lax.rsqrt(jnp.mean(center * center, axis=-1, keepdims=True) + EPS)
    return center * scale, scale


def norm_back(gy, normal, scale, gain):
    a = gy * gain
    return (
        a - jnp.mean(a, axis=-1, keepdims=True)
        - normal * jnp.mean(a * normal, axis=-1, keepdims=True)
    ) * scale


def aug_rows(top, row):
    index = lax.broadcasted_iota(jnp.int32, (AUG - top.shape[0], top.shape[1]), 0)
    tail = jnp.where(index == 0, row, 0.0).astype(BF16)
    return jnp.concatenate([top, tail], axis=0)


def spread_states(total_ref, out_ref, parts, rows_per):
    for part in range(parts):
        out_ref[part] = total_ref[:, part * rows_per : (part + 1) * rows_per, :].astype(BF16)


def collect_states(in_ref, total_ref, parts, rows_per):
    for part in range(parts):
        total_ref[:, part * rows_per : (part + 1) * rows_per, :] = in_ref[part].astype(F32)


def project_rows(meta, j, w, n, pb_ref):
    line = jnp.broadcast_to(pb_ref[pl.ds(meta[j], 1), :], (128, w.shape[0])).T
    bias = jnp.concatenate([line] * (n.shape[0] // 128), axis=1)
    return (mm(w[...], n, NT) + bias).astype(BF16)


def near_kernel(meta, x_ref, p_ref, w0, w1, pb_ref, n_ref, half_ref):
    ready(x_ref)
    normal, _ = norm_parts(x_ref[...].astype(F32))
    n = (normal * p_ref[0:1] + p_ref[1:2]).astype(BF16)
    n_ref[...] = n
    flush(n_ref)
    span = w0.shape[0]
    for j, w in enumerate((w0, w1)):
        ready(w)
        start = pl.multiple_of((meta[j] & 1) * span, 64)
        half_ref[pl.ds(start, span), :] = project_rows(meta, j, w, n, pb_ref)


def far_kernel(meta, n_ref, near_ref, w2, w3, pb_ref, qkv_ref):
    span = w2.shape[0]
    ready(n_ref)
    start = pl.multiple_of((meta[0] >> 1) * 2 * span, 64)
    qkv_ref[pl.ds(start, 2 * span), :] = near_ref[...]
    for j, w in ((2, w2), (3, w3)):
        ready(w)
        start = pl.multiple_of(meta[j] * span, 64)
        qkv_ref[pl.ds(start, span), :] = project_rows(meta, j, w, n_ref[...], pb_ref)


def phi(rows_ref, base, map_ref, h):
    rows = rows_ref[pl.ds(pl.multiple_of(base + h * 64, 64), 64), :]
    logits = mm(map_ref[h], rows, TN)
    up = jnp.exp(logits - jnp.max(logits, axis=0, keepdims=True))
    down = jnp.exp(jnp.min(logits, axis=0, keepdims=True) - logits)
    p1 = up / jnp.sum(up, axis=0, keepdims=True)
    p2 = down / jnp.sum(down, axis=0, keepdims=True)
    return p1.astype(BF16), p2.astype(BF16)


def key_kernel(heads, slots, parts, meta, qkv_ref, map_ref, fk_ref, s_ref, total):
    width = heads * 64
    cols = qkv_ref.shape[1] // slots
    rows_per = s_ref.shape[2]
    total[...] = jnp.zeros_like(total)

    def head(h, carry):
        p1, p2 = phi(qkv_ref, width, map_ref, h)
        at = pl.multiple_of(h * 128, 128)
        fk_ref[pl.ds(at, 64), :] = p1
        fk_ref[pl.ds(pl.multiple_of(at + 64, 64), 64), :] = p2
        v = qkv_ref[pl.ds(pl.multiple_of(2 * width + h * 64, 64), 64), :]
        va = aug_rows(v, 1.0)
        fk = jnp.concatenate([p1, p2], axis=0)
        for s in range(slots):
            part = slice(s * cols, (s + 1) * cols)
            state = mm(va[:, part], fk[:, part], NT)
            total[s ^ meta[4], pl.ds(pl.multiple_of(h * KEEP, 8), KEEP), :] = state[:KEEP]
        return carry

    lax.fori_loop(0, heads, head, 0)
    flush(fk_ref)
    spread_states(total, s_ref, parts, rows_per)


def query_kernel(heads, qkv_ref, map_ref, fq_ref):
    def head(h, carry):
        p1, p2 = phi(qkv_ref, 0, map_ref, h)
        at = pl.multiple_of(h * 128, 128)
        fq_ref[pl.ds(at, 64), :] = p1
        fq_ref[pl.ds(pl.multiple_of(at + 64, 64), 64), :] = p2
        return carry

    lax.fori_loop(0, heads, head, 0)


def scan_kernel(nctx, backward, keep, in_ref, out_ref):
    blocks = 2 * nctx
    order = [(b, 0) if b < nctx else (blocks - 1 - b, 1) for b in range(blocks)]
    acc = jnp.zeros(in_ref.shape[2:], F32)
    for b in reversed(range(blocks)) if backward else range(blocks):
        c, lane = order[b]
        acc = acc * keep[b] + in_ref[c, lane].astype(F32)
        out_ref[c, lane] = acc.astype(BF16)


def fill_output(meta, wo_refs, wo):
    rows = wo_refs[0].shape[0]
    for j, ref in enumerate(wo_refs):
        wo[pl.ds(pl.multiple_of(meta[j] * rows, 64), rows), :] = ref[...]


def attend_kernel(
    heads, slots, parts, meta, c_ref, fq_ref, x_ref, w0, w1, w2, w3, p_ref,
    mixed_ref, den_ref, middle_ref, n2_ref, total, wo,
):
    cols = fq_ref.shape[1] // slots
    collect_states(c_ref, total, parts, c_ref.shape[2])
    ready(fq_ref)

    def head(h, carry):
        fq = fq_ref[pl.ds(pl.multiple_of(h * 128, 128), 128), :]
        for s in range(slots):
            part = slice(s * cols, (s + 1) * cols)
            c = total[s ^ meta[4], pl.ds(pl.multiple_of(h * KEEP, 8), AUG), :].astype(BF16)
            both = mm(c, fq[:, part], NN)
            den = both[64:65]
            mixed_ref[pl.ds(pl.multiple_of(h * 64, 64), 64), part] = (both[:64] / den).astype(BF16)
            den_ref[pl.ds(pl.multiple_of(h * 8, 8), 8), part] = jnp.broadcast_to(den, (8, cols))
        return carry

    lax.fori_loop(0, heads, head, 0)
    flush(mixed_ref, den_ref)
    ready(x_ref, w0, w1, w2, w3)
    fill_output(meta, (w0, w1, w2, w3), wo)
    middle = x_ref[...].astype(F32) + mm(mixed_ref[...], wo[...], TN) + p_ref[4:5]
    middle_ref[...] = middle
    flush(middle_ref)
    normal, _ = norm_parts(middle)
    n2 = (normal * p_ref[2:3] + p_ref[3:4]).astype(BF16)
    n2_ref[...] = n2


def mlp_kernel(tile, first, meta, n2_ref, n2o_ref, cot_ref, coto_ref, base_ref, eb_ref, we, wr, *refs):
    if first:
        out_ref, dn_ref, outo_ref, dno_ref, ge, gr, gb_ref, n2t, acc = refs
        dn_ref[...] = jnp.zeros_like(dn_ref)
        acc[...] = jnp.zeros_like(acc)
    else:
        back_ref, baseo_ref, backo_ref = refs[:3]
        out_ref, dn_ref, outo_ref, dno_ref, ge, gr, gb_ref, n2t, acc = refs[3:]
        dn_ref[...] = back_ref[...]
        acc[0] = baseo_ref[...].astype(F32)
        acc[1] = backo_ref[...].astype(F32)
    ready(base_ref)
    out_ref[...] = base_ref[...]
    rows_n = n2_ref.shape[0]
    line = meta[2] if first else meta[0]
    ready(n2_ref, n2o_ref)
    for half, ref in enumerate((n2_ref, n2o_ref)):
        n2t[:, half * rows_n : (half + 1) * rows_n] = ref[...].T
    ready(we, wr, cot_ref, coto_ref)

    def step(t, carry):
        at = pl.ds(pl.multiple_of(t * tile, tile), tile)
        w_in = we[:, at]
        w_out = wr[at, :]
        bias = eb_ref[pl.ds(line, 1), at]
        actives, hiddens, sums = [], [], None
        for half, (n_ref, c_ref) in enumerate(((n2_ref, cot_ref), (n2o_ref, coto_ref))):
            hidden = mm(n_ref[...], w_in, NN) + bias
            square = hidden * hidden
            inner = 0.7978845608028654 * hidden * (1.0 + 0.044715 * square)
            tanh = jnp.tanh(inner)
            part = 0.5 * (1.0 + tanh)
            active = (hidden * part).astype(BF16)
            slope = part + 0.5 * hidden * (1.0 - tanh * tanh) * (
                0.7978845608028654 * (1.0 + 0.134145 * square)
            )
            r_active = mm(c_ref[...], w_out, NT).astype(BF16).astype(F32)
            r_hidden = (r_active * slope).astype(BF16)
            if half == 0:
                out_ref[...] += mm(active, w_out, NN)
                dn_ref[...] += mm(r_hidden, w_in, NT)
            else:
                acc[0] += mm(active, w_out, NN)
                acc[1] += mm(r_hidden, w_in, NT)
            actives.append(active)
            hiddens.append(r_hidden)
            total = jnp.sum(r_hidden.astype(F32), axis=0, keepdims=True)
            sums = total if sums is None else sums + total
        gr[at, :] = (
            mm(actives[0], cot_ref[...], TN) + mm(actives[1], coto_ref[...], TN)
        ).astype(BF16)
        ge[:, at] = (
            mm(n2t[:, :rows_n], hiddens[0], NN) + mm(n2t[:, rows_n:], hiddens[1], NN)
        ).astype(BF16)
        gb_ref[:, at] = jnp.broadcast_to(sums, (8, tile))
        return carry

    lax.fori_loop(0, we.shape[1] // tile, step, 0)
    flush(ge, gr)
    outo_ref[...] = acc[0].astype(BF16)
    dno_ref[...] = acc[1].astype(BF16)


def middle_kernel(
    heads, slots, parts, meta, dn_ref, dnin_ref, middle_ref, cot_ref, p_ref, mixed_ref, den_ref, fq_ref,
    w0, w1, w2, w3, gm_ref, ratt_ref, raug_ref, g_ref, small_ref, total, wo, rmix,
):
    cols = fq_ref.shape[1] // slots
    ready(middle_ref, dnin_ref, cot_ref)
    normal, scale = norm_parts(middle_ref[...])
    gy = dn_ref[...] + dnin_ref[...].astype(F32)
    cot = cot_ref[...].astype(F32)
    g_middle = cot + norm_back(gy, normal, scale, p_ref[2:3])
    gm_ref[...] = g_middle
    r_att = g_middle.astype(BF16)
    ratt_ref[...] = r_att
    flush(gm_ref, ratt_ref)
    small_ref[...] = jnp.concatenate(
        [
            jnp.sum(gy * normal, axis=0, keepdims=True),
            jnp.sum(gy, axis=0, keepdims=True),
            jnp.sum(r_att.astype(F32), axis=0, keepdims=True),
            jnp.sum(cot, axis=0, keepdims=True),
            jnp.zeros((4, gy.shape[1]), F32),
        ],
        axis=0,
    )
    ready(w0, w1, w2, w3)
    fill_output(meta, (w0, w1, w2, w3), wo)
    rmix[...] = mm(wo[...], r_att, NT).astype(BF16)
    total[...] = jnp.zeros_like(total)
    ready(mixed_ref, den_ref, fq_ref)

    def head(h, carry):
        rows = pl.ds(pl.multiple_of(h * 64, 64), 64)
        rm = rmix[rows, :].astype(F32)
        inverse = 1.0 / den_ref[pl.ds(pl.multiple_of(h * 8, 8), 8), :][0:1]
        rn = (rm * inverse).astype(BF16)
        rd = -jnp.sum(rm * mixed_ref[rows, :].astype(F32), axis=0, keepdims=True) * inverse
        ra = aug_rows(rn, rd)
        raug_ref[pl.ds(pl.multiple_of(h * AUG, 16), AUG), :] = ra
        fq = fq_ref[pl.ds(pl.multiple_of(h * 128, 128), 128), :]
        for s in range(slots):
            part = slice(s * cols, (s + 1) * cols)
            state = mm(ra[:, part], fq[:, part], NT)
            total[s ^ meta[4], pl.ds(pl.multiple_of(h * KEEP, 8), KEEP), :] = state[:KEEP]
        return carry

    lax.fori_loop(0, heads, head, 0)
    spread_states(total, g_ref, parts, g_ref.shape[2])
    flush(g_ref, raug_ref)


def logits_back(p_both, g_both):
    p1, p2 = p_both[:64].astype(F32), p_both[64:].astype(F32)
    g1, g2 = g_both[:64], g_both[64:]
    s1 = jnp.sum(p1 * g1, axis=0, keepdims=True)
    s2 = jnp.sum(p2 * g2, axis=0, keepdims=True)
    return (p1 * (g1 - s1) - p2 * (g2 - s2)).astype(BF16)


def query_back_kernel(
    heads, slots, parts, meta, c_ref, raug_ref, fq_ref, qkv_ref, map_ref, mixed_ref, ratt_ref,
    rq_ref, gmap_ref, g0, g1, g2, g3, total,
):
    cols = fq_ref.shape[1] // slots
    ready(c_ref)
    collect_states(c_ref, total, parts, c_ref.shape[2])
    ready(raug_ref, fq_ref, qkv_ref)

    def head(h, carry):
        ra = raug_ref[pl.ds(pl.multiple_of(h * AUG, 16), AUG), :]
        fq = fq_ref[pl.ds(pl.multiple_of(h * 128, 128), 128), :]
        pieces = []
        for s in range(slots):
            part = slice(s * cols, (s + 1) * cols)
            c = total[s ^ meta[4], pl.ds(pl.multiple_of(h * KEEP, 8), AUG), :].astype(BF16)
            pieces.append(mm(c, ra[:, part], TN))
        r_fq = jnp.concatenate(pieces, axis=1).astype(BF16).astype(F32)
        r_l = logits_back(fq, r_fq)
        rows = pl.ds(pl.multiple_of(h * 64, 64), 64)
        rq_ref[rows, :] = mm(map_ref[h], r_l, NN).astype(BF16)
        gmap_ref[h] = mm(qkv_ref[rows, :], r_l, NT)
        return carry

    lax.fori_loop(0, heads, head, 0)
    flush(rq_ref, gmap_ref)
    ready(mixed_ref, ratt_ref)
    rows = g0.shape[0]
    for j, g in enumerate((g0, g1, g2, g3)):
        mixed = mixed_ref[pl.ds(pl.multiple_of(meta[j] * rows, 64), rows), :]
        g[...] = mm(mixed, ratt_ref[...], NN).astype(BF16)
        flush(g)


def key_back_kernel(
    heads, slots, parts, meta, d_ref, fk_ref, qkv_ref, map_ref, rq_ref, n_ref,
    rp_ref, gmap_ref, g1, g3, total,
):
    width = heads * 64
    cols = fk_ref.shape[1] // slots
    collect_states(d_ref, total, parts, d_ref.shape[2])
    ready(fk_ref, qkv_ref, rq_ref)
    rp_ref[0:width, :] = rq_ref[...]

    def head(h, carry):
        fk = fk_ref[pl.ds(pl.multiple_of(h * 128, 128), 128), :]
        v = qkv_ref[pl.ds(pl.multiple_of(2 * width + h * 64, 64), 64), :]
        va = aug_rows(v, 1.0)
        pieces = []
        for s in range(slots):
            part = slice(s * cols, (s + 1) * cols)
            d = total[s ^ meta[4], pl.ds(pl.multiple_of(h * KEEP, 8), AUG), :].astype(BF16)
            pieces.append(mm(d, va[:, part], TN))
            rv = mm(d[:64], fk[:, part], NN).astype(BF16)
            rp_ref[pl.ds(pl.multiple_of(2 * width + h * 64, 64), 64), part] = rv
        r_fk = jnp.concatenate(pieces, axis=1).astype(BF16).astype(F32)
        r_l = logits_back(fk, r_fk)
        rows = pl.ds(pl.multiple_of(width + h * 64, 64), 64)
        rp_ref[rows, :] = mm(map_ref[h], r_l, NN).astype(BF16)
        gmap_ref[h] = mm(qkv_ref[rows, :], r_l, NT)
        return carry

    lax.fori_loop(0, heads, head, 0)
    flush(gmap_ref)
    ready(n_ref)
    span = g1.shape[0]
    for j, g in ((1, g1), (3, g3)):
        rp = rp_ref[pl.ds(pl.multiple_of(meta[j] * span, 64), span), :]
        g[...] = mm(rp, n_ref[...], NN).astype(BF16)
        flush(g)


def project_grad_kernel(meta, rp_ref, n_ref, in0, in2, g0, g2):
    span = g0.shape[0]
    ready(n_ref, in0, in2)
    for j, more, g in ((2, in2, g2), (0, in0, g0)):
        rp = rp_ref[pl.ds(pl.multiple_of(meta[j] * span, 64), span), :]
        g[...] = (mm(rp, n_ref[...], NN) + more[...].astype(F32)).astype(BF16)
        flush(g)


def input_kernel(
    heads, meta, rp_ref, x_ref, p_ref, gm_ref, out_ref, outin_ref, two_ref, ebo_ref, ebc_ref,
    mq_ref, mk_ref, w0, w1, w2, w3, dx_ref, full_ref, b0, b1, b2, b3, pack,
):
    ready(out_ref, outin_ref)
    full_ref[...] = out_ref[...] + outin_ref[...].astype(F32) + p_ref[5:6]
    flush(full_ref)
    span, width = w0.shape
    shard = width // 4
    own_heads = heads // 4
    ones = jnp.ones((8, x_ref.shape[0]), BF16)
    pack[...] = jnp.zeros_like(pack)
    gy = None
    ready(w0, w1, w2, w3, x_ref, gm_ref)
    for j, w in enumerate((w0, w1, w2, w3)):
        rp = rp_ref[pl.ds(pl.multiple_of(meta[j] * span, 64), span), :]
        part = mm(rp, w[...], TN)
        gy = part if gy is None else gy + part
        pack[meta[j], 8:16, :span] = mm(ones, rp, NT)
    pack[meta[0], 16:24, :] = ebo_ref[...]
    pack[meta[2], 16:24, :] = ebc_ref[...]
    normal, scale = norm_parts(x_ref[...].astype(F32))
    dx_ref[...] = gm_ref[...] + norm_back(gy, normal, scale, p_ref[0:1])
    flush(dx_ref)
    ready(mq_ref, mk_ref)
    lines = [
        jnp.sum(gy * normal, axis=0, keepdims=True),
        jnp.sum(gy, axis=0, keepdims=True),
        two_ref[0:1], two_ref[1:2], two_ref[2:3], two_ref[3:4],
    ]
    for i in range(4):
        cut = slice(i * shard, (i + 1) * shard)
        for k, line in enumerate(lines):
            pack[i, k : k + 1, :shard] = line[:, cut]
        for base, ref in ((24, mq_ref), (40, mk_ref)):
            for k in range(4):
                for h in range(own_heads):
                    at = k * shard + h * 64
                    pack[i, base : base + 16, at : at + 64] = ref[
                        i * own_heads + h, 16 * k : 16 * k + 16, :
                    ]
    for j, b in enumerate((b0, b1, b2, b3)):
        b[...] = pack[meta[j]].astype(BF16)


def unpack_kernel(rest_ref, g1, s1, g2, s2, bo, br, pb, eb, mq, mk):
    shard = g1.shape[1]
    own_heads = mq.shape[0]
    for k, ref in enumerate((g1, s1, g2, s2, bo, br)):
        ref[...] = rest_ref[k : k + 1, :shard]
    pb[...] = rest_ref[8:9, : pb.shape[1]]
    eb[...] = rest_ref[16:17, :]
    for base, ref in ((24, mq), (40, mk)):
        for k in range(4):
            for h in range(own_heads):
                at = k * shard + h * 64
                ref[h, 16 * k : 16 * k + 16, :] = rest_ref[base : base + 16, at : at + 64]


def core_swap(a):
    return lax.ppermute(a, "fsdp", CORE)


def cross_swap(a):
    return lax.ppermute(a, "fsdp", CROSS)


def after(value, *others):
    return lax.optimization_barrier((value, *others))[0]


def spread(shard, cross):
    return [shard, core_swap(shard), cross, core_swap(cross)]


def add(a, b):
    return (a.astype(F32) + b.astype(F32)).astype(BF16)


def ctx_pairs(nctx, bit):
    return [(i, i ^ (1 << bit)) for i in range(nctx)]


def rows_sum(parts, start, size):
    out = None
    for offset, part in parts:
        piece = lax.dynamic_slice_in_dim(part, start + offset, size, 0).astype(F32)
        out = piece if out is None else out + piece
    return out.astype(BF16)


class Reduction:
    def __init__(self, parts, nctx, place):
        self.parts = [(0, part) for part in parts]
        self.rows, self.nctx, self.place = parts[0].shape[0], nctx, place
        self.bits = nctx.bit_length() - 1

    def halve(self, bit):
        half = self.rows // 2
        mine = (self.place >> bit) & 1
        sent = rows_sum(self.parts, (1 - mine) * half, half)
        got = lax.ppermute(sent, "ctx", ctx_pairs(self.nctx, bit))
        self.parts = [(offset + mine * half, part) for offset, part in self.parts] + [(0, got)]
        self.rows = half
        return got

    def hold(self, *others):
        offset, last = self.parts[-1]
        self.parts[-1] = (offset, after(last, *others))

    def spread(self):
        cur = rows_sum(self.parts, 0, self.rows)
        for bit in reversed(range(self.bits)):
            other = lax.ppermute(cur, "ctx", ctx_pairs(self.nctx, bit))
            first = ((self.place >> bit) & 1) == 0
            cur = jnp.concatenate(
                [jnp.where(first, cur, other), jnp.where(first, other, cur)], axis=0
            )
        return cur

    def total(self, begin=0):
        for bit in range(begin, self.bits):
            self.halve(bit)
        return self.spread()


def small_sum(parts, nctx):
    own, core, cross, far = parts
    far_in, core_in = core_swap(far), core_swap(core)
    cross_in = cross_swap(add(cross, far_in))
    cur = own.astype(F32) + core_in.astype(F32) + cross_in.astype(F32)
    for bit in range(nctx.bit_length() - 1):
        low = cur.astype(BF16)
        cur = low.astype(F32) + lax.ppermute(low, "ctx", ctx_pairs(nctx, bit)).astype(F32)
    return cur


def straighten(parts, mine):
    a, b, c, d = parts
    odd = (mine & 1) == 1
    upper = (mine & 2) == 2
    a, b = jnp.where(odd, b, a), jnp.where(odd, a, b)
    c, d = jnp.where(odd, d, c), jnp.where(odd, c, d)
    return [
        jnp.where(upper, c, a), jnp.where(upper, d, b),
        jnp.where(upper, a, c), jnp.where(upper, b, d),
    ]


def exchange(a):
    return lax.all_to_all(a, "ctx", 0, 0, tiled=True)


def body(
    tokens, cotangent, pair_table, seq_ids, first_gain, first_shift, project_weight, project_bias,
    feature_query, feature_key, output_weight, output_bias, second_gain, second_shift,
    expand_weight, expand_bias, reduce_weight, reduce_bias,
):
    x = tokens[0]
    cot = cotangent[0]
    rows_n, width = x.shape
    heads = width // feature_query.shape[1]
    own_heads = feature_query.shape[0]
    slots = pair_table.shape[2]
    nctx = lax.axis_size("ctx")
    place = lax.axis_index("ctx")
    mine = lax.axis_index("fsdp")
    span = project_weight.shape[1]
    hidden_own = expand_weight.shape[1]
    shard = width // 4
    wide = heads * 128

    project_t = project_weight.T
    cross_project = cross_swap(project_t)
    vector = jnp.concatenate(
        [first_gain, first_shift, second_gain, second_shift, output_bias, reduce_bias,
         project_bias, expand_bias]
    )
    room = -vector.shape[0] % 1024
    vector = jnp.concatenate([vector, jnp.zeros((room,), BF16)]).reshape(-1, 64)
    map_rows = own_heads * 64
    pack = jnp.concatenate(
        [feature_query.reshape(-1, 64), feature_key.reshape(-1, 64), vector]
    )
    packs = spread(pack, cross_swap(pack))
    ordered = straighten(packs, mine)
    query_map = jnp.concatenate([p[:map_rows] for p in ordered]).reshape(heads, 64, 64)
    key_map = jnp.concatenate([p[map_rows : 2 * map_rows] for p in ordered]).reshape(heads, 64, 64)
    vectors = jnp.stack([p[2 * map_rows :] for p in ordered]).reshape(4, -1).astype(F32)
    params = vectors[:, : 6 * shard].reshape(4, 6, shard).transpose(1, 0, 2).reshape(6, width)
    project_line = vectors[:, 6 * shard : 6 * shard + span]
    expand_line = vectors[:, 6 * shard + span : 6 * shard + span + hidden_own]
    project_core = core_swap(project_t)
    project_far = core_swap(cross_project)
    projects = [project_t, project_core, cross_project, project_far]
    near_expand = jnp.concatenate([expand_weight, output_weight])
    cross_expand = cross_swap(after(near_expand, cross_project))
    core_output = core_swap(output_weight)
    far_output = core_swap(cross_expand[width:])
    outputs = [output_weight, core_output, (cross_expand, width, shard), far_output]
    cross_reduce = cross_swap(after(reduce_weight, cross_expand))
    cot_other = core_swap(cot)

    positions = pair_table[0, 0]
    swap = (positions[0] > positions[1]).astype(jnp.int32)
    meta = jnp.stack([mine, mine ^ 1, mine ^ 2, mine ^ 3, swap]).astype(jnp.int32)
    ids = seq_ids[0]
    same = (ids[1:] == ids[:-1]).astype(F32)
    none = jnp.zeros((1,), F32)
    keep = jnp.concatenate([none, same])
    keep_next = jnp.concatenate([same, none])

    rows_per = -(-(heads * KEEP) // (nctx * 16)) * 16
    state_shape = shaped((nctx, slots, rows_per, 128), BF16)
    total = pltpu.VMEM((slots, nctx * rows_per, 128), F32)
    wo_scratch = pltpu.VMEM((width, width), BF16)
    low = shaped((rows_n, width), BF16)
    full = shaped((rows_n, width))
    table = shaped((width, rows_n), BF16)
    square = shaped((heads, 64, 64))

    n1, near = call(
        near_kernel, [low, shaped((2 * span, rows_n), BF16)], "shvaav",
        [meta, x, params, projects[0], projects[1], project_line], "project_near", (), "hv",
    )
    (qkv,) = call(
        far_kernel, [shaped((3 * width, rows_n), BF16)], "shvaav",
        [meta, n1, near, projects[2], projects[3], project_line], "project_far",
    )
    fk, states = call(
        functools.partial(key_kernel, heads, slots, nctx),
        [shaped((wide, rows_n), BF16), state_shape], "svv",
        [meta, qkv, key_map], "keys", [total], "hh",
    )
    arrived = exchange(states)
    (fq,) = call(
        functools.partial(query_kernel, heads), [shaped((wide, rows_n), BF16)], "vv",
        [after(qkv, states), query_map], "queries", (), "h",
    )
    (running,) = call(
        functools.partial(scan_kernel, nctx, False), [state_shape], "sv",
        [keep, after(arrived, fq, cross_expand)], "scan", (), "h",
    )
    carried = exchange(running)
    mixed, den, middle, n2 = call(
        functools.partial(attend_kernel, heads, slots, nctx),
        [table, shaped((heads * 8, rows_n)), full, low],
        "svhhaaaav", [meta, carried, fq, x, *outputs, params], "attend",
        [total, wo_scratch], "hhhh",
    )
    n2_other = core_swap(n2)

    def mlp(first, base, w_in, w_out, more, name):
        return call(
            functools.partial(mlp_kernel, 384, first),
            [full, full, low, low, shaped((width, hidden_own), BF16),
             shaped((hidden_own, width), BF16), shaped((8, hidden_own))],
            "shaaa" + ("h" if first else "v") + "vaa" + "v" * len(more),
            [meta, n2, n2_other, cot, cot_other, base, expand_line, w_in, w_out, *more], name,
            [pltpu.VMEM((width, 2 * rows_n), BF16), pltpu.VMEM((2, rows_n, width), F32)],
            "vvvvhhv" if first else "hvhhhhv", 40,
        )

    out1, dn1, out1_o, dn1_o, ge_cross, gr_cross, gb_cross = mlp(
        True, middle, (cross_expand, 0, width), cross_reduce, [], "mlp_far"
    )
    ge_in = cross_swap(ge_cross)
    out2, dn2, out2_o, dn2_o, ge_own, gr_own, gb_own = mlp(
        False, out1, expand_weight, reduce_weight, [dn1, out1_o, dn1_o], "mlp_near"
    )
    dn2_in = core_swap(dn2_o)

    g_middle, r_att, raug, g_states, small_two = call(
        functools.partial(middle_kernel, heads, slots, nctx),
        [full, low, shaped((heads * AUG, rows_n), BF16), state_shape, shaped((8, width))],
        "svahavhhhaaaa",
        [meta, dn2, dn2_in, middle, cot, params, mixed, den, fq, *outputs], "middle",
        [total, wo_scratch, pltpu.VMEM((width, rows_n), BF16)], "hhhhv",
    )
    g_arrived = exchange(g_states)
    gr_in = cross_swap(after(gr_cross, ge_in))
    out2_in = core_swap(after(out2_o, g_states))
    rq, g_query_map, *go = call(
        functools.partial(query_back_kernel, heads, slots, nctx),
        [table, square] + [shaped((shard, width), BF16)] * 4,
        "sahhavhh", [meta, carried, raug, fq, (qkv, 0, width), query_map, mixed, r_att], "query_back",
        [total], "hhhhhh",
    )
    (g_running,) = call(
        functools.partial(scan_kernel, nctx, True), [state_shape], "sv",
        [keep_next, after(g_arrived, rq, ge_in)], "scan_back", (), "h",
    )
    g_carried = exchange(g_running)
    sum_e = Reduction([ge_own, after(ge_in, g_running)], nctx, place)
    e_half = sum_e.halve(0)
    go_far, go_core = core_swap(after(go[3], g_running)), core_swap(after(go[1], g_running))
    rp, g_key_map, gp1, gp3 = call(
        functools.partial(key_back_kernel, heads, slots, nctx),
        [shaped((3 * width, rows_n), BF16), square] + [shaped((span, width), BF16)] * 2,
        "svhavhh", [meta, after(g_carried, e_half), fk, qkv, key_map, rq, n1],
        "key_back", [total], "vhhh",
    )
    gp3_in, gp1_in = core_swap(gp3), core_swap(gp1)
    gp_own, gp_cross = call(
        project_grad_kernel, [shaped((span, width), BF16)] * 2, "svhaa",
        [meta, rp, n1, gp1_in, gp3_in], "project_grad", (), "hh",
    )
    go_in = cross_swap(after(add(go[2], go_far), gr_in))
    gp_in = cross_swap(after(gp_cross, go_in))
    small = shaped((64, width), BF16)
    dx, layer_out, *blocks = call(
        functools.partial(input_kernel, heads), [full, full, small, small, small, small],
        "svhvhhavvvhhaaaa",
        [meta, rp, after(x, gp_own), params, g_middle, out2, out2_in, small_two, gb_own, gb_cross,
         g_query_map, g_key_map, *projects],
        "input", [pltpu.VMEM((4, 64, width), F32)], "hhvvvv",
    )
    sum_e.hold(gp_own)
    gr_in = after(gr_in, gp_own)
    g_expand = sum_e.total(1)
    g_reduce = Reduction([gr_own, gr_in], nctx, place).total()
    own_go = add(add(go[0], go_core), go_in)
    g_project = Reduction(
        [jnp.concatenate([gp_own, own_go]),
         jnp.concatenate([gp_in, jnp.zeros_like(own_go)])], nctx, place
    ).total()
    rest = small_sum(blocks, nctx)
    line = shaped((1, shard))
    g1, s1, g2, s2, bo, br, pb, eb, mq, mk = call(
        unpack_kernel,
        [line] * 6 + [shaped((1, span)), shaped((1, hidden_own))]
        + [shaped((own_heads, 64, 64))] * 2, "v", [rest], "unpack",
    )
    return (
        layer_out[None], dx[None], g1[0], s1[0], g_project[:span].T.astype(F32), pb[0], mq, mk,
        g_project[span:].astype(F32), bo[0], g2[0], s2[0], g_expand.astype(F32), eb[0],
        g_reduce.astype(F32), br[0],
    )


def solution(mesh):
    row = P("fsdp", "ctx", None)
    vec = P("fsdp")
    maps = P("fsdp", None, None)
    in_specs = (
        row, row, row, P("fsdp", None), vec, vec, P(None, "fsdp"), vec, maps, maps,
        P("fsdp", None), vec, vec, vec, P(None, "fsdp"), vec, P("fsdp", None), vec,
    )
    out_specs = (
        row, row, vec, vec, P(None, "fsdp"), vec, maps, maps, P("fsdp", None), vec, vec, vec,
        P(None, "fsdp"), vec, P("fsdp", None), vec,
    )
    return jax.shard_map(body, mesh=mesh, in_specs=in_specs, out_specs=out_specs, check_vma=False)
```

```python
import functools

import jax
import jax.numpy as jnp
from jax import lax
from jax.experimental import pallas as pl
from jax.experimental.pallas import tpu as pltpu
from jax.sharding import PartitionSpec as P

EPS = 1e-05
F32 = jnp.float32
BF16 = jnp.bfloat16
AUG = 80
KEEP = 72
UNROLL = 3
NN = (((1,), (0,)), ((), ()))
NT = (((1,), (1,)), ((), ()))
TN = (((0,), (0,)), ((), ()))
CORE = [(i, i ^ 1) for i in range(4)]
CROSS = [(i, i ^ 2) for i in range(4)]
VMEM = pl.BlockSpec(memory_space=pltpu.VMEM)
SMEM = pl.BlockSpec(memory_space=pltpu.SMEM)
FAR = pl.BlockSpec(memory_space=pltpu.HBM)
ANYWHERE = pl.BlockSpec(memory_space=pl.ANY)
SPECS = {"v": VMEM, "s": SMEM, "h": FAR, "a": ANYWHERE}


def mm(a, b, dims):
    return lax.dot_general(a, b, dims, preferred_element_type=F32)


class Staged:
    def __init__(self, far, near, sems, out):
        self.near, self.state = near, "out" if out else "in"
        self.copies, at = [], 0
        for part, sem in zip(far, sems):
            here = near if len(far) == 1 else near.at[pl.ds(at, part.shape[0])]
            pair = (here, part) if out else (part, here)
            self.copies.append(pltpu.make_async_copy(*pair, sem))
            at += part.shape[0]
        self.shape, self.dtype = near.shape, near.dtype
        if not out:
            self.start()

    def start(self):
        for copy in self.copies:
            copy.start()

    def wait(self):
        for copy in self.copies:
            copy.wait()

    def ready(self):
        if self.state == "in":
            self.wait()
            self.state = "ready"

    def flush(self):
        if self.state == "out":
            self.start()
            self.state = "flushed"

    def finish(self):
        self.ready()
        self.flush()
        if self.state == "flushed":
            self.wait()
            self.state = "done"

    def __getitem__(self, index):
        assert self.state in ("ready", "out", "flushed")
        return self.near[index]

    def __setitem__(self, index, value):
        assert self.state == "out"
        self.near[index] = value


def ready(*refs):
    for ref in refs:
        if isinstance(ref, Staged):
            ref.ready()


def flush(*refs):
    for ref in refs:
        if isinstance(ref, Staged):
            ref.flush()


def call(kernel, outs, kinds, args, name, scratch=(), out_kinds=None, limit=32):
    out_kinds = out_kinds or "v" * len(outs)
    both = kinds + out_kinds
    groups = [a if isinstance(a, list) else [a] for a in [*args, *outs]]
    groups = [
        [p if isinstance(p, tuple) else (p, 0, p.shape[0]) for p in group] for group in groups
    ]
    operands = [(p[0], k) for group, k in zip(groups[: len(kinds)], kinds) for p in group]
    pieces = sum(len(group) for group, k in zip(groups, both) if k in "ha")
    staged = [
        pltpu.VMEM((sum(p[2] for p in group), *group[0][0].shape[1:]), group[0][0].dtype)
        for group, k in zip(groups, both) if k in "ha"
    ]

    def run(*refs):
        count = sum(len(group) for group in groups)
        extra = len(staged)
        near = refs[count : count + extra]
        sems = refs[count + extra] if extra else None
        rest = refs[count + extra + (1 if extra else 0) :]
        use, at, ref_at, sem_at = [], 0, 0, 0
        for i, (kind, group) in enumerate(zip(both, groups)):
            mine = refs[ref_at : ref_at + len(group)]
            ref_at += len(group)
            if kind in "ha":
                far = [
                    ref if ref.shape[0] == size else ref.at[pl.ds(start, size)]
                    for ref, (_, start, size) in zip(mine, group)
                ]
                own = [sems.at[sem_at + j] for j in range(len(group))]
                sem_at += len(group)
                use.append(Staged(far, near[at], own, i >= len(kinds)))
                at += 1
            else:
                use.append(mine[0])
        kernel(*use, *rest)
        for ref in use:
            if isinstance(ref, Staged):
                ref.finish()

    sems = [pltpu.SemaphoreType.DMA((pieces,))] if staged else []
    return pl.pallas_call(
        run,
        out_shape=[
            pltpu.HBM(o.shape, o.dtype) if k == "h" else o for o, k in zip(outs, out_kinds)
        ],
        in_specs=[SPECS[k] for _, k in operands],
        out_specs=[SPECS[k] for k in out_kinds],
        scratch_shapes=[*staged, *sems, *scratch],
        compiler_params=pltpu.CompilerParams(vmem_limit_bytes=limit << 20),
        cost_estimate=pl.CostEstimate(flops=1, bytes_accessed=1, transcendentals=0),
        name=name,
    )(*[
        pltpu.with_memory_space_constraint(a, pltpu.HBM) if k == "h" else a
        for a, k in operands
    ])


def shaped(shape, dtype=F32):
    return jax.ShapeDtypeStruct(shape, dtype)


def norm_parts(v):
    center = v - jnp.mean(v, axis=-1, keepdims=True)
    scale = lax.rsqrt(jnp.mean(center * center, axis=-1, keepdims=True) + EPS)
    return center * scale, scale


def norm_back(gy, normal, scale, gain):
    a = gy * gain
    return (
        a - jnp.mean(a, axis=-1, keepdims=True)
        - normal * jnp.mean(a * normal, axis=-1, keepdims=True)
    ) * scale


def aug_rows(top, row):
    index = lax.broadcasted_iota(jnp.int32, (AUG - top.shape[0], top.shape[1]), 0)
    tail = jnp.where(index == 0, row, 0.0).astype(BF16)
    return jnp.concatenate([top, tail], axis=0)


def spread_states(total_ref, out_ref, parts, rows_per):
    for part in range(parts):
        out_ref[part] = total_ref[:, part * rows_per : (part + 1) * rows_per, :].astype(BF16)


def collect_states(in_ref, total_ref, parts, rows_per):
    for part in range(parts):
        total_ref[:, part * rows_per : (part + 1) * rows_per, :] = in_ref[part].astype(F32)


def project_rows(meta, j, w, n, pb_ref):
    line = jnp.broadcast_to(pb_ref[pl.ds(meta[j], 1), :], (128, w.shape[0])).T
    bias = jnp.concatenate([line] * (n.shape[0] // 128), axis=1)
    return (mm(w[...], n, NT) + bias).astype(BF16)


def near_kernel(meta, x_ref, p_ref, w0, w1, pb_ref, n_ref, half_ref):
    ready(x_ref)
    normal, _ = norm_parts(x_ref[...].astype(F32))
    n = (normal * p_ref[0:1] + p_ref[1:2]).astype(BF16)
    n_ref[...] = n
    flush(n_ref)
    span = w0.shape[0]
    for j, w in enumerate((w0, w1)):
        ready(w)
        start = pl.multiple_of((meta[j] & 1) * span, 64)
        half_ref[pl.ds(start, span), :] = project_rows(meta, j, w, n, pb_ref)


def far_kernel(meta, n_ref, near_ref, w2, w3, pb_ref, qkv_ref):
    span = w2.shape[0]
    ready(n_ref)
    start = pl.multiple_of((meta[0] >> 1) * 2 * span, 64)
    qkv_ref[pl.ds(start, 2 * span), :] = near_ref[...]
    for j, w in ((2, w2), (3, w3)):
        ready(w)
        start = pl.multiple_of(meta[j] * span, 64)
        qkv_ref[pl.ds(start, span), :] = project_rows(meta, j, w, n_ref[...], pb_ref)


def phi(rows_ref, base, map_ref, h):
    rows = rows_ref[pl.ds(pl.multiple_of(base + h * 64, 64), 64), :]
    logits = mm(map_ref[h], rows, TN)
    up = jnp.exp(logits - jnp.max(logits, axis=0, keepdims=True))
    down = jnp.exp(jnp.min(logits, axis=0, keepdims=True) - logits)
    p1 = up * (1.0 / jnp.sum(up, axis=0, keepdims=True))
    p2 = down * (1.0 / jnp.sum(down, axis=0, keepdims=True))
    return p1.astype(BF16), p2.astype(BF16)


def key_kernel(heads, slots, parts, meta, qkv_ref, map_ref, fk_ref, s_ref, total):
    width = heads * 64
    cols = qkv_ref.shape[1] // slots
    rows_per = s_ref.shape[2]
    total[...] = jnp.zeros_like(total)

    def head(h, carry):
        p1, p2 = phi(qkv_ref, width, map_ref, h)
        at = pl.multiple_of(h * 128, 128)
        fk_ref[pl.ds(at, 64), :] = p1
        fk_ref[pl.ds(pl.multiple_of(at + 64, 64), 64), :] = p2
        v = qkv_ref[pl.ds(pl.multiple_of(2 * width + h * 64, 64), 64), :]
        va = aug_rows(v, 1.0)
        fk = jnp.concatenate([p1, p2], axis=0)
        for s in range(slots):
            part = slice(s * cols, (s + 1) * cols)
            state = mm(va[:, part], fk[:, part], NT)
            total[s ^ meta[4], pl.ds(pl.multiple_of(h * KEEP, 8), KEEP), :] = state[:KEEP]
        return carry

    lax.fori_loop(0, heads, head, 0, unroll=UNROLL)
    flush(fk_ref)
    spread_states(total, s_ref, parts, rows_per)


def query_kernel(heads, qkv_ref, map_ref, fq_ref):
    def head(h, carry):
        p1, p2 = phi(qkv_ref, 0, map_ref, h)
        at = pl.multiple_of(h * 128, 128)
        fq_ref[pl.ds(at, 64), :] = p1
        fq_ref[pl.ds(pl.multiple_of(at + 64, 64), 64), :] = p2
        return carry

    lax.fori_loop(0, heads, head, 0, unroll=UNROLL)


def scan_kernel(nctx, backward, keep, in_ref, out_ref):
    blocks = 2 * nctx
    order = [(b, 0) if b < nctx else (blocks - 1 - b, 1) for b in range(blocks)]
    acc = jnp.zeros(in_ref.shape[2:], F32)
    for b in reversed(range(blocks)) if backward else range(blocks):
        c, lane = order[b]
        acc = acc * keep[b] + in_ref[c, lane].astype(F32)
        out_ref[c, lane] = acc.astype(BF16)


def fill_output(meta, wo_refs, wo):
    rows = wo_refs[0].shape[0]
    for j, ref in enumerate(wo_refs):
        wo[pl.ds(pl.multiple_of(meta[j] * rows, 64), rows), :] = ref[...]


def attend_kernel(
    heads, slots, parts, meta, c_ref, fq_ref, x_ref, w0, w1, w2, w3, p_ref,
    mixed_ref, den_ref, middle_ref, n2_ref, wo, total,
):
    cols = fq_ref.shape[1] // slots
    collect_states(c_ref, total, parts, c_ref.shape[2])
    ready(fq_ref)

    def head(h, carry):
        fq = fq_ref[pl.ds(pl.multiple_of(h * 128, 128), 128), :]
        for s in range(slots):
            part = slice(s * cols, (s + 1) * cols)
            c = total[s ^ meta[4], pl.ds(pl.multiple_of(h * KEEP, 8), AUG), :].astype(BF16)
            both = mm(c, fq[:, part], NN)
            den = both[64:65]
            mixed = both[:64] * (1.0 / den)
            mixed_ref[pl.ds(pl.multiple_of(h * 64, 64), 64), part] = mixed.astype(BF16)
            den_ref[pl.ds(pl.multiple_of(h * 8, 8), 8), part] = jnp.broadcast_to(den, (8, cols))
        return carry

    lax.fori_loop(0, heads, head, 0, unroll=UNROLL)
    flush(mixed_ref, den_ref)
    ready(x_ref, w0, w1, w2, w3)
    fill_output(meta, (w0, w1, w2, w3), wo)
    flush(wo)
    middle = x_ref[...].astype(F32) + mm(mixed_ref[...], wo[...], TN) + p_ref[4:5]
    middle_ref[...] = middle
    flush(middle_ref)
    normal, _ = norm_parts(middle)
    n2 = (normal * p_ref[2:3] + p_ref[3:4]).astype(BF16)
    n2_ref[...] = n2


def mlp_kernel(first, meta, n2_ref, we, n2o_ref, cot_ref, wr, coto_ref, base_ref, eb_ref, *refs):
    if first:
        out_ref, dn_ref, outo_ref, dno_ref, ge, ge_low, gr, gb_ref, act, hid = refs
    else:
        back_ref, baseo_ref, backo_ref, out_ref, dn_ref, outo_ref, dno_ref, ge, gr, gb_ref, act, hid = refs
    rows_n, width = n2_ref.shape
    line = meta[2] if first else meta[0]
    tile = we.shape[1] // 2
    ready(n2_ref, we, n2o_ref, cot_ref, wr, coto_ref)

    def step(t, carry):
        at = pl.ds(pl.multiple_of(t * tile, tile), tile)
        bias = eb_ref[pl.ds(line, 1), at]
        pre = [
            (mm(n[...], we[:, at], NN) + bias, mm(c[...], wr[at, :], NT))
            for n, c in ((n2_ref, cot_ref), (n2o_ref, coto_ref))
        ]
        actives, hiddens, sums = [], [], None
        for k, (hidden, back) in enumerate(pre):
            square = hidden * hidden
            part = 0.5 + 0.5 * jnp.tanh(
                hidden * (0.7978845608028654 + 0.035677408136300125 * square)
            )
            active = hidden * part
            slope = part + active * (1.0 - part) * (
                1.5957691216057308 + 0.21406444881780075 * square
            )
            r_hidden = back.astype(BF16).astype(F32) * slope
            actives.append(active.astype(BF16))
            hiddens.append(r_hidden.astype(BF16))
            act[k, :, at] = actives[k]
            hid[k, :, at] = hiddens[k]
            total = jnp.sum(r_hidden, axis=0, keepdims=True)
            sums = total if sums is None else sums + total
        gb_ref[:, at] = jnp.broadcast_to(sums, (8, tile))
        grad = (mm(n2_ref[...], hiddens[0], TN) + mm(n2o_ref[...], hiddens[1], TN)).astype(BF16)
        if first:
            ge[:, at] = grad[: width // 2]
            ge_low[:, at] = grad[width // 2 :]
        else:
            ge[:, at] = grad
        gr[at, :] = (
            mm(actives[0], cot_ref[...], TN) + mm(actives[1], coto_ref[...], TN)
        ).astype(BF16)
        return carry

    lax.fori_loop(0, 2, step, 0)
    flush(ge, gr)
    if first:
        flush(ge_low)
    ready(base_ref)
    dno = mm(hid[1], we[...], NT)
    outo = mm(act[1], wr[...], NN)
    if first:
        dno_ref[...] = dno.astype(BF16)
        outo_ref[...] = outo.astype(BF16)
        dn_ref[...] = mm(hid[0], we[...], NT)
    else:
        dno_ref[...] = (backo_ref[...].astype(F32) + dno).astype(BF16)
        flush(dno_ref)
        outo_ref[...] = (baseo_ref[...].astype(F32) + outo).astype(BF16)
        flush(outo_ref)
        dn_ref[...] = back_ref[...] + mm(hid[0], we[...], NT)
    out_ref[...] = base_ref[...] + mm(act[0], wr[...], NN)


def middle_kernel(
    heads, slots, parts, meta, dn_ref, dnin_ref, middle_ref, cot_ref, p_ref, mixed_ref, den_ref, fq_ref,
    wo, gm_ref, ratt_ref, raug_ref, g_ref, small_ref, total, rmix,
):
    cols = fq_ref.shape[1] // slots
    ready(middle_ref, dnin_ref, cot_ref)
    normal, scale = norm_parts(middle_ref[...])
    gy = dn_ref[...] + dnin_ref[...].astype(F32)
    cot = cot_ref[...].astype(F32)
    g_middle = cot + norm_back(gy, normal, scale, p_ref[2:3])
    gm_ref[...] = g_middle
    r_att = g_middle.astype(BF16)
    ratt_ref[...] = r_att
    flush(gm_ref, ratt_ref)
    small_ref[...] = jnp.concatenate(
        [
            jnp.sum(gy * normal, axis=0, keepdims=True),
            jnp.sum(gy, axis=0, keepdims=True),
            jnp.sum(r_att.astype(F32), axis=0, keepdims=True),
            jnp.sum(cot, axis=0, keepdims=True),
            jnp.zeros((4, gy.shape[1]), F32),
        ],
        axis=0,
    )
    ready(wo)
    rmix[...] = mm(wo[...], r_att, NT).astype(BF16)
    total[...] = jnp.zeros_like(total)
    ready(mixed_ref, den_ref, fq_ref)

    def head(h, carry):
        rows = pl.ds(pl.multiple_of(h * 64, 64), 64)
        rm = rmix[rows, :].astype(F32)
        inverse = 1.0 / den_ref[pl.ds(pl.multiple_of(h * 8, 8), 8), :][0:1]
        rn = (rm * inverse).astype(BF16)
        rd = -jnp.sum(rm * mixed_ref[rows, :].astype(F32), axis=0, keepdims=True) * inverse
        ra = aug_rows(rn, rd)
        raug_ref[pl.ds(pl.multiple_of(h * AUG, 16), AUG), :] = ra
        fq = fq_ref[pl.ds(pl.multiple_of(h * 128, 128), 128), :]
        for s in range(slots):
            part = slice(s * cols, (s + 1) * cols)
            state = mm(ra[:, part], fq[:, part], NT)
            total[s ^ meta[4], pl.ds(pl.multiple_of(h * KEEP, 8), KEEP), :] = state[:KEEP]
        return carry

    lax.fori_loop(0, heads, head, 0, unroll=UNROLL)
    spread_states(total, g_ref, parts, g_ref.shape[2])
    flush(g_ref, raug_ref)


def logits_back(p_both, g_both):
    p1, p2 = p_both[:64].astype(F32), p_both[64:].astype(F32)
    g1, g2 = g_both[:64], g_both[64:]
    s1 = jnp.sum(p1 * g1, axis=0, keepdims=True)
    s2 = jnp.sum(p2 * g2, axis=0, keepdims=True)
    return (p1 * (g1 - s1) - p2 * (g2 - s2)).astype(BF16)


def query_back_kernel(
    heads, slots, parts, meta, c_ref, raug_ref, fq_ref, qkv_ref, map_ref, mixed_ref, ratt_ref,
    rq_ref, gmap_ref, g0, g1, g2, g3, total,
):
    cols = fq_ref.shape[1] // slots
    ready(c_ref)
    collect_states(c_ref, total, parts, c_ref.shape[2])
    ready(raug_ref, fq_ref, qkv_ref)

    def head(h, carry):
        ra = raug_ref[pl.ds(pl.multiple_of(h * AUG, 16), AUG), :]
        fq = fq_ref[pl.ds(pl.multiple_of(h * 128, 128), 128), :]
        pieces = []
        for s in range(slots):
            part = slice(s * cols, (s + 1) * cols)
            c = total[s ^ meta[4], pl.ds(pl.multiple_of(h * KEEP, 8), AUG), :].astype(BF16)
            pieces.append(mm(c, ra[:, part], TN))
        r_fq = jnp.concatenate(pieces, axis=1).astype(BF16).astype(F32)
        r_l = logits_back(fq, r_fq)
        rows = pl.ds(pl.multiple_of(h * 64, 64), 64)
        rq_ref[rows, :] = mm(map_ref[h], r_l, NN).astype(BF16)
        gmap_ref[h] = mm(qkv_ref[rows, :], r_l, NT)
        return carry

    lax.fori_loop(0, heads, head, 0, unroll=UNROLL)
    flush(rq_ref, gmap_ref)
    ready(mixed_ref, ratt_ref)
    rows = g0.shape[0]
    for j, g in enumerate((g0, g1, g2, g3)):
        mixed = mixed_ref[pl.ds(pl.multiple_of(meta[j] * rows, 64), rows), :]
        g[...] = mm(mixed, ratt_ref[...], NN).astype(BF16)
        flush(g)


def key_back_kernel(
    heads, slots, parts, meta, d_ref, fk_ref, qkv_ref, map_ref, rq_ref, n_ref,
    rp_ref, gmap_ref, g1, g3, total,
):
    width = heads * 64
    cols = fk_ref.shape[1] // slots
    collect_states(d_ref, total, parts, d_ref.shape[2])
    ready(fk_ref, qkv_ref, rq_ref)
    rp_ref[0:width, :] = rq_ref[...]

    def head(h, carry):
        fk = fk_ref[pl.ds(pl.multiple_of(h * 128, 128), 128), :]
        v = qkv_ref[pl.ds(pl.multiple_of(width + h * 64, 64), 64), :]
        va = aug_rows(v, 1.0)
        pieces = []
        for s in range(slots):
            part = slice(s * cols, (s + 1) * cols)
            d = total[s ^ meta[4], pl.ds(pl.multiple_of(h * KEEP, 8), AUG), :].astype(BF16)
            pieces.append(mm(d, va[:, part], TN))
            rv = mm(d[:64], fk[:, part], NN).astype(BF16)
            rp_ref[pl.ds(pl.multiple_of(2 * width + h * 64, 64), 64), part] = rv
        r_fk = jnp.concatenate(pieces, axis=1).astype(BF16).astype(F32)
        r_l = logits_back(fk, r_fk)
        rows = pl.ds(pl.multiple_of(width + h * 64, 64), 64)
        rp_ref[rows, :] = mm(map_ref[h], r_l, NN).astype(BF16)
        keys = qkv_ref[pl.ds(pl.multiple_of(h * 64, 64), 64), :]
        gmap_ref[h] = mm(keys, r_l, NT)
        return carry

    lax.fori_loop(0, heads, head, 0, unroll=UNROLL)
    flush(rp_ref, gmap_ref)
    ready(n_ref)
    span = g1.shape[0]
    for j, g in ((1, g1), (3, g3)):
        rp = rp_ref[pl.ds(pl.multiple_of(meta[j] * span, 64), span), :]
        g[...] = mm(rp, n_ref[...], NN).astype(BF16)
        flush(g)


def project_grad_kernel(meta, rp_ref, n_ref, in0, in2, go0, go0_in, go2, go2_in, own, cross):
    span = in0.shape[0]
    ready(rp_ref, n_ref, in0, in2, go0, go0_in, go2, go2_in)
    for j, more, go, go_in, out in ((2, in2, go2, go2_in, cross), (0, in0, go0, go0_in, own)):
        rp = rp_ref[pl.ds(pl.multiple_of(meta[j] * span, 64), span), :]
        out[:span, :] = (mm(rp, n_ref[...], NN) + more[...].astype(F32)).astype(BF16)
        out[span:, :] = (go[...].astype(F32) + go_in[...].astype(F32)).astype(BF16)
        flush(out)


def input_kernel(
    heads, meta, rp_ref, x_ref, p_ref, gm_ref, out_ref, outin_ref, two_ref, ebo_ref, ebc_ref,
    mq_ref, mk_ref, w0, w1, w2, w3, dx_ref, full_ref, b0, b1, b2, b3, pack,
):
    ready(out_ref, outin_ref)
    full_ref[...] = out_ref[...] + outin_ref[...].astype(F32) + p_ref[5:6]
    flush(full_ref)
    span, width = w0.shape
    shard = width // 4
    own_heads = heads // 4
    ones = jnp.ones((8, x_ref.shape[0]), BF16)
    pack[...] = jnp.zeros_like(pack)
    gy = None
    ready(rp_ref, w0, w1, w2, w3, x_ref, gm_ref)
    for j, w in enumerate((w0, w1, w2, w3)):
        rp = rp_ref[pl.ds(pl.multiple_of(meta[j] * span, 64), span), :]
        part = mm(rp, w[...], TN)
        gy = part if gy is None else gy + part
        pack[meta[j], 8:16, :span] = mm(ones, rp, NT)
    ready(ebo_ref, ebc_ref, two_ref)
    pack[meta[0], 16:24, :] = ebo_ref[...]
    pack[meta[2], 16:24, :] = ebc_ref[...]
    normal, scale = norm_parts(x_ref[...].astype(F32))
    dx_ref[...] = gm_ref[...] + norm_back(gy, normal, scale, p_ref[0:1])
    flush(dx_ref)
    ready(mq_ref, mk_ref)
    lines = [
        jnp.sum(gy * normal, axis=0, keepdims=True),
        jnp.sum(gy, axis=0, keepdims=True),
        two_ref[0:1], two_ref[1:2], two_ref[2:3], two_ref[3:4],
    ]
    for i in range(4):
        cut = slice(i * shard, (i + 1) * shard)
        for k, line in enumerate(lines):
            pack[i, k : k + 1, :shard] = line[:, cut]
        for base, ref in ((24, mq_ref), (40, mk_ref)):
            for k in range(4):
                for h in range(own_heads):
                    at = k * shard + h * 64
                    pack[i, base : base + 16, at : at + 64] = ref[
                        i * own_heads + h, 16 * k : 16 * k + 16, :
                    ]
    for j, b in enumerate((b0, b1, b2, b3)):
        b[...] = pack[meta[j]].astype(BF16)


def unpack_kernel(rest_ref, g1, s1, g2, s2, bo, br, pb, eb, mq, mk):
    shard = g1.shape[1]
    own_heads = mq.shape[0]
    for k, ref in enumerate((g1, s1, g2, s2, bo, br)):
        ref[...] = rest_ref[k : k + 1, :shard]
    pb[...] = rest_ref[8:9, : pb.shape[1]]
    eb[...] = rest_ref[16:17, :]
    for base, ref in ((24, mq), (40, mk)):
        for k in range(4):
            for h in range(own_heads):
                at = k * shard + h * 64
                ref[h, 16 * k : 16 * k + 16, :] = rest_ref[base : base + 16, at : at + 64]


def line1(a):
    return a.reshape(-1)


def core_swap(a):
    return lax.ppermute(a, "fsdp", CORE)


def cross_swap(a):
    return lax.ppermute(a, "fsdp", CROSS)


def after(value, *others):
    return lax.optimization_barrier((value, *others))[0]


def spread(shard, cross):
    return [shard, core_swap(shard), cross, core_swap(cross)]


def add(a, b):
    return (a.astype(F32) + b.astype(F32)).astype(BF16)


def rows_sum(parts, start, size):
    out = None
    for offset, part in parts:
        if isinstance(part, tuple):
            part, offset = jnp.where(start + offset < part[0].shape[0], *part), -start
        piece = lax.dynamic_slice_in_dim(part, start + offset, size, 0).astype(F32)
        out = piece if out is None else out + piece
    return out.astype(BF16)


class Reduction:
    def __init__(self, parts, nctx, place):
        self.parts = [(0, part) for part in parts]
        self.rows, self.nctx, self.place = parts[0].shape[0], nctx, place
        self.groups = [[bit] for bit in range(nctx.bit_length() - 1)]

    def member(self, group):
        return sum(((self.place >> bit) & 1) << k for k, bit in enumerate(group))

    def send(self, value, group, other):
        flip = sum(((other >> k) & 1) << bit for k, bit in enumerate(group))
        return lax.ppermute(value, "ctx", [(i, i ^ flip) for i in range(self.nctx)])

    def scatter(self, level):
        group = self.groups[level]
        count = 1 << len(group)
        mine = self.member(group)
        self.rows //= count
        self.sent = [
            rows_sum(self.parts, (mine ^ d) * self.rows, self.rows) for d in range(1, count)
        ]
        got = [self.send(sent, group, d) for d, sent in enumerate(self.sent, 1)]
        self.parts = [
            (0, jnp.where(mine == 0, *part)) if isinstance(part, tuple)
            else (offset + mine * self.rows, part)
            for offset, part in self.parts
        ]
        self.fresh = len(got)
        self.parts += [(0, g) for g in got]
        return got

    def hold(self, *others):
        last = self.parts[-self.fresh :]
        held = lax.optimization_barrier((tuple(part for _, part in last), others))[0]
        self.parts[-self.fresh :] = [(at, part) for (at, _), part in zip(last, held)]

    def own(self):
        self.cur = rows_sum(self.parts, 0, self.rows)

    def spread(self, level):
        group = self.groups[level]
        self.others = [self.send(self.cur, group, d) for d in range(1, 1 << len(group))]
        self.level = level
        return self.others

    def join(self, *others):
        group = self.groups[self.level]
        parts = [self.cur, *self.others]
        if others:
            parts = list(lax.optimization_barrier((tuple(parts), others))[0])
        for k, bit in enumerate(group):
            swap = ((self.place >> bit) & 1) == 1
            parts = [
                jnp.where(swap, parts[j ^ (1 << k)], parts[j]) for j in range(len(parts))
            ]
        self.cur = jnp.concatenate(parts, axis=0)

    def deep(self, first):
        for level in range(first, len(self.groups)):
            self.scatter(level)
        self.own()
        for level in reversed(range(first, len(self.groups))):
            self.spread(level)
            self.join()


def straighten(parts, mine):
    a, b, c, d = parts
    odd = (mine & 1) == 1
    upper = (mine & 2) == 2
    a, b = jnp.where(odd, b, a), jnp.where(odd, a, b)
    c, d = jnp.where(odd, d, c), jnp.where(odd, c, d)
    return [
        jnp.where(upper, c, a), jnp.where(upper, d, b),
        jnp.where(upper, a, c), jnp.where(upper, b, d),
    ]


def exchange(a):
    return lax.all_to_all(a, "ctx", 0, 0, tiled=True)


def body(
    tokens, cotangent, pair_table, seq_ids, first_gain, first_shift, project_weight, project_bias,
    feature_query, feature_key, output_weight, output_bias, second_gain, second_shift,
    expand_weight, expand_bias, reduce_weight, reduce_bias,
):
    x = tokens[0]
    cot = cotangent[0]
    rows_n, width = x.shape
    heads = width // feature_query.shape[1]
    own_heads = feature_query.shape[0]
    slots = pair_table.shape[2]
    nctx = lax.axis_size("ctx")
    place = lax.axis_index("ctx")
    mine = lax.axis_index("fsdp")
    span = project_weight.shape[1]
    hidden_own = expand_weight.shape[1]
    shard = width // 4
    wide = heads * 128

    project_t = project_weight.T
    cross_project = cross_swap(project_t)
    vector = jnp.concatenate(
        [first_gain, first_shift, second_gain, second_shift, output_bias, reduce_bias,
         project_bias, expand_bias]
    )
    room = -vector.shape[0] % 1024
    vector = jnp.concatenate([vector, jnp.zeros((room,), BF16)]).reshape(-1, 64)
    map_rows = own_heads * 64
    pack = jnp.concatenate(
        [feature_query.reshape(-1, 64), feature_key.reshape(-1, 64), vector]
    )
    packs = spread(pack, cross_swap(pack))
    ordered = straighten(packs, mine)
    query_map = jnp.concatenate([p[:map_rows] for p in ordered]).reshape(heads, 64, 64)
    key_map = jnp.concatenate([p[map_rows : 2 * map_rows] for p in ordered]).reshape(heads, 64, 64)
    vectors = jnp.stack([p[2 * map_rows :] for p in ordered]).reshape(4, -1).astype(F32)
    params = vectors[:, : 6 * shard].reshape(4, 6, shard).transpose(1, 0, 2).reshape(6, width)
    project_line = vectors[:, 6 * shard : 6 * shard + span]
    expand_line = vectors[:, 6 * shard + span : 6 * shard + span + hidden_own]
    project_core = core_swap(project_t)
    project_far = core_swap(cross_project)
    projects = [project_t, project_core, cross_project, project_far]
    near_first = jnp.concatenate([expand_weight, output_weight])
    cross_first = cross_swap(after(near_first, cross_project))
    core_output = core_swap(output_weight)
    cross_reduce = cross_swap(after(reduce_weight, cross_first))
    cot_other = core_swap(cot)

    positions = pair_table[0, 0]
    swap = (positions[0] > positions[1]).astype(jnp.int32)
    meta = jnp.stack([mine, mine ^ 1, mine ^ 2, mine ^ 3, swap]).astype(jnp.int32)
    ids = seq_ids[0]
    same = (ids[1:] == ids[:-1]).astype(F32)
    none = jnp.zeros((1,), F32)
    keep = jnp.concatenate([none, same])
    keep_next = jnp.concatenate([same, none])

    rows_per = -(-(heads * KEEP) // (nctx * 16)) * 16
    state_shape = shaped((nctx, slots, rows_per, 128), BF16)
    total = pltpu.VMEM((slots, nctx * rows_per, 128), F32)
    wo_scratch = pltpu.VMEM((width, width), BF16)
    low = shaped((rows_n, width), BF16)
    full = shaped((rows_n, width))
    table = shaped((width, rows_n), BF16)
    square = shaped((heads, 64, 64))

    n1, near = call(
        near_kernel, [low, shaped((2 * span, rows_n), BF16)], "shvaav",
        [meta, x, params, projects[0], projects[1], project_line], "project_near", (), "hv",
    )
    (qkv,) = call(
        far_kernel, [shaped((3 * width, rows_n), BF16)], "shvaav",
        [meta, n1, near, projects[2], projects[3], project_line], "project_far",
    )
    fk, states = call(
        functools.partial(key_kernel, heads, slots, nctx),
        [shaped((wide, rows_n), BF16), state_shape], "svv",
        [meta, qkv, key_map], "keys", [total], "hh",
    )
    arrived = exchange(states)
    (fq,) = call(
        functools.partial(query_kernel, heads), [shaped((wide, rows_n), BF16)], "vv",
        [after(qkv, states), query_map], "queries", (), "h",
    )
    (running,) = call(
        functools.partial(scan_kernel, nctx, False), [state_shape], "sv",
        [keep, after(arrived, fq, cross_first)], "scan", (), "h",
    )
    carried = exchange(running)
    far_output = core_swap(after(cross_first, running)[width : width + shard])
    outputs = [output_weight, core_output, (cross_first, width, shard), far_output]
    mixed, den, middle, n2, wo = call(
        functools.partial(attend_kernel, heads, slots, nctx),
        [table, shaped((heads * 8, rows_n)), full, low, shaped((width, width), BF16)],
        "svhhaaaav", [meta, carried, fq, x, *outputs, params], "attend",
        [total], "hhhvh",
    )
    n2_other = core_swap(n2)

    def mlp(first, base, w_in, w_out, more, name):
        half = shaped((width // 2, hidden_own), BF16)
        grads = [half, half] if first else [shaped((width, hidden_own), BF16)]
        return call(
            functools.partial(mlp_kernel, first),
            [full, full, low, low, *grads, shaped((hidden_own, width), BF16),
             shaped((8, hidden_own))],
            "saaaaaa" + ("h" if first else "v") + "v" + "v" * len(more),
            [meta, n2, w_in, n2_other, cot, w_out, cot_other, base, expand_line, *more], name,
            [pltpu.VMEM((2, rows_n, hidden_own), BF16)] * 2,
            "vvvvhhhv" if first else "hvhhhhv", 48,
        )

    out1, dn1, out1_o, dn1_o, ge_top, ge_low, gr_cross, gb_cross = mlp(
        True, middle, (cross_first, 0, width), cross_reduce, [], "mlp_far"
    )
    top_in = cross_swap(ge_top)
    low_in = cross_swap(after(ge_low, top_in))
    out2, dn2, out2_o, dn2_o, ge_own, gr_own, gb_own = mlp(
        False, out1, expand_weight, reduce_weight, [dn1, out1_o, dn1_o], "mlp_near"
    )
    dn2_in = core_swap(dn2_o)

    g_middle, r_att, raug, g_states, small_two = call(
        functools.partial(middle_kernel, heads, slots, nctx),
        [full, low, shaped((heads * AUG, rows_n), BF16), state_shape, shaped((8, width))],
        "svahavhhhh",
        [meta, dn2, dn2_in, middle, cot, params, mixed, den, fq, wo], "middle",
        [total, pltpu.VMEM((width, rows_n), BF16)], "hhhhv",
    )
    g_arrived = exchange(g_states)
    gr_in = cross_swap(after(gr_cross, low_in))
    out2_in = core_swap(after(out2_o, g_states))
    rq, g_query_map, *go = call(
        functools.partial(query_back_kernel, heads, slots, nctx),
        [table, square] + [shaped((shard, width), BF16)] * 4,
        "sahhavhh", [meta, carried, raug, fq, (qkv, 0, width), query_map, mixed, r_att], "query_back",
        [total], "hhhhhh",
    )
    (g_running,) = call(
        functools.partial(scan_kernel, nctx, True), [state_shape], "sv",
        [keep_next, after(g_arrived, rq, low_in)], "scan_back", (), "h",
    )
    g_carried = exchange(g_running)
    top_in, low_in = lax.optimization_barrier((top_in, low_in, g_running))[:2]
    sum_e = Reduction([ge_own, (top_in, low_in)], nctx, place)
    e_got = sum_e.scatter(0)
    sum_r = Reduction([gr_own, after(gr_in, g_running)], nctx, place)
    r_got = sum_r.scatter(0)
    go_far, go_core = core_swap(after(go[3], g_running)), core_swap(after(go[1], g_running))
    rp, g_key_map, gp1, gp3 = call(
        functools.partial(key_back_kernel, heads, slots, nctx),
        [shaped((3 * width, rows_n), BF16), square] + [shaped((span, width), BF16)] * 2,
        "svhavhh", [meta, after(g_carried, sum_e.sent, sum_r.sent), fk, (qkv, width, 2 * width), key_map, rq, n1],
        "key_back", [total], "hhhh",
    )
    gp3_in, gp1_in = core_swap(after(gp3, e_got)), core_swap(after(gp1, e_got))
    p_own, p_cross = call(
        project_grad_kernel, [shaped((width, width), BF16)] * 2, "shhaahaha",
        [meta, rp, n1, gp1_in, gp3_in, go[0], go_core, go[2], go_far], "project_grad", (), "hh",
    )
    p_in = cross_swap(p_cross)
    sum_e.hold(p_own)
    sum_e.scatter(1)
    small = shaped((64, width), BF16)
    dx, layer_out, own_s, core_s, cross_s, far_s = call(
        functools.partial(input_kernel, heads), [full, full, small, small, small, small],
        "shhvhhaaaahhaaaa",
        [meta, rp, after(x, p_own, sum_e.sent), params, g_middle, out2, out2_in, small_two,
         gb_own, gb_cross, g_query_map, g_key_map, *projects],
        "input", [pltpu.VMEM((4, 64, width), F32)], "hhvvvv",
    )
    far_in, core_in = core_swap(far_s), core_swap(core_s)
    cross_in = cross_swap(add(cross_s, far_in))
    small_own = add(own_s, core_in)
    sum_e.hold(far_in, core_in)
    e_got = sum_e.scatter(2)
    sum_r.hold(far_in, core_in)
    r_got = sum_r.scatter(1)
    sum_p = Reduction([p_own, p_in], nctx, place)
    p_got = sum_p.scatter(0)
    sum_e.hold(sum_p.sent)
    sum_r.hold(sum_p.sent)
    sum_e.deep(3)
    e_got = sum_e.spread(2)
    r_got = sum_r.scatter(2)
    sum_p.hold(e_got, r_got)
    sum_p.scatter(1)
    sum_e.join(sum_p.sent)
    e_got = sum_e.spread(1)
    sum_r.hold(sum_p.sent)
    sum_r.deep(3)
    r_got = sum_r.spread(2)
    sum_p.hold(e_got, r_got)
    sum_p.scatter(2)
    sum_e.join(sum_p.sent)
    e_got = sum_e.spread(0)
    sum_r.join(sum_p.sent)
    r_got = sum_r.spread(1)
    sum_p.hold(r_got)
    sum_p.deep(3)
    sum_r.join(sum_p.cur)
    r_got = sum_r.spread(0)
    sum_p.spread(2)
    sum_p.join(e_got)
    sum_p.spread(1)
    sum_p.join(r_got)
    sum_p.spread(0)
    sum_p.join()
    sum_e.join()
    sum_r.join()
    g_expand, g_reduce, g_project = sum_e.cur, sum_r.cur, sum_p.cur
    rest = small_own.astype(F32) + cross_in.astype(F32)
    for level in range(len(sum_p.groups)):
        low_rest = rest.astype(BF16)
        rest = low_rest.astype(F32) + sum_p.send(low_rest, sum_p.groups[level], 1).astype(F32)
    g_output = g_project[span : span + shard]
    line = shaped((1, shard))
    g1, s1, g2, s2, bo, br, pb, eb, mq, mk = call(
        unpack_kernel,
        [line] * 6 + [shaped((1, span)), shaped((1, hidden_own))]
        + [shaped((own_heads, 64, 64))] * 2, "v", [rest], "unpack",
    )
    return (
        layer_out[None], dx[None], line1(g1), line1(s1), g_project[:span].T.astype(F32), line1(pb), mq, mk,
        g_output.astype(F32), line1(bo), line1(g2), line1(s2), g_expand.astype(F32), line1(eb),
        g_reduce.astype(F32), line1(br),
    )


def solution(mesh):
    row = P("fsdp", "ctx", None)
    vec = P("fsdp")
    maps = P("fsdp", None, None)
    in_specs = (
        row, row, row, P("fsdp", None), vec, vec, P(None, "fsdp"), vec, maps, maps,
        P("fsdp", None), vec, vec, vec, P(None, "fsdp"), vec, P("fsdp", None), vec,
    )
    out_specs = (
        row, row, vec, vec, P(None, "fsdp"), vec, maps, maps, P("fsdp", None), vec, vec, vec,
        P(None, "fsdp"), vec, P("fsdp", None), vec,
    )
    return jax.shard_map(body, mesh=mesh, in_specs=in_specs, out_specs=out_specs, check_vma=False)
```

```python
import functools

import jax
import jax.numpy as jnp
from jax import lax
from jax.experimental import pallas as pl
from jax.experimental.pallas import tpu as pltpu
from jax.sharding import PartitionSpec as P

EPS = 1e-05
F32 = jnp.float32
BF16 = jnp.bfloat16
AUG = 80
KEEP = 72
UNROLL = 3
NN = (((1,), (0,)), ((), ()))
NT = (((1,), (1,)), ((), ()))
TN = (((0,), (0,)), ((), ()))
CORE = [(i, i ^ 1) for i in range(4)]
CROSS = [(i, i ^ 2) for i in range(4)]
VMEM = pl.BlockSpec(memory_space=pltpu.VMEM)
SMEM = pl.BlockSpec(memory_space=pltpu.SMEM)
FAR = pl.BlockSpec(memory_space=pltpu.HBM)
ANYWHERE = pl.BlockSpec(memory_space=pl.ANY)
SPECS = {"v": VMEM, "s": SMEM, "h": FAR, "a": ANYWHERE}


def mm(a, b, dims):
    return lax.dot_general(a, b, dims, preferred_element_type=F32)


class Staged:
    def __init__(self, far, near, sems, out):
        self.near, self.state = near, "out" if out else "in"
        self.copies, at = [], 0
        for part, sem in zip(far, sems):
            here = near if len(far) == 1 else near.at[pl.ds(at, part.shape[0])]
            pair = (here, part) if out else (part, here)
            self.copies.append(pltpu.make_async_copy(*pair, sem))
            at += part.shape[0]
        self.shape, self.dtype = near.shape, near.dtype
        if not out:
            self.start()

    def start(self):
        for copy in self.copies:
            copy.start()

    def wait(self):
        for copy in self.copies:
            copy.wait()

    def ready(self):
        if self.state == "in":
            self.wait()
            self.state = "ready"

    def flush(self):
        if self.state == "out":
            self.start()
            self.state = "flushed"

    def finish(self):
        self.ready()
        self.flush()
        if self.state == "flushed":
            self.wait()
            self.state = "done"

    def __getitem__(self, index):
        assert self.state in ("ready", "out", "flushed")
        return self.near[index]

    def __setitem__(self, index, value):
        assert self.state == "out"
        self.near[index] = value


def ready(*refs):
    for ref in refs:
        if isinstance(ref, Staged):
            ref.ready()


def flush(*refs):
    for ref in refs:
        if isinstance(ref, Staged):
            ref.flush()


def call(kernel, outs, kinds, args, name, scratch=(), out_kinds=None, limit=32, flops=1):
    out_kinds = out_kinds or "v" * len(outs)
    both = kinds + out_kinds
    groups = [a if isinstance(a, list) else [a] for a in [*args, *outs]]
    groups = [
        [p if isinstance(p, tuple) else (p, 0, p.shape[0]) for p in group] for group in groups
    ]
    operands = [(p[0], k) for group, k in zip(groups[: len(kinds)], kinds) for p in group]
    pieces = sum(len(group) for group, k in zip(groups, both) if k in "ha")
    staged = [
        pltpu.VMEM((sum(p[2] for p in group), *group[0][0].shape[1:]), group[0][0].dtype)
        for group, k in zip(groups, both) if k in "ha"
    ]

    def run(*refs):
        count = sum(len(group) for group in groups)
        extra = len(staged)
        near = refs[count : count + extra]
        sems = refs[count + extra] if extra else None
        rest = refs[count + extra + (1 if extra else 0) :]
        use, at, ref_at, sem_at = [], 0, 0, 0
        for i, (kind, group) in enumerate(zip(both, groups)):
            mine = refs[ref_at : ref_at + len(group)]
            ref_at += len(group)
            if kind in "ha":
                far = [
                    ref if ref.shape[0] == size else ref.at[pl.ds(start, size)]
                    for ref, (_, start, size) in zip(mine, group)
                ]
                own = [sems.at[sem_at + j] for j in range(len(group))]
                sem_at += len(group)
                use.append(Staged(far, near[at], own, i >= len(kinds)))
                at += 1
            else:
                use.append(mine[0])
        kernel(*use, *rest)
        for ref in use:
            if isinstance(ref, Staged):
                ref.finish()

    sems = [pltpu.SemaphoreType.DMA((pieces,))] if staged else []
    return pl.pallas_call(
        run,
        out_shape=[
            pltpu.HBM(o.shape, o.dtype) if k == "h" else o for o, k in zip(outs, out_kinds)
        ],
        in_specs=[SPECS[k] for _, k in operands],
        out_specs=[SPECS[k] for k in out_kinds],
        scratch_shapes=[*staged, *sems, *scratch],
        compiler_params=pltpu.CompilerParams(vmem_limit_bytes=limit << 20),
        cost_estimate=pl.CostEstimate(flops=flops, bytes_accessed=1, transcendentals=0),
        name=name,
    )(*[
        pltpu.with_memory_space_constraint(a, pltpu.HBM) if k == "h" else a
        for a, k in operands
    ])


def shaped(shape, dtype=F32):
    return jax.ShapeDtypeStruct(shape, dtype)


def norm_parts(v):
    center = v - jnp.mean(v, axis=-1, keepdims=True)
    scale = lax.rsqrt(jnp.mean(center * center, axis=-1, keepdims=True) + EPS)
    return center * scale, scale


def norm_back(gy, normal, scale, gain):
    a = gy * gain
    return (
        a - jnp.mean(a, axis=-1, keepdims=True)
        - normal * jnp.mean(a * normal, axis=-1, keepdims=True)
    ) * scale


def aug_rows(top, row):
    index = lax.broadcasted_iota(jnp.int32, (AUG - top.shape[0], top.shape[1]), 0)
    tail = jnp.where(index == 0, row, 0.0).astype(BF16)
    return jnp.concatenate([top, tail], axis=0)


def spread_states(total_ref, out_ref, parts, rows_per):
    for part in range(parts):
        out_ref[part] = total_ref[:, part * rows_per : (part + 1) * rows_per, :].astype(BF16)


def collect_states(in_ref, total_ref, parts, rows_per):
    for part in range(parts):
        total_ref[:, part * rows_per : (part + 1) * rows_per, :] = in_ref[part].astype(F32)


def project_rows(meta, j, w, n, pb_ref):
    line = jnp.broadcast_to(pb_ref[pl.ds(meta[j], 1), :], (128, w.shape[0])).T
    bias = jnp.concatenate([line] * (n.shape[0] // 128), axis=1)
    return (mm(w[...], n, NT) + bias).astype(BF16)


def near_kernel(meta, x_ref, p_ref, w0, w1, pb_ref, n_ref, half_ref):
    ready(x_ref)
    normal, _ = norm_parts(x_ref[...].astype(F32))
    n = (normal * p_ref[0:1] + p_ref[1:2]).astype(BF16)
    n_ref[...] = n
    flush(n_ref)
    span = w0.shape[0]
    for j, w in enumerate((w0, w1)):
        ready(w)
        start = pl.multiple_of((meta[j] & 1) * span, 64)
        half_ref[pl.ds(start, span), :] = project_rows(meta, j, w, n, pb_ref)


def far_kernel(meta, n_ref, near_ref, w2, w3, pb_ref, qkv_ref):
    span = w2.shape[0]
    ready(n_ref)
    start = pl.multiple_of((meta[0] >> 1) * 2 * span, 64)
    qkv_ref[pl.ds(start, 2 * span), :] = near_ref[...]
    for j, w in ((2, w2), (3, w3)):
        ready(w)
        start = pl.multiple_of(meta[j] * span, 64)
        qkv_ref[pl.ds(start, span), :] = project_rows(meta, j, w, n_ref[...], pb_ref)


def phi(rows_ref, base, map_ref, h):
    rows = rows_ref[pl.ds(pl.multiple_of(base + h * 64, 64), 64), :]
    logits = mm(map_ref[h], rows, TN)
    up = jnp.exp(logits - jnp.max(logits, axis=0, keepdims=True))
    down = jnp.exp(jnp.min(logits, axis=0, keepdims=True) - logits)
    p1 = up * (1.0 / jnp.sum(up, axis=0, keepdims=True))
    p2 = down * (1.0 / jnp.sum(down, axis=0, keepdims=True))
    return p1.astype(BF16), p2.astype(BF16)


def key_kernel(heads, slots, parts, meta, qkv_ref, map_ref, fk_ref, s_ref, total):
    width = heads * 64
    cols = qkv_ref.shape[1] // slots
    rows_per = s_ref.shape[2]
    total[...] = jnp.zeros_like(total)

    def head(h, carry):
        p1, p2 = phi(qkv_ref, width, map_ref, h)
        at = pl.multiple_of(h * 128, 128)
        fk_ref[pl.ds(at, 64), :] = p1
        fk_ref[pl.ds(pl.multiple_of(at + 64, 64), 64), :] = p2
        v = qkv_ref[pl.ds(pl.multiple_of(2 * width + h * 64, 64), 64), :]
        va = aug_rows(v, 1.0)
        fk = jnp.concatenate([p1, p2], axis=0)
        for s in range(slots):
            part = slice(s * cols, (s + 1) * cols)
            state = mm(va[:, part], fk[:, part], NT)
            total[s ^ meta[4], pl.ds(pl.multiple_of(h * KEEP, 8), KEEP), :] = state[:KEEP]
        return carry

    lax.fori_loop(0, heads, head, 0, unroll=UNROLL)
    flush(fk_ref)
    spread_states(total, s_ref, parts, rows_per)


def query_kernel(heads, qkv_ref, map_ref, fq_ref):
    def head(h, carry):
        p1, p2 = phi(qkv_ref, 0, map_ref, h)
        at = pl.multiple_of(h * 128, 128)
        fq_ref[pl.ds(at, 64), :] = p1
        fq_ref[pl.ds(pl.multiple_of(at + 64, 64), 64), :] = p2
        return carry

    lax.fori_loop(0, heads, head, 0, unroll=UNROLL)


def scan_kernel(nctx, backward, keep, in_ref, out_ref):
    blocks = 2 * nctx
    order = [(b, 0) if b < nctx else (blocks - 1 - b, 1) for b in range(blocks)]
    acc = jnp.zeros(in_ref.shape[2:], F32)
    for b in reversed(range(blocks)) if backward else range(blocks):
        c, lane = order[b]
        acc = acc * keep[b] + in_ref[c, lane].astype(F32)
        out_ref[c, lane] = acc.astype(BF16)


def fill_output(meta, wo_refs, wo):
    rows = wo_refs[0].shape[0]
    for j, ref in enumerate(wo_refs):
        wo[pl.ds(pl.multiple_of(meta[j] * rows, 64), rows), :] = ref[...]


def attend_kernel(
    heads, slots, parts, meta, c_ref, fq_ref, x_ref, w0, w1, w2, w3, p_ref,
    mixed_ref, den_ref, middle_ref, n2_ref, wo, total,
):
    cols = fq_ref.shape[1] // slots
    collect_states(c_ref, total, parts, c_ref.shape[2])
    ready(fq_ref)

    def head(h, carry):
        fq = fq_ref[pl.ds(pl.multiple_of(h * 128, 128), 128), :]
        for s in range(slots):
            part = slice(s * cols, (s + 1) * cols)
            c = total[s ^ meta[4], pl.ds(pl.multiple_of(h * KEEP, 8), AUG), :].astype(BF16)
            both = mm(c, fq[:, part], NN)
            den = both[64:65]
            mixed = both[:64] * (1.0 / den)
            mixed_ref[pl.ds(pl.multiple_of(h * 64, 64), 64), part] = mixed.astype(BF16)
            den_ref[pl.ds(pl.multiple_of(h * 8, 8), 8), part] = jnp.broadcast_to(den, (8, cols))
        return carry

    lax.fori_loop(0, heads, head, 0, unroll=UNROLL)
    flush(mixed_ref, den_ref)
    ready(x_ref, w0, w1, w2, w3)
    fill_output(meta, (w0, w1, w2, w3), wo)
    flush(wo)
    middle = x_ref[...].astype(F32) + mm(mixed_ref[...], wo[...], TN) + p_ref[4:5]
    middle_ref[...] = middle
    flush(middle_ref)
    normal, _ = norm_parts(middle)
    n2 = (normal * p_ref[2:3] + p_ref[3:4]).astype(BF16)
    n2_ref[...] = n2


def mlp_kernel(first, meta, n2_ref, we, n2o_ref, cot_ref, wr, coto_ref, base_ref, eb_ref, *refs):
    if first:
        out_ref, dn_ref, outo_ref, dno_ref, ge, ge_low, gr, gb_ref, act, hid = refs
    else:
        back_ref, baseo_ref, backo_ref, out_ref, dn_ref, outo_ref, dno_ref, ge, gr, gb_ref, act, hid = refs
    rows_n, width = n2_ref.shape
    line = meta[2] if first else meta[0]
    tile = we.shape[1] // 2
    ready(n2_ref, we, n2o_ref, cot_ref, wr, coto_ref)

    def step(t, carry):
        at = pl.ds(pl.multiple_of(t * tile, tile), tile)
        bias = eb_ref[pl.ds(line, 1), at]
        pre = [
            (mm(n[...], we[:, at], NN) + bias, mm(c[...], wr[at, :], NT))
            for n, c in ((n2_ref, cot_ref), (n2o_ref, coto_ref))
        ]
        actives, hiddens, sums = [], [], None
        for k, (hidden, back) in enumerate(pre):
            square = hidden * hidden
            part = 0.5 + 0.5 * jnp.tanh(
                hidden * (0.7978845608028654 + 0.035677408136300125 * square)
            )
            active = hidden * part
            slope = part + active * (1.0 - part) * (
                1.5957691216057308 + 0.21406444881780075 * square
            )
            r_hidden = back.astype(BF16).astype(F32) * slope
            actives.append(active.astype(BF16))
            hiddens.append(r_hidden.astype(BF16))
            act[k, :, at] = actives[k]
            hid[k, :, at] = hiddens[k]
            total = jnp.sum(r_hidden, axis=0, keepdims=True)
            sums = total if sums is None else sums + total
        gb_ref[:, at] = jnp.broadcast_to(sums, (8, tile))
        grad = (mm(n2_ref[...], hiddens[0], TN) + mm(n2o_ref[...], hiddens[1], TN)).astype(BF16)
        if first:
            ge[:, at] = grad[: width // 2]
            ge_low[:, at] = grad[width // 2 :]
        else:
            ge[:, at] = grad
        gr[at, :] = (
            mm(actives[0], cot_ref[...], TN) + mm(actives[1], coto_ref[...], TN)
        ).astype(BF16)
        return carry

    lax.fori_loop(0, 2, step, 0)
    flush(ge, gr)
    if first:
        flush(ge_low)
    ready(base_ref)
    dno = mm(hid[1], we[...], NT)
    outo = mm(act[1], wr[...], NN)
    if first:
        dno_ref[...] = dno.astype(BF16)
        outo_ref[...] = outo.astype(BF16)
        dn_ref[...] = mm(hid[0], we[...], NT)
    else:
        dno_ref[...] = (backo_ref[...].astype(F32) + dno).astype(BF16)
        flush(dno_ref)
        outo_ref[...] = (baseo_ref[...].astype(F32) + outo).astype(BF16)
        flush(outo_ref)
        dn_ref[...] = back_ref[...] + mm(hid[0], we[...], NT)
    out_ref[...] = base_ref[...] + mm(act[0], wr[...], NN)


def middle_kernel(
    heads, slots, parts, meta, dn_ref, dnin_ref, middle_ref, cot_ref, p_ref, mixed_ref, den_ref, fq_ref,
    wo, gm_ref, ratt_ref, raug_ref, g_ref, small_ref, total, rmix,
):
    cols = fq_ref.shape[1] // slots
    ready(middle_ref, dnin_ref, cot_ref)
    normal, scale = norm_parts(middle_ref[...])
    gy = dn_ref[...] + dnin_ref[...].astype(F32)
    cot = cot_ref[...].astype(F32)
    g_middle = cot + norm_back(gy, normal, scale, p_ref[2:3])
    gm_ref[...] = g_middle
    r_att = g_middle.astype(BF16)
    ratt_ref[...] = r_att
    flush(gm_ref, ratt_ref)
    small_ref[...] = jnp.concatenate(
        [
            jnp.sum(gy * normal, axis=0, keepdims=True),
            jnp.sum(gy, axis=0, keepdims=True),
            jnp.sum(r_att.astype(F32), axis=0, keepdims=True),
            jnp.sum(cot, axis=0, keepdims=True),
            jnp.zeros((4, gy.shape[1]), F32),
        ],
        axis=0,
    )
    ready(wo)
    rmix[...] = mm(wo[...], r_att, NT).astype(BF16)
    total[...] = jnp.zeros_like(total)
    ready(mixed_ref, den_ref, fq_ref)

    def head(h, carry):
        rows = pl.ds(pl.multiple_of(h * 64, 64), 64)
        rm = rmix[rows, :].astype(F32)
        inverse = 1.0 / den_ref[pl.ds(pl.multiple_of(h * 8, 8), 8), :][0:1]
        rn = (rm * inverse).astype(BF16)
        rd = -jnp.sum(rm * mixed_ref[rows, :].astype(F32), axis=0, keepdims=True) * inverse
        ra = aug_rows(rn, rd)
        raug_ref[pl.ds(pl.multiple_of(h * AUG, 16), AUG), :] = ra
        fq = fq_ref[pl.ds(pl.multiple_of(h * 128, 128), 128), :]
        for s in range(slots):
            part = slice(s * cols, (s + 1) * cols)
            state = mm(ra[:, part], fq[:, part], NT)
            total[s ^ meta[4], pl.ds(pl.multiple_of(h * KEEP, 8), KEEP), :] = state[:KEEP]
        return carry

    lax.fori_loop(0, heads, head, 0, unroll=UNROLL)
    spread_states(total, g_ref, parts, g_ref.shape[2])
    flush(g_ref, raug_ref)


def logits_back(p_both, g_both):
    p1, p2 = p_both[:64].astype(F32), p_both[64:].astype(F32)
    g1, g2 = g_both[:64], g_both[64:]
    s1 = jnp.sum(p1 * g1, axis=0, keepdims=True)
    s2 = jnp.sum(p2 * g2, axis=0, keepdims=True)
    return (p1 * (g1 - s1) - p2 * (g2 - s2)).astype(BF16)


def query_back_kernel(
    heads, slots, parts, meta, c_ref, raug_ref, fq_ref, qkv_ref, map_ref, mixed_ref, ratt_ref,
    rq_ref, gmap_ref, g0, g1, g2, g3, total,
):
    cols = fq_ref.shape[1] // slots
    ready(c_ref)
    collect_states(c_ref, total, parts, c_ref.shape[2])
    ready(raug_ref, fq_ref, qkv_ref)

    def head(h, carry):
        ra = raug_ref[pl.ds(pl.multiple_of(h * AUG, 16), AUG), :]
        fq = fq_ref[pl.ds(pl.multiple_of(h * 128, 128), 128), :]
        pieces = []
        for s in range(slots):
            part = slice(s * cols, (s + 1) * cols)
            c = total[s ^ meta[4], pl.ds(pl.multiple_of(h * KEEP, 8), AUG), :].astype(BF16)
            pieces.append(mm(c, ra[:, part], TN))
        r_fq = jnp.concatenate(pieces, axis=1).astype(BF16).astype(F32)
        r_l = logits_back(fq, r_fq)
        rows = pl.ds(pl.multiple_of(h * 64, 64), 64)
        rq_ref[rows, :] = mm(map_ref[h], r_l, NN).astype(BF16)
        gmap_ref[h] = mm(qkv_ref[rows, :], r_l, NT)
        return carry

    lax.fori_loop(0, heads, head, 0, unroll=UNROLL)
    flush(rq_ref, gmap_ref)
    ready(mixed_ref, ratt_ref)
    rows = g0.shape[0]
    for j, g in enumerate((g0, g1, g2, g3)):
        mixed = mixed_ref[pl.ds(pl.multiple_of(meta[j] * rows, 64), rows), :]
        g[...] = mm(mixed, ratt_ref[...], NN).astype(BF16)
        flush(g)


def key_back_kernel(
    heads, slots, parts, meta, d_ref, fk_ref, qkv_ref, map_ref, rq_ref, n_ref,
    rp_ref, gmap_ref, g1, g3, total,
):
    width = heads * 64
    cols = fk_ref.shape[1] // slots
    collect_states(d_ref, total, parts, d_ref.shape[2])
    ready(fk_ref, qkv_ref, rq_ref)
    rp_ref[0:width, :] = rq_ref[...]

    def head(h, carry):
        fk = fk_ref[pl.ds(pl.multiple_of(h * 128, 128), 128), :]
        v = qkv_ref[pl.ds(pl.multiple_of(width + h * 64, 64), 64), :]
        va = aug_rows(v, 1.0)
        pieces = []
        for s in range(slots):
            part = slice(s * cols, (s + 1) * cols)
            d = total[s ^ meta[4], pl.ds(pl.multiple_of(h * KEEP, 8), AUG), :].astype(BF16)
            pieces.append(mm(d, va[:, part], TN))
            rv = mm(d[:64], fk[:, part], NN).astype(BF16)
            rp_ref[pl.ds(pl.multiple_of(2 * width + h * 64, 64), 64), part] = rv
        r_fk = jnp.concatenate(pieces, axis=1).astype(BF16).astype(F32)
        r_l = logits_back(fk, r_fk)
        rows = pl.ds(pl.multiple_of(width + h * 64, 64), 64)
        rp_ref[rows, :] = mm(map_ref[h], r_l, NN).astype(BF16)
        keys = qkv_ref[pl.ds(pl.multiple_of(h * 64, 64), 64), :]
        gmap_ref[h] = mm(keys, r_l, NT)
        return carry

    lax.fori_loop(0, heads, head, 0, unroll=UNROLL)
    flush(rp_ref, gmap_ref)
    ready(n_ref)
    span = g1.shape[0]
    for j, g in ((1, g1), (3, g3)):
        rp = rp_ref[pl.ds(pl.multiple_of(meta[j] * span, 64), span), :]
        g[...] = mm(rp, n_ref[...], NN).astype(BF16)
        flush(g)


def project_grad_kernel(meta, rp_ref, n_ref, in0, in2, go0, go0_in, go2, go2_in, own, cross):
    span = in0.shape[0]
    ready(rp_ref, n_ref, in0, in2, go0, go0_in, go2, go2_in)
    for j, more, go, go_in, out in ((2, in2, go2, go2_in, cross), (0, in0, go0, go0_in, own)):
        rp = rp_ref[pl.ds(pl.multiple_of(meta[j] * span, 64), span), :]
        out[:span, :] = (mm(rp, n_ref[...], NN) + more[...].astype(F32)).astype(BF16)
        out[span:, :] = (go[...].astype(F32) + go_in[...].astype(F32)).astype(BF16)
        flush(out)


def input_kernel(
    heads, meta, rp_ref, x_ref, p_ref, gm_ref, out_ref, outin_ref, two_ref, ebo_ref, ebc_ref,
    mq_ref, mk_ref, w0, w1, w2, w3, dx_ref, full_ref, b0, b1, b2, b3, pack,
):
    ready(out_ref, outin_ref)
    full_ref[...] = out_ref[...] + outin_ref[...].astype(F32) + p_ref[5:6]
    flush(full_ref)
    span, width = w0.shape
    shard = width // 4
    own_heads = heads // 4
    ones = jnp.ones((8, x_ref.shape[0]), BF16)
    pack[...] = jnp.zeros_like(pack)
    gy = None
    ready(rp_ref, w0, w1, w2, w3, x_ref, gm_ref)
    for j, w in enumerate((w0, w1, w2, w3)):
        rp = rp_ref[pl.ds(pl.multiple_of(meta[j] * span, 64), span), :]
        part = mm(rp, w[...], TN)
        gy = part if gy is None else gy + part
        pack[meta[j], 8:16, :span] = mm(ones, rp, NT)
    ready(ebo_ref, ebc_ref, two_ref)
    pack[meta[0], 16:24, :] = ebo_ref[...]
    pack[meta[2], 16:24, :] = ebc_ref[...]
    normal, scale = norm_parts(x_ref[...].astype(F32))
    dx_ref[...] = gm_ref[...] + norm_back(gy, normal, scale, p_ref[0:1])
    flush(dx_ref)
    ready(mq_ref, mk_ref)
    lines = [
        jnp.sum(gy * normal, axis=0, keepdims=True),
        jnp.sum(gy, axis=0, keepdims=True),
        two_ref[0:1], two_ref[1:2], two_ref[2:3], two_ref[3:4],
    ]
    for i in range(4):
        cut = slice(i * shard, (i + 1) * shard)
        for k, line in enumerate(lines):
            pack[i, k : k + 1, :shard] = line[:, cut]
        for base, ref in ((24, mq_ref), (40, mk_ref)):
            for k in range(4):
                for h in range(own_heads):
                    at = k * shard + h * 64
                    pack[i, base : base + 16, at : at + 64] = ref[
                        i * own_heads + h, 16 * k : 16 * k + 16, :
                    ]
    for j, b in enumerate((b0, b1, b2, b3)):
        b[...] = pack[meta[j]].astype(BF16)


def unpack_kernel(rest_ref, g1, s1, g2, s2, bo, br, pb, eb, mq, mk):
    shard = g1.shape[1]
    own_heads = mq.shape[0]
    for k, ref in enumerate((g1, s1, g2, s2, bo, br)):
        ref[...] = rest_ref[k : k + 1, :shard]
    pb[...] = rest_ref[8:9, : pb.shape[1]]
    eb[...] = rest_ref[16:17, :]
    for base, ref in ((24, mq), (40, mk)):
        for k in range(4):
            for h in range(own_heads):
                at = k * shard + h * 64
                ref[h, 16 * k : 16 * k + 16, :] = rest_ref[base : base + 16, at : at + 64]


def line1(a):
    return a.reshape(-1)


def core_swap(a):
    return lax.ppermute(a, "fsdp", CORE)


def cross_swap(a):
    return lax.ppermute(a, "fsdp", CROSS)


def after(value, *others):
    return lax.optimization_barrier((value, *others))[0]


def spread(shard, cross):
    return [shard, core_swap(shard), cross, core_swap(cross)]


def add(a, b):
    return (a.astype(F32) + b.astype(F32)).astype(BF16)


def rows_sum(parts, start, size):
    out = None
    for offset, part in parts:
        if isinstance(part, tuple):
            part, offset = jnp.where(start + offset < part[0].shape[0], *part), -start
        piece = lax.dynamic_slice_in_dim(part, start + offset, size, 0).astype(F32)
        out = piece if out is None else out + piece
    return out.astype(BF16)


class Reduction:
    def __init__(self, parts, nctx, place):
        self.parts = [(0, part) for part in parts]
        self.rows, self.nctx, self.place = parts[0].shape[0], nctx, place
        self.groups = [[bit] for bit in range(nctx.bit_length() - 1)]

    def member(self, group):
        return sum(((self.place >> bit) & 1) << k for k, bit in enumerate(group))

    def send(self, value, group, other):
        flip = sum(((other >> k) & 1) << bit for k, bit in enumerate(group))
        return lax.ppermute(value, "ctx", [(i, i ^ flip) for i in range(self.nctx)])

    def scatter(self, level):
        group = self.groups[level]
        count = 1 << len(group)
        mine = self.member(group)
        self.rows //= count
        self.sent = [
            rows_sum(self.parts, (mine ^ d) * self.rows, self.rows) for d in range(1, count)
        ]
        got = [self.send(sent, group, d) for d, sent in enumerate(self.sent, 1)]
        self.parts = [
            (0, jnp.where(mine == 0, *part)) if isinstance(part, tuple)
            else (offset + mine * self.rows, part)
            for offset, part in self.parts
        ]
        self.fresh = len(got)
        self.parts += [(0, g) for g in got]
        return got

    def hold(self, *others):
        last = self.parts[-self.fresh :]
        held = lax.optimization_barrier((tuple(part for _, part in last), others))[0]
        self.parts[-self.fresh :] = [(at, part) for (at, _), part in zip(last, held)]

    def own(self):
        self.cur = rows_sum(self.parts, 0, self.rows)

    def spread(self, level):
        group = self.groups[level]
        self.others = [self.send(self.cur, group, d) for d in range(1, 1 << len(group))]
        self.level = level
        return self.others

    def join(self, *others):
        group = self.groups[self.level]
        parts = [self.cur, *self.others]
        if others:
            parts = list(lax.optimization_barrier((tuple(parts), others))[0])
        for k, bit in enumerate(group):
            swap = ((self.place >> bit) & 1) == 1
            parts = [
                jnp.where(swap, parts[j ^ (1 << k)], parts[j]) for j in range(len(parts))
            ]
        self.cur = jnp.concatenate(parts, axis=0)

    def deep(self, first):
        for level in range(first, len(self.groups)):
            self.scatter(level)
        self.own()
        for level in reversed(range(first, len(self.groups))):
            self.spread(level)
            self.join()


def straighten(parts, mine):
    a, b, c, d = parts
    odd = (mine & 1) == 1
    upper = (mine & 2) == 2
    a, b = jnp.where(odd, b, a), jnp.where(odd, a, b)
    c, d = jnp.where(odd, d, c), jnp.where(odd, c, d)
    return [
        jnp.where(upper, c, a), jnp.where(upper, d, b),
        jnp.where(upper, a, c), jnp.where(upper, b, d),
    ]


def exchange(a):
    return lax.all_to_all(a, "ctx", 0, 0, tiled=True)


def body(
    tokens, cotangent, pair_table, seq_ids, first_gain, first_shift, project_weight, project_bias,
    feature_query, feature_key, output_weight, output_bias, second_gain, second_shift,
    expand_weight, expand_bias, reduce_weight, reduce_bias,
):
    x = tokens[0]
    cot = cotangent[0]
    rows_n, width = x.shape
    heads = width // feature_query.shape[1]
    own_heads = feature_query.shape[0]
    slots = pair_table.shape[2]
    nctx = lax.axis_size("ctx")
    place = lax.axis_index("ctx")
    mine = lax.axis_index("fsdp")
    span = project_weight.shape[1]
    hidden_own = expand_weight.shape[1]
    shard = width // 4
    wide = heads * 128

    project_t = project_weight.T
    cross_project = cross_swap(project_t)
    vector = jnp.concatenate(
        [first_gain, first_shift, second_gain, second_shift, output_bias, reduce_bias,
         project_bias, expand_bias]
    )
    room = -vector.shape[0] % 1024
    vector = jnp.concatenate([vector, jnp.zeros((room,), BF16)]).reshape(-1, 64)
    map_rows = own_heads * 64
    pack = jnp.concatenate(
        [feature_query.reshape(-1, 64), feature_key.reshape(-1, 64), vector]
    )
    packs = spread(pack, cross_swap(pack))
    ordered = straighten(packs, mine)
    query_map = jnp.concatenate([p[:map_rows] for p in ordered]).reshape(heads, 64, 64)
    key_map = jnp.concatenate([p[map_rows : 2 * map_rows] for p in ordered]).reshape(heads, 64, 64)
    vectors = jnp.stack([p[2 * map_rows :] for p in ordered]).reshape(4, -1).astype(F32)
    params = vectors[:, : 6 * shard].reshape(4, 6, shard).transpose(1, 0, 2).reshape(6, width)
    project_line = vectors[:, 6 * shard : 6 * shard + span]
    expand_line = vectors[:, 6 * shard + span : 6 * shard + span + hidden_own]
    project_core = core_swap(project_t)
    project_far = core_swap(cross_project)
    projects = [project_t, project_core, cross_project, project_far]
    near_first = jnp.concatenate([expand_weight, output_weight])
    cross_first = cross_swap(after(near_first, cross_project))
    core_output = core_swap(output_weight)
    cross_reduce = cross_swap(after(reduce_weight, cross_first))
    cot_other = core_swap(cot)

    positions = pair_table[0, 0]
    swap = (positions[0] > positions[1]).astype(jnp.int32)
    meta = jnp.stack([mine, mine ^ 1, mine ^ 2, mine ^ 3, swap]).astype(jnp.int32)
    ids = seq_ids[0]
    same = (ids[1:] == ids[:-1]).astype(F32)
    none = jnp.zeros((1,), F32)
    keep = jnp.concatenate([none, same])
    keep_next = jnp.concatenate([same, none])

    rows_per = -(-(heads * KEEP) // (nctx * 16)) * 16
    state_shape = shaped((nctx, slots, rows_per, 128), BF16)
    total = pltpu.VMEM((slots, nctx * rows_per, 128), F32)
    wo_scratch = pltpu.VMEM((width, width), BF16)
    low = shaped((rows_n, width), BF16)
    full = shaped((rows_n, width))
    table = shaped((width, rows_n), BF16)
    square = shaped((heads, 64, 64))

    n1, near = call(
        near_kernel, [low, shaped((2 * span, rows_n), BF16)], "shvaav",
        [meta, x, params, projects[0], projects[1], project_line], "project_near", (), "hv",
    )
    (qkv,) = call(
        far_kernel, [shaped((3 * width, rows_n), BF16)], "shvaav",
        [meta, n1, near, projects[2], projects[3], project_line], "project_far",
    )
    fk, states = call(
        functools.partial(key_kernel, heads, slots, nctx),
        [shaped((wide, rows_n), BF16), state_shape], "svv",
        [meta, qkv, key_map], "keys", [total], "hh",
    )
    arrived = exchange(states)
    (fq,) = call(
        functools.partial(query_kernel, heads), [shaped((wide, rows_n), BF16)], "vv",
        [after(qkv, states), query_map], "queries", (), "h", flops=10**12,
    )
    (running,) = call(
        functools.partial(scan_kernel, nctx, False), [state_shape], "sv",
        [keep, after(arrived, cross_first)], "scan", (), "h",
    )
    carried = exchange(running)
    far_output = core_swap(after(cross_first, running)[width : width + shard])
    outputs = [output_weight, core_output, (cross_first, width, shard), far_output]
    mixed, den, middle, n2, wo = call(
        functools.partial(attend_kernel, heads, slots, nctx),
        [table, shaped((heads * 8, rows_n)), full, low, shaped((width, width), BF16)],
        "svhhhvavv", [meta, carried, fq, x, *outputs, params], "attend",
        [total], "hhhvh",
    )
    n2_other = core_swap(n2)

    def mlp(first, base, w_in, w_out, more, name):
        half = shaped((width // 2, hidden_own), BF16)
        grads = [half, half] if first else [shaped((width, hidden_own), BF16)]
        return call(
            functools.partial(mlp_kernel, first),
            [full, full, low, low, *grads, shaped((hidden_own, width), BF16),
             shaped((8, hidden_own))],
            "saaaaaa" + ("h" if first else "v") + "v" + "v" * len(more),
            [meta, n2, w_in, n2_other, cot, w_out, cot_other, base, expand_line, *more], name,
            [pltpu.VMEM((2, rows_n, hidden_own), BF16)] * 2,
            "vvvvhhhv" if first else "hvhhhhv", 48,
        )

    out1, dn1, out1_o, dn1_o, ge_top, ge_low, gr_cross, gb_cross = mlp(
        True, middle, (cross_first, 0, width), cross_reduce, [], "mlp_far"
    )
    top_in = cross_swap(ge_top)
    low_in = cross_swap(after(ge_low, top_in))
    out2, dn2, out2_o, dn2_o, ge_own, gr_own, gb_own = mlp(
        False, out1, expand_weight, reduce_weight, [dn1, out1_o, dn1_o], "mlp_near"
    )
    dn2_in = core_swap(dn2_o)

    g_middle, r_att, raug, g_states, small_two = call(
        functools.partial(middle_kernel, heads, slots, nctx),
        [full, low, shaped((heads * AUG, rows_n), BF16), state_shape, shaped((8, width))],
        "svahavhhhh",
        [meta, dn2, dn2_in, middle, cot, params, mixed, den, fq, wo], "middle",
        [total, pltpu.VMEM((width, rows_n), BF16)], "hhhhv",
    )
    g_arrived = exchange(g_states)
    gr_in = cross_swap(after(gr_cross, low_in))
    out2_in = core_swap(after(out2_o, g_states))
    rq, g_query_map, *go = call(
        functools.partial(query_back_kernel, heads, slots, nctx),
        [table, square] + [shaped((shard, width), BF16)] * 4,
        "sahhavhh", [meta, carried, raug, fq, (qkv, 0, width), query_map, mixed, r_att], "query_back",
        [total], "hhhhhh",
    )
    (g_running,) = call(
        functools.partial(scan_kernel, nctx, True), [state_shape], "sv",
        [keep_next, after(g_arrived, rq, low_in)], "scan_back", (), "h",
    )
    g_carried = exchange(g_running)
    top_in, low_in = lax.optimization_barrier((top_in, low_in, g_running))[:2]
    sum_e = Reduction([ge_own, (top_in, low_in)], nctx, place)
    e_got = sum_e.scatter(0)
    sum_r = Reduction([gr_own, after(gr_in, g_running)], nctx, place)
    r_got = sum_r.scatter(0)
    go_far, go_core = core_swap(after(go[3], g_running)), core_swap(after(go[1], g_running))
    rp, g_key_map, gp1, gp3 = call(
        functools.partial(key_back_kernel, heads, slots, nctx),
        [shaped((3 * width, rows_n), BF16), square] + [shaped((span, width), BF16)] * 2,
        "svhavhh", [meta, after(g_carried, sum_e.sent, sum_r.sent), fk, (qkv, width, 2 * width), key_map, rq, n1],
        "key_back", [total], "hhhh",
    )
    gp3_in, gp1_in = core_swap(after(gp3, e_got)), core_swap(after(gp1, e_got))
    p_own, p_cross = call(
        project_grad_kernel, [shaped((width, width), BF16)] * 2, "shhaahaha",
        [meta, rp, n1, gp1_in, gp3_in, go[0], go_core, go[2], go_far], "project_grad", (), "hh",
    )
    p_in = cross_swap(p_cross)
    sum_e.hold(p_own)
    sum_e.scatter(1)
    small = shaped((64, width), BF16)
    dx, layer_out, own_s, core_s, cross_s, far_s = call(
        functools.partial(input_kernel, heads), [full, full, small, small, small, small],
        "shhvhhaaaahhaaaa",
        [meta, rp, after(x, p_own, sum_e.sent), params, g_middle, out2, out2_in, small_two,
         gb_own, gb_cross, g_query_map, g_key_map, *projects],
        "input", [pltpu.VMEM((4, 64, width), F32)], "hhvvvv",
    )
    far_in, core_in = core_swap(far_s), core_swap(core_s)
    cross_in = cross_swap(add(cross_s, far_in))
    small_own = add(own_s, core_in)
    sum_e.hold(far_in, core_in)
    e_got = sum_e.scatter(2)
    sum_r.hold(far_in, core_in)
    r_got = sum_r.scatter(1)
    sum_p = Reduction([p_own, p_in], nctx, place)
    p_got = sum_p.scatter(0)
    sum_e.hold(sum_p.sent)
    sum_r.hold(sum_p.sent)
    sum_e.deep(3)
    e_got = sum_e.spread(2)
    r_got = sum_r.scatter(2)
    sum_p.hold(e_got, r_got)
    sum_p.scatter(1)
    sum_e.join(sum_p.sent)
    e_got = sum_e.spread(1)
    sum_r.hold(sum_p.sent)
    sum_r.deep(3)
    r_got = sum_r.spread(2)
    sum_p.hold(e_got, r_got)
    sum_p.scatter(2)
    sum_e.join(sum_p.sent)
    e_got = sum_e.spread(0)
    sum_r.join(sum_p.sent)
    r_got = sum_r.spread(1)
    sum_p.hold(r_got)
    sum_p.deep(3)
    sum_r.join(sum_p.cur)
    r_got = sum_r.spread(0)
    sum_p.spread(2)
    sum_p.join(e_got)
    sum_p.spread(1)
    sum_p.join(r_got)
    sum_p.spread(0)
    sum_p.join()
    sum_e.join()
    sum_r.join()
    g_expand, g_reduce, g_project = sum_e.cur, sum_r.cur, sum_p.cur
    rest = small_own.astype(F32) + cross_in.astype(F32)
    for level in range(len(sum_p.groups)):
        low_rest = rest.astype(BF16)
        rest = low_rest.astype(F32) + sum_p.send(low_rest, sum_p.groups[level], 1).astype(F32)
    g_output = g_project[span : span + shard]
    line = shaped((1, shard))
    g1, s1, g2, s2, bo, br, pb, eb, mq, mk = call(
        unpack_kernel,
        [line] * 6 + [shaped((1, span)), shaped((1, hidden_own))]
        + [shaped((own_heads, 64, 64))] * 2, "v", [rest], "unpack",
    )
    return (
        layer_out[None], dx[None], line1(g1), line1(s1), g_project[:span].T.astype(F32), line1(pb), mq, mk,
        g_output.astype(F32), line1(bo), line1(g2), line1(s2), g_expand.astype(F32), line1(eb),
        g_reduce.astype(F32), line1(br),
    )


def solution(mesh):
    row = P("fsdp", "ctx", None)
    vec = P("fsdp")
    maps = P("fsdp", None, None)
    in_specs = (
        row, row, row, P("fsdp", None), vec, vec, P(None, "fsdp"), vec, maps, maps,
        P("fsdp", None), vec, vec, vec, P(None, "fsdp"), vec, P("fsdp", None), vec,
    )
    out_specs = (
        row, row, vec, vec, P(None, "fsdp"), vec, maps, maps, P("fsdp", None), vec, vec, vec,
        P(None, "fsdp"), vec, P("fsdp", None), vec,
    )
    return jax.shard_map(body, mesh=mesh, in_specs=in_specs, out_specs=out_specs, check_vma=False)
```

```python
import functools

import jax
import jax.numpy as jnp
from jax import lax
from jax.experimental import pallas as pl
from jax.experimental.pallas import tpu as pltpu
from jax.sharding import PartitionSpec as P

EPS = 1e-05
F32 = jnp.float32
BF16 = jnp.bfloat16
AUG = 80
KEEP = 72
UNROLL = 3
NN = (((1,), (0,)), ((), ()))
NT = (((1,), (1,)), ((), ()))
TN = (((0,), (0,)), ((), ()))
CORE = [(i, i ^ 1) for i in range(4)]
CROSS = [(i, i ^ 2) for i in range(4)]
VMEM = pl.BlockSpec(memory_space=pltpu.VMEM)
SMEM = pl.BlockSpec(memory_space=pltpu.SMEM)
FAR = pl.BlockSpec(memory_space=pltpu.HBM)
ANYWHERE = pl.BlockSpec(memory_space=pl.ANY)
SPECS = {"v": VMEM, "s": SMEM, "h": FAR, "a": ANYWHERE}


def mm(a, b, dims):
    return lax.dot_general(a, b, dims, preferred_element_type=F32)


class Staged:
    def __init__(self, far, near, sems, out):
        self.near, self.state = near, "out" if out else "in"
        self.copies, at = [], 0
        for part, sem in zip(far, sems):
            here = near if len(far) == 1 else near.at[pl.ds(at, part.shape[0])]
            pair = (here, part) if out else (part, here)
            self.copies.append(pltpu.make_async_copy(*pair, sem))
            at += part.shape[0]
        self.shape, self.dtype = near.shape, near.dtype
        if not out:
            self.start()

    def start(self):
        for copy in self.copies:
            copy.start()

    def wait(self):
        for copy in self.copies:
            copy.wait()

    def ready(self):
        if self.state == "in":
            self.wait()
            self.state = "ready"

    def flush(self):
        if self.state == "out":
            self.start()
            self.state = "flushed"

    def finish(self):
        self.ready()
        self.flush()
        if self.state == "flushed":
            self.wait()
            self.state = "done"

    def __getitem__(self, index):
        assert self.state in ("ready", "out", "flushed")
        return self.near[index]

    def __setitem__(self, index, value):
        assert self.state == "out"
        self.near[index] = value


def ready(*refs):
    for ref in refs:
        if isinstance(ref, Staged):
            ref.ready()


def flush(*refs):
    for ref in refs:
        if isinstance(ref, Staged):
            ref.flush()


def call(kernel, outs, kinds, args, name, scratch=(), out_kinds=None, limit=32, flops=1):
    out_kinds = out_kinds or "v" * len(outs)
    both = kinds + out_kinds
    groups = [a if isinstance(a, list) else [a] for a in [*args, *outs]]
    groups = [
        [p if isinstance(p, tuple) else (p, 0, p.shape[0]) for p in group] for group in groups
    ]
    operands = [(p[0], k) for group, k in zip(groups[: len(kinds)], kinds) for p in group]
    pieces = sum(len(group) for group, k in zip(groups, both) if k in "ha")
    staged = [
        pltpu.VMEM((sum(p[2] for p in group), *group[0][0].shape[1:]), group[0][0].dtype)
        for group, k in zip(groups, both) if k in "ha"
    ]

    def run(*refs):
        count = sum(len(group) for group in groups)
        extra = len(staged)
        near = refs[count : count + extra]
        sems = refs[count + extra] if extra else None
        rest = refs[count + extra + (1 if extra else 0) :]
        use, at, ref_at, sem_at = [], 0, 0, 0
        for i, (kind, group) in enumerate(zip(both, groups)):
            mine = refs[ref_at : ref_at + len(group)]
            ref_at += len(group)
            if kind in "ha":
                far = [
                    ref if ref.shape[0] == size else ref.at[pl.ds(start, size)]
                    for ref, (_, start, size) in zip(mine, group)
                ]
                own = [sems.at[sem_at + j] for j in range(len(group))]
                sem_at += len(group)
                use.append(Staged(far, near[at], own, i >= len(kinds)))
                at += 1
            else:
                use.append(mine[0])
        kernel(*use, *rest)
        for ref in use:
            if isinstance(ref, Staged):
                ref.finish()

    sems = [pltpu.SemaphoreType.DMA((pieces,))] if staged else []
    return pl.pallas_call(
        run,
        out_shape=[
            pltpu.HBM(o.shape, o.dtype) if k == "h" else o for o, k in zip(outs, out_kinds)
        ],
        in_specs=[SPECS[k] for _, k in operands],
        out_specs=[SPECS[k] for k in out_kinds],
        scratch_shapes=[*staged, *sems, *scratch],
        compiler_params=pltpu.CompilerParams(vmem_limit_bytes=limit << 20),
        cost_estimate=pl.CostEstimate(flops=flops, bytes_accessed=1, transcendentals=0),
        name=name,
    )(*[
        pltpu.with_memory_space_constraint(a, pltpu.HBM) if k == "h" else a
        for a, k in operands
    ])


def shaped(shape, dtype=F32):
    return jax.ShapeDtypeStruct(shape, dtype)


def norm_parts(v):
    center = v - jnp.mean(v, axis=-1, keepdims=True)
    scale = lax.rsqrt(jnp.mean(center * center, axis=-1, keepdims=True) + EPS)
    return center * scale, scale


def norm_back(gy, normal, scale, gain):
    a = gy * gain
    return (
        a - jnp.mean(a, axis=-1, keepdims=True)
        - normal * jnp.mean(a * normal, axis=-1, keepdims=True)
    ) * scale


def aug_rows(top, row):
    index = lax.broadcasted_iota(jnp.int32, (AUG - top.shape[0], top.shape[1]), 0)
    tail = jnp.where(index == 0, row, 0.0).astype(BF16)
    return jnp.concatenate([top, tail], axis=0)


def spread_states(total_ref, out_ref, parts, rows_per):
    for part in range(parts):
        out_ref[part] = total_ref[:, part * rows_per : (part + 1) * rows_per, :].astype(BF16)


def collect_states(in_ref, total_ref, parts, rows_per):
    for part in range(parts):
        total_ref[:, part * rows_per : (part + 1) * rows_per, :] = in_ref[part].astype(F32)


def project_rows(meta, j, w, n, pb_ref):
    line = jnp.broadcast_to(pb_ref[pl.ds(meta[j], 1), :], (128, w.shape[0])).T
    bias = jnp.concatenate([line] * (n.shape[0] // 128), axis=1)
    return (mm(w[...], n, NT) + bias).astype(BF16)


def near_kernel(meta, x_ref, p_ref, w0, w1, pb_ref, n_ref, half_ref):
    ready(x_ref)
    normal, _ = norm_parts(x_ref[...].astype(F32))
    n = (normal * p_ref[0:1] + p_ref[1:2]).astype(BF16)
    n_ref[...] = n
    flush(n_ref)
    span = w0.shape[0]
    for j, w in enumerate((w0, w1)):
        ready(w)
        start = pl.multiple_of((meta[j] & 1) * span, 64)
        half_ref[pl.ds(start, span), :] = project_rows(meta, j, w, n, pb_ref)


def far_kernel(meta, n_ref, near_ref, w2, w3, pb_ref, qkv_ref):
    span = w2.shape[0]
    ready(n_ref)
    start = pl.multiple_of((meta[0] >> 1) * 2 * span, 64)
    qkv_ref[pl.ds(start, 2 * span), :] = near_ref[...]
    for j, w in ((2, w2), (3, w3)):
        ready(w)
        start = pl.multiple_of(meta[j] * span, 64)
        qkv_ref[pl.ds(start, span), :] = project_rows(meta, j, w, n_ref[...], pb_ref)


def phi(rows_ref, base, map_ref, h):
    rows = rows_ref[pl.ds(pl.multiple_of(base + h * 64, 64), 64), :]
    logits = mm(map_ref[h], rows, TN)
    up = jnp.exp(logits - jnp.max(logits, axis=0, keepdims=True))
    down = jnp.exp(jnp.min(logits, axis=0, keepdims=True) - logits)
    p1 = up * (1.0 / jnp.sum(up, axis=0, keepdims=True))
    p2 = down * (1.0 / jnp.sum(down, axis=0, keepdims=True))
    return p1.astype(BF16), p2.astype(BF16)


def key_kernel(heads, slots, parts, meta, qkv_ref, map_ref, fk_ref, s_ref, total):
    width = heads * 64
    cols = qkv_ref.shape[1] // slots
    rows_per = s_ref.shape[2]
    total[...] = jnp.zeros_like(total)

    def head(h, carry):
        p1, p2 = phi(qkv_ref, width, map_ref, h)
        at = pl.multiple_of(h * 128, 128)
        fk_ref[pl.ds(at, 64), :] = p1
        fk_ref[pl.ds(pl.multiple_of(at + 64, 64), 64), :] = p2
        v = qkv_ref[pl.ds(pl.multiple_of(2 * width + h * 64, 64), 64), :]
        va = aug_rows(v, 1.0)
        fk = jnp.concatenate([p1, p2], axis=0)
        for s in range(slots):
            part = slice(s * cols, (s + 1) * cols)
            state = mm(va[:, part], fk[:, part], NT)
            total[s ^ meta[4], pl.ds(pl.multiple_of(h * KEEP, 8), KEEP), :] = state[:KEEP]
        return carry

    lax.fori_loop(0, heads, head, 0, unroll=UNROLL)
    flush(fk_ref)
    spread_states(total, s_ref, parts, rows_per)


def query_kernel(heads, qkv_ref, map_ref, fq_ref):
    def head(h, carry):
        p1, p2 = phi(qkv_ref, 0, map_ref, h)
        at = pl.multiple_of(h * 128, 128)
        fq_ref[pl.ds(at, 64), :] = p1
        fq_ref[pl.ds(pl.multiple_of(at + 64, 64), 64), :] = p2
        return carry

    lax.fori_loop(0, heads, head, 0, unroll=UNROLL)


def scan_kernel(nctx, backward, keep, in_ref, out_ref):
    blocks = 2 * nctx
    order = [(b, 0) if b < nctx else (blocks - 1 - b, 1) for b in range(blocks)]
    acc = jnp.zeros(in_ref.shape[2:], F32)
    for b in reversed(range(blocks)) if backward else range(blocks):
        c, lane = order[b]
        acc = acc * keep[b] + in_ref[c, lane].astype(F32)
        out_ref[c, lane] = acc.astype(BF16)


def fill_output(meta, wo_refs, wo):
    rows = wo_refs[0].shape[0]
    for j, ref in enumerate(wo_refs):
        wo[pl.ds(pl.multiple_of(meta[j] * rows, 64), rows), :] = ref[...]


def attend_kernel(
    heads, slots, parts, meta, c_ref, fq_ref, x_ref, w0, w1, w2, w3, p_ref,
    mixed_ref, den_ref, middle_ref, n2_ref, wo, total,
):
    cols = fq_ref.shape[1] // slots
    collect_states(c_ref, total, parts, c_ref.shape[2])
    ready(fq_ref)

    def head(h, carry):
        fq = fq_ref[pl.ds(pl.multiple_of(h * 128, 128), 128), :]
        for s in range(slots):
            part = slice(s * cols, (s + 1) * cols)
            c = total[s ^ meta[4], pl.ds(pl.multiple_of(h * KEEP, 8), AUG), :].astype(BF16)
            both = mm(c, fq[:, part], NN)
            den = both[64:65]
            mixed = both[:64] * (1.0 / den)
            mixed_ref[pl.ds(pl.multiple_of(h * 64, 64), 64), part] = mixed.astype(BF16)
            den_ref[pl.ds(pl.multiple_of(h * 8, 8), 8), part] = jnp.broadcast_to(den, (8, cols))
        return carry

    lax.fori_loop(0, heads, head, 0, unroll=UNROLL)
    flush(mixed_ref, den_ref)
    ready(x_ref, w0, w1, w2, w3)
    fill_output(meta, (w0, w1, w2, w3), wo)
    flush(wo)
    middle = x_ref[...].astype(F32) + mm(mixed_ref[...], wo[...], TN) + p_ref[4:5]
    middle_ref[...] = middle
    flush(middle_ref)
    normal, _ = norm_parts(middle)
    n2 = (normal * p_ref[2:3] + p_ref[3:4]).astype(BF16)
    n2_ref[...] = n2


def mlp_kernel(first, meta, n2_ref, we, n2o_ref, cot_ref, wr, coto_ref, base_ref, eb_ref, *refs):
    if first:
        out_ref, dn_ref, outo_ref, dno_ref, ge, ge_low, gr, gb_ref, act, hid = refs
    else:
        back_ref, baseo_ref, backo_ref, out_ref, dn_ref, outo_ref, dno_ref, ge, gr, gb_ref, act, hid = refs
    rows_n, width = n2_ref.shape
    line = meta[2] if first else meta[0]
    tile = we.shape[1] // 2
    ready(n2_ref, we, n2o_ref, cot_ref, wr, coto_ref)

    def step(t, carry):
        at = pl.ds(pl.multiple_of(t * tile, tile), tile)
        bias = eb_ref[pl.ds(line, 1), at]
        pre = [
            (mm(n[...], we[:, at], NN) + bias, mm(c[...], wr[at, :], NT))
            for n, c in ((n2_ref, cot_ref), (n2o_ref, coto_ref))
        ]
        actives, hiddens, sums = [], [], None
        for k, (hidden, back) in enumerate(pre):
            square = hidden * hidden
            part = 0.5 + 0.5 * jnp.tanh(
                hidden * (0.7978845608028654 + 0.035677408136300125 * square)
            )
            active = hidden * part
            slope = part + active * (1.0 - part) * (
                1.5957691216057308 + 0.21406444881780075 * square
            )
            r_hidden = back.astype(BF16).astype(F32) * slope
            actives.append(active.astype(BF16))
            hiddens.append(r_hidden.astype(BF16))
            act[k, :, at] = actives[k]
            hid[k, :, at] = hiddens[k]
            total = jnp.sum(r_hidden, axis=0, keepdims=True)
            sums = total if sums is None else sums + total
        gb_ref[:, at] = jnp.broadcast_to(sums, (8, tile))
        grad = (mm(n2_ref[...], hiddens[0], TN) + mm(n2o_ref[...], hiddens[1], TN)).astype(BF16)
        if first:
            ge[:, at] = grad[: width // 2]
            ge_low[:, at] = grad[width // 2 :]
        else:
            ge[:, at] = grad
        gr[at, :] = (
            mm(actives[0], cot_ref[...], TN) + mm(actives[1], coto_ref[...], TN)
        ).astype(BF16)
        return carry

    lax.fori_loop(0, 2, step, 0)
    flush(ge, gr)
    if first:
        flush(ge_low)
    ready(base_ref)
    out_ref[...] = base_ref[...] + mm(act[0], wr[...], NN)
    flush(out_ref)
    dn = mm(hid[0], we[...], NT)
    if first:
        dn_ref[...] = dn
        outo_ref[...] = mm(act[1], wr[...], NN).astype(BF16)
        dno_ref[...] = mm(hid[1], we[...], NT).astype(BF16)
    else:
        dn_ref[...] = back_ref[...] + dn
        flush(dn_ref)
        outo_ref[...] = (baseo_ref[...].astype(F32) + mm(act[1], wr[...], NN)).astype(BF16)
        flush(outo_ref)
        dno_ref[...] = (backo_ref[...].astype(F32) + mm(hid[1], we[...], NT)).astype(BF16)


def middle_kernel(
    heads, slots, parts, meta, dn_ref, dnin_ref, middle_ref, cot_ref, p_ref, mixed_ref, den_ref, fq_ref,
    wo, gm_ref, ratt_ref, raug_ref, g_ref, small_ref, total, rmix,
):
    cols = fq_ref.shape[1] // slots
    ready(middle_ref, dn_ref, dnin_ref, cot_ref)
    normal, scale = norm_parts(middle_ref[...])
    gy = dn_ref[...] + dnin_ref[...].astype(F32)
    cot = cot_ref[...].astype(F32)
    g_middle = cot + norm_back(gy, normal, scale, p_ref[2:3])
    gm_ref[...] = g_middle
    r_att = g_middle.astype(BF16)
    ratt_ref[...] = r_att
    flush(gm_ref, ratt_ref)
    small_ref[...] = jnp.concatenate(
        [
            jnp.sum(gy * normal, axis=0, keepdims=True),
            jnp.sum(gy, axis=0, keepdims=True),
            jnp.sum(r_att.astype(F32), axis=0, keepdims=True),
            jnp.sum(cot, axis=0, keepdims=True),
            jnp.zeros((4, gy.shape[1]), F32),
        ],
        axis=0,
    )
    ready(wo)
    rmix[...] = mm(wo[...], r_att, NT).astype(BF16)
    total[...] = jnp.zeros_like(total)
    ready(mixed_ref, den_ref, fq_ref)

    def head(h, carry):
        rows = pl.ds(pl.multiple_of(h * 64, 64), 64)
        rm = rmix[rows, :].astype(F32)
        inverse = 1.0 / den_ref[pl.ds(pl.multiple_of(h * 8, 8), 8), :][0:1]
        rn = (rm * inverse).astype(BF16)
        rd = -jnp.sum(rm * mixed_ref[rows, :].astype(F32), axis=0, keepdims=True) * inverse
        ra = aug_rows(rn, rd)
        raug_ref[pl.ds(pl.multiple_of(h * AUG, 16), AUG), :] = ra
        fq = fq_ref[pl.ds(pl.multiple_of(h * 128, 128), 128), :]
        for s in range(slots):
            part = slice(s * cols, (s + 1) * cols)
            state = mm(ra[:, part], fq[:, part], NT)
            total[s ^ meta[4], pl.ds(pl.multiple_of(h * KEEP, 8), KEEP), :] = state[:KEEP]
        return carry

    lax.fori_loop(0, heads, head, 0, unroll=UNROLL)
    spread_states(total, g_ref, parts, g_ref.shape[2])
    flush(g_ref, raug_ref)


def logits_back(p_both, g_both):
    p1, p2 = p_both[:64].astype(F32), p_both[64:].astype(F32)
    g1, g2 = g_both[:64], g_both[64:]
    s1 = jnp.sum(p1 * g1, axis=0, keepdims=True)
    s2 = jnp.sum(p2 * g2, axis=0, keepdims=True)
    return (p1 * (g1 - s1) - p2 * (g2 - s2)).astype(BF16)


def query_back_kernel(
    heads, slots, parts, meta, c_ref, raug_ref, fq_ref, qkv_ref, map_ref, mixed_ref, ratt_ref,
    rq_ref, gmap_ref, g0, g1, g2, g3, total,
):
    cols = fq_ref.shape[1] // slots
    ready(c_ref)
    collect_states(c_ref, total, parts, c_ref.shape[2])
    ready(raug_ref, fq_ref, qkv_ref)

    def head(h, carry):
        ra = raug_ref[pl.ds(pl.multiple_of(h * AUG, 16), AUG), :]
        fq = fq_ref[pl.ds(pl.multiple_of(h * 128, 128), 128), :]
        pieces = []
        for s in range(slots):
            part = slice(s * cols, (s + 1) * cols)
            c = total[s ^ meta[4], pl.ds(pl.multiple_of(h * KEEP, 8), AUG), :].astype(BF16)
            pieces.append(mm(c, ra[:, part], TN))
        r_fq = jnp.concatenate(pieces, axis=1).astype(BF16).astype(F32)
        r_l = logits_back(fq, r_fq)
        rows = pl.ds(pl.multiple_of(h * 64, 64), 64)
        rq_ref[rows, :] = mm(map_ref[h], r_l, NN).astype(BF16)
        gmap_ref[h] = mm(qkv_ref[rows, :], r_l, NT)
        return carry

    lax.fori_loop(0, heads, head, 0, unroll=UNROLL)
    flush(rq_ref, gmap_ref)
    ready(mixed_ref, ratt_ref)
    rows = g0.shape[0]
    for j, g in enumerate((g0, g1, g2, g3)):
        mixed = mixed_ref[pl.ds(pl.multiple_of(meta[j] * rows, 64), rows), :]
        g[...] = mm(mixed, ratt_ref[...], NN).astype(BF16)
        flush(g)


def key_back_kernel(
    heads, slots, parts, meta, d_ref, fk_ref, qkv_ref, map_ref, rq_ref, n_ref,
    rp_ref, gmap_ref, g1, g3, total,
):
    width = heads * 64
    cols = fk_ref.shape[1] // slots
    collect_states(d_ref, total, parts, d_ref.shape[2])
    ready(fk_ref, qkv_ref, rq_ref)
    rp_ref[0:width, :] = rq_ref[...]

    def head(h, carry):
        fk = fk_ref[pl.ds(pl.multiple_of(h * 128, 128), 128), :]
        v = qkv_ref[pl.ds(pl.multiple_of(width + h * 64, 64), 64), :]
        va = aug_rows(v, 1.0)
        pieces = []
        for s in range(slots):
            part = slice(s * cols, (s + 1) * cols)
            d = total[s ^ meta[4], pl.ds(pl.multiple_of(h * KEEP, 8), AUG), :].astype(BF16)
            pieces.append(mm(d, va[:, part], TN))
            rv = mm(d[:64], fk[:, part], NN).astype(BF16)
            rp_ref[pl.ds(pl.multiple_of(2 * width + h * 64, 64), 64), part] = rv
        r_fk = jnp.concatenate(pieces, axis=1).astype(BF16).astype(F32)
        r_l = logits_back(fk, r_fk)
        rows = pl.ds(pl.multiple_of(width + h * 64, 64), 64)
        rp_ref[rows, :] = mm(map_ref[h], r_l, NN).astype(BF16)
        keys = qkv_ref[pl.ds(pl.multiple_of(h * 64, 64), 64), :]
        gmap_ref[h] = mm(keys, r_l, NT)
        return carry

    lax.fori_loop(0, heads, head, 0, unroll=UNROLL)
    flush(rp_ref, gmap_ref)
    ready(n_ref)
    span = g1.shape[0]
    for j, g in ((1, g1), (3, g3)):
        rp = rp_ref[pl.ds(pl.multiple_of(meta[j] * span, 64), span), :]
        g[...] = mm(rp, n_ref[...], NN).astype(BF16)
        flush(g)


def project_grad_kernel(meta, rp_ref, n_ref, in0, in2, go0, go0_in, go2, go2_in, own, cross):
    span = in0.shape[0]
    ready(rp_ref, n_ref, in0, in2, go0, go0_in, go2, go2_in)
    for j, more, go, go_in, out in ((2, in2, go2, go2_in, cross), (0, in0, go0, go0_in, own)):
        rp = rp_ref[pl.ds(pl.multiple_of(meta[j] * span, 64), span), :]
        out[:span, :] = (mm(rp, n_ref[...], NN) + more[...].astype(F32)).astype(BF16)
        out[span:, :] = (go[...].astype(F32) + go_in[...].astype(F32)).astype(BF16)
        flush(out)


def input_kernel(
    heads, meta, rp_ref, x_ref, p_ref, gm_ref, out_ref, outin_ref, two_ref, ebo_ref, ebc_ref,
    mq_ref, mk_ref, w0, w1, w2, w3, dx_ref, full_ref, b0, b1, b2, b3, pack,
):
    ready(out_ref, outin_ref)
    full_ref[...] = out_ref[...] + outin_ref[...].astype(F32) + p_ref[5:6]
    flush(full_ref)
    span, width = w0.shape
    shard = width // 4
    own_heads = heads // 4
    ones = jnp.ones((8, x_ref.shape[0]), BF16)
    pack[...] = jnp.zeros_like(pack)
    gy = None
    ready(rp_ref, w0, w1, w2, w3, x_ref, gm_ref)
    for j, w in enumerate((w0, w1, w2, w3)):
        rp = rp_ref[pl.ds(pl.multiple_of(meta[j] * span, 64), span), :]
        part = mm(rp, w[...], TN)
        gy = part if gy is None else gy + part
        pack[meta[j], 8:16, :span] = mm(ones, rp, NT)
    ready(ebo_ref, ebc_ref, two_ref)
    pack[meta[0], 16:24, :] = ebo_ref[...]
    pack[meta[2], 16:24, :] = ebc_ref[...]
    normal, scale = norm_parts(x_ref[...].astype(F32))
    dx_ref[...] = gm_ref[...] + norm_back(gy, normal, scale, p_ref[0:1])
    flush(dx_ref)
    ready(mq_ref, mk_ref)
    lines = [
        jnp.sum(gy * normal, axis=0, keepdims=True),
        jnp.sum(gy, axis=0, keepdims=True),
        two_ref[0:1], two_ref[1:2], two_ref[2:3], two_ref[3:4],
    ]
    for i in range(4):
        cut = slice(i * shard, (i + 1) * shard)
        for k, line in enumerate(lines):
            pack[i, k : k + 1, :shard] = line[:, cut]
        for base, ref in ((24, mq_ref), (40, mk_ref)):
            for k in range(4):
                for h in range(own_heads):
                    at = k * shard + h * 64
                    pack[i, base : base + 16, at : at + 64] = ref[
                        i * own_heads + h, 16 * k : 16 * k + 16, :
                    ]
    for j, b in enumerate((b0, b1, b2, b3)):
        b[...] = pack[meta[j]].astype(BF16)


def unpack_kernel(rest_ref, g1, s1, g2, s2, bo, br, pb, eb, mq, mk):
    shard = g1.shape[1]
    own_heads = mq.shape[0]
    for k, ref in enumerate((g1, s1, g2, s2, bo, br)):
        ref[...] = rest_ref[k : k + 1, :shard]
    pb[...] = rest_ref[8:9, : pb.shape[1]]
    eb[...] = rest_ref[16:17, :]
    for base, ref in ((24, mq), (40, mk)):
        for k in range(4):
            for h in range(own_heads):
                at = k * shard + h * 64
                ref[h, 16 * k : 16 * k + 16, :] = rest_ref[base : base + 16, at : at + 64]


def line1(a):
    return a.reshape(-1)


def core_swap(a):
    return lax.ppermute(a, "fsdp", CORE)


def cross_swap(a):
    return lax.ppermute(a, "fsdp", CROSS)


def after(value, *others):
    return lax.optimization_barrier((value, *others))[0]


def spread(shard, cross):
    return [shard, core_swap(shard), cross, core_swap(cross)]


def add(a, b):
    return (a.astype(F32) + b.astype(F32)).astype(BF16)


def rows_sum(parts, start, size):
    out = None
    for offset, part in parts:
        if isinstance(part, tuple):
            part, offset = jnp.where(start + offset < part[0].shape[0], *part), -start
        piece = lax.dynamic_slice_in_dim(part, start + offset, size, 0).astype(F32)
        out = piece if out is None else out + piece
    return out.astype(BF16)


class Reduction:
    def __init__(self, parts, nctx, place):
        self.parts = [(0, part) for part in parts]
        self.rows, self.nctx, self.place = parts[0].shape[0], nctx, place
        self.groups = [[bit] for bit in range(nctx.bit_length() - 1)]

    def member(self, group):
        return sum(((self.place >> bit) & 1) << k for k, bit in enumerate(group))

    def send(self, value, group, other):
        flip = sum(((other >> k) & 1) << bit for k, bit in enumerate(group))
        return lax.ppermute(value, "ctx", [(i, i ^ flip) for i in range(self.nctx)])

    def scatter(self, level):
        group = self.groups[level]
        count = 1 << len(group)
        mine = self.member(group)
        self.rows //= count
        self.sent = [
            rows_sum(self.parts, (mine ^ d) * self.rows, self.rows) for d in range(1, count)
        ]
        got = [self.send(sent, group, d) for d, sent in enumerate(self.sent, 1)]
        self.parts = [
            (0, jnp.where(mine == 0, *part)) if isinstance(part, tuple)
            else (offset + mine * self.rows, part)
            for offset, part in self.parts
        ]
        self.fresh = len(got)
        self.parts += [(0, g) for g in got]
        return got

    def hold(self, *others):
        last = self.parts[-self.fresh :]
        held = lax.optimization_barrier((tuple(part for _, part in last), others))[0]
        self.parts[-self.fresh :] = [(at, part) for (at, _), part in zip(last, held)]

    def own(self):
        self.cur = rows_sum(self.parts, 0, self.rows)

    def spread(self, level):
        group = self.groups[level]
        self.others = [self.send(self.cur, group, d) for d in range(1, 1 << len(group))]
        self.level = level
        return self.others

    def join(self, *others):
        group = self.groups[self.level]
        parts = [self.cur, *self.others]
        if others:
            parts = list(lax.optimization_barrier((tuple(parts), others))[0])
        for k, bit in enumerate(group):
            swap = ((self.place >> bit) & 1) == 1
            parts = [
                jnp.where(swap, parts[j ^ (1 << k)], parts[j]) for j in range(len(parts))
            ]
        self.cur = jnp.concatenate(parts, axis=0)

    def deep(self, first):
        for level in range(first, len(self.groups)):
            self.scatter(level)
        self.own()
        for level in reversed(range(first, len(self.groups))):
            self.spread(level)
            self.join()


def straighten(parts, mine):
    a, b, c, d = parts
    odd = (mine & 1) == 1
    upper = (mine & 2) == 2
    a, b = jnp.where(odd, b, a), jnp.where(odd, a, b)
    c, d = jnp.where(odd, d, c), jnp.where(odd, c, d)
    return [
        jnp.where(upper, c, a), jnp.where(upper, d, b),
        jnp.where(upper, a, c), jnp.where(upper, b, d),
    ]


def exchange(a):
    return lax.all_to_all(a, "ctx", 0, 0, tiled=True)


def body(
    tokens, cotangent, pair_table, seq_ids, first_gain, first_shift, project_weight, project_bias,
    feature_query, feature_key, output_weight, output_bias, second_gain, second_shift,
    expand_weight, expand_bias, reduce_weight, reduce_bias,
):
    x = tokens[0]
    cot = cotangent[0]
    rows_n, width = x.shape
    heads = width // feature_query.shape[1]
    own_heads = feature_query.shape[0]
    slots = pair_table.shape[2]
    nctx = lax.axis_size("ctx")
    place = lax.axis_index("ctx")
    mine = lax.axis_index("fsdp")
    span = project_weight.shape[1]
    hidden_own = expand_weight.shape[1]
    shard = width // 4
    wide = heads * 128

    project_t = project_weight.T
    cross_project = cross_swap(project_t)
    vector = jnp.concatenate(
        [first_gain, first_shift, second_gain, second_shift, output_bias, reduce_bias,
         project_bias, expand_bias]
    )
    room = -vector.shape[0] % 1024
    vector = jnp.concatenate([vector, jnp.zeros((room,), BF16)]).reshape(-1, 64)
    map_rows = own_heads * 64
    pack = jnp.concatenate(
        [feature_query.reshape(-1, 64), feature_key.reshape(-1, 64), vector]
    )
    packs = spread(pack, cross_swap(pack))
    ordered = straighten(packs, mine)
    query_map = jnp.concatenate([p[:map_rows] for p in ordered]).reshape(heads, 64, 64)
    key_map = jnp.concatenate([p[map_rows : 2 * map_rows] for p in ordered]).reshape(heads, 64, 64)
    vectors = jnp.stack([p[2 * map_rows :] for p in ordered]).reshape(4, -1).astype(F32)
    params = vectors[:, : 6 * shard].reshape(4, 6, shard).transpose(1, 0, 2).reshape(6, width)
    project_line = vectors[:, 6 * shard : 6 * shard + span]
    expand_line = vectors[:, 6 * shard + span : 6 * shard + span + hidden_own]
    project_core = core_swap(project_t)
    project_far = core_swap(cross_project)
    projects = [project_t, project_core, cross_project, project_far]
    near_first = jnp.concatenate([expand_weight, output_weight])
    cross_first = cross_swap(after(near_first, cross_project))
    core_output = core_swap(output_weight)
    cross_reduce = cross_swap(after(reduce_weight, cross_first))
    cot_other = core_swap(cot)

    positions = pair_table[0, 0]
    swap = (positions[0] > positions[1]).astype(jnp.int32)
    meta = jnp.stack([mine, mine ^ 1, mine ^ 2, mine ^ 3, swap]).astype(jnp.int32)
    ids = seq_ids[0]
    same = (ids[1:] == ids[:-1]).astype(F32)
    none = jnp.zeros((1,), F32)
    keep = jnp.concatenate([none, same])
    keep_next = jnp.concatenate([same, none])

    rows_per = -(-(heads * KEEP) // (nctx * 16)) * 16
    state_shape = shaped((nctx, slots, rows_per, 128), BF16)
    total = pltpu.VMEM((slots, nctx * rows_per, 128), F32)
    wo_scratch = pltpu.VMEM((width, width), BF16)
    low = shaped((rows_n, width), BF16)
    full = shaped((rows_n, width))
    table = shaped((width, rows_n), BF16)
    square = shaped((heads, 64, 64))

    n1, near = call(
        near_kernel, [low, shaped((2 * span, rows_n), BF16)], "shvaav",
        [meta, x, params, projects[0], projects[1], project_line], "project_near", (), "hv",
    )
    (qkv,) = call(
        far_kernel, [shaped((3 * width, rows_n), BF16)], "shvaav",
        [meta, n1, near, projects[2], projects[3], project_line], "project_far",
    )
    fk, states = call(
        functools.partial(key_kernel, heads, slots, nctx),
        [shaped((wide, rows_n), BF16), state_shape], "svv",
        [meta, qkv, key_map], "keys", [total], "hh",
    )
    arrived = exchange(states)
    (fq,) = call(
        functools.partial(query_kernel, heads), [shaped((wide, rows_n), BF16)], "vv",
        [after(qkv, states), query_map], "queries", (), "h", flops=10**12,
    )
    (running,) = call(
        functools.partial(scan_kernel, nctx, False), [state_shape], "sv",
        [keep, after(arrived, cross_first)], "scan", (), "h",
    )
    carried = exchange(running)
    far_output = core_swap(after(cross_first, running)[width : width + shard])
    outputs = [output_weight, core_output, (cross_first, width, shard), far_output]
    mixed, den, middle, n2, wo = call(
        functools.partial(attend_kernel, heads, slots, nctx),
        [table, shaped((heads * 8, rows_n)), full, low, shaped((width, width), BF16)],
        "svhhhvavv", [meta, carried, fq, x, *outputs, params], "attend",
        [total], "hhhvh",
    )
    n2_other = core_swap(n2)

    def mlp(first, base, w_in, w_out, more, name):
        half = shaped((width // 2, hidden_own), BF16)
        grads = [half, half] if first else [shaped((width, hidden_own), BF16)]
        return call(
            functools.partial(mlp_kernel, first),
            [full, full, low, low, *grads, shaped((hidden_own, width), BF16),
             shaped((8, hidden_own))],
            "saaaaaa" + ("h" if first else "v") + "v" + "v" * len(more),
            [meta, n2, w_in, n2_other, cot, w_out, cot_other, base, expand_line, *more], name,
            [pltpu.VMEM((2, rows_n, hidden_own), BF16)] * 2,
            "vvvvhhhv" if first else "hhhvhhv", 48,
        )

    out1, dn1, out1_o, dn1_o, ge_top, ge_low, gr_cross, gb_cross = mlp(
        True, middle, (cross_first, 0, width), cross_reduce, [], "mlp_far"
    )
    top_in = cross_swap(ge_top)
    low_in = cross_swap(after(ge_low, top_in))
    out2, dn2, out2_o, dn2_o, ge_own, gr_own, gb_own = mlp(
        False, out1, expand_weight, reduce_weight, [dn1, out1_o, dn1_o], "mlp_near"
    )
    dn2_in = core_swap(after(dn2_o, top_in))

    g_middle, r_att, raug, g_states, small_two = call(
        functools.partial(middle_kernel, heads, slots, nctx),
        [full, low, shaped((heads * AUG, rows_n), BF16), state_shape, shaped((8, width))],
        "shahavhhhh",
        [meta, dn2, dn2_in, middle, cot, params, mixed, den, fq, wo], "middle",
        [total, pltpu.VMEM((width, rows_n), BF16)], "hhhhv",
    )
    g_arrived = exchange(g_states)
    gr_in = cross_swap(after(gr_cross, low_in))
    out2_in = core_swap(after(out2_o, g_states))
    rq, g_query_map, *go = call(
        functools.partial(query_back_kernel, heads, slots, nctx),
        [table, square] + [shaped((shard, width), BF16)] * 4,
        "sahhavhh", [meta, carried, raug, fq, (qkv, 0, width), query_map, mixed, r_att], "query_back",
        [total], "hhhhhh",
    )
    (g_running,) = call(
        functools.partial(scan_kernel, nctx, True), [state_shape], "sv",
        [keep_next, after(g_arrived, rq, low_in)], "scan_back", (), "h",
    )
    g_carried = exchange(g_running)
    top_in, low_in = lax.optimization_barrier((top_in, low_in, g_running))[:2]
    sum_e = Reduction([ge_own, (top_in, low_in)], nctx, place)
    e_got = sum_e.scatter(0)
    sum_r = Reduction([gr_own, after(gr_in, g_running)], nctx, place)
    r_got = sum_r.scatter(0)
    go_far, go_core = core_swap(after(go[3], g_running)), core_swap(after(go[1], g_running))
    rp, g_key_map, gp1, gp3 = call(
        functools.partial(key_back_kernel, heads, slots, nctx),
        [shaped((3 * width, rows_n), BF16), square] + [shaped((span, width), BF16)] * 2,
        "svhavhh", [meta, after(g_carried, sum_e.sent, sum_r.sent), fk, (qkv, width, 2 * width), key_map, rq, n1],
        "key_back", [total], "hhhh",
    )
    gp3_in, gp1_in = core_swap(after(gp3, e_got)), core_swap(after(gp1, e_got))
    p_own, p_cross = call(
        project_grad_kernel, [shaped((width, width), BF16)] * 2, "shhaahaha",
        [meta, rp, n1, gp1_in, gp3_in, go[0], go_core, go[2], go_far], "project_grad", (), "hh",
    )
    p_in = cross_swap(p_cross)
    sum_e.hold(p_own)
    sum_e.scatter(1)
    small = shaped((64, width), BF16)
    dx, layer_out, own_s, core_s, cross_s, far_s = call(
        functools.partial(input_kernel, heads), [full, full, small, small, small, small],
        "shhvhhaaaahhaaaa",
        [meta, rp, after(x, p_own, sum_e.sent), params, g_middle, out2, out2_in, small_two,
         gb_own, gb_cross, g_query_map, g_key_map, *projects],
        "input", [pltpu.VMEM((4, 64, width), F32)], "hhvvvv",
    )
    far_in, core_in = core_swap(far_s), core_swap(core_s)
    cross_in = cross_swap(add(cross_s, far_in))
    small_own = add(own_s, core_in)
    sum_e.hold(far_in, core_in)
    e_got = sum_e.scatter(2)
    sum_r.hold(far_in, core_in)
    r_got = sum_r.scatter(1)
    sum_p = Reduction([p_own, p_in], nctx, place)
    p_got = sum_p.scatter(0)
    sum_e.hold(sum_p.sent)
    sum_r.hold(sum_p.sent)
    sum_e.deep(3)
    e_got = sum_e.spread(2)
    r_got = sum_r.scatter(2)
    sum_p.hold(e_got, r_got)
    sum_p.scatter(1)
    sum_e.join(sum_p.sent)
    e_got = sum_e.spread(1)
    sum_r.hold(sum_p.sent)
    sum_r.deep(3)
    r_got = sum_r.spread(2)
    sum_p.hold(e_got, r_got)
    sum_p.scatter(2)
    sum_e.join(sum_p.sent)
    e_got = sum_e.spread(0)
    sum_r.join(sum_p.sent)
    r_got = sum_r.spread(1)
    sum_p.hold(r_got)
    sum_p.deep(3)
    sum_r.join(sum_p.cur)
    r_got = sum_r.spread(0)
    sum_p.spread(2)
    sum_p.join(e_got)
    sum_p.spread(1)
    sum_p.join(r_got)
    sum_p.spread(0)
    sum_p.join()
    sum_e.join()
    sum_r.join()
    g_expand, g_reduce, g_project = sum_e.cur, sum_r.cur, sum_p.cur
    rest = small_own.astype(F32) + cross_in.astype(F32)
    for level in range(len(sum_p.groups)):
        low_rest = rest.astype(BF16)
        rest = low_rest.astype(F32) + sum_p.send(low_rest, sum_p.groups[level], 1).astype(F32)
    g_output = g_project[span : span + shard]
    line = shaped((1, shard))
    g1, s1, g2, s2, bo, br, pb, eb, mq, mk = call(
        unpack_kernel,
        [line] * 6 + [shaped((1, span)), shaped((1, hidden_own))]
        + [shaped((own_heads, 64, 64))] * 2, "v", [rest], "unpack",
    )
    return (
        layer_out[None], dx[None], line1(g1), line1(s1), g_project[:span].T.astype(F32), line1(pb), mq, mk,
        g_output.astype(F32), line1(bo), line1(g2), line1(s2), g_expand.astype(F32), line1(eb),
        g_reduce.astype(F32), line1(br),
    )


def solution(mesh):
    row = P("fsdp", "ctx", None)
    vec = P("fsdp")
    maps = P("fsdp", None, None)
    in_specs = (
        row, row, row, P("fsdp", None), vec, vec, P(None, "fsdp"), vec, maps, maps,
        P("fsdp", None), vec, vec, vec, P(None, "fsdp"), vec, P("fsdp", None), vec,
    )
    out_specs = (
        row, row, vec, vec, P(None, "fsdp"), vec, maps, maps, P("fsdp", None), vec, vec, vec,
        P(None, "fsdp"), vec, P("fsdp", None), vec,
    )
    return jax.shard_map(body, mesh=mesh, in_specs=in_specs, out_specs=out_specs, check_vma=False)
```

```python
import functools

import jax
import jax.numpy as jnp
from jax import lax
from jax.experimental import pallas as pl
from jax.experimental.pallas import tpu as pltpu
from jax.sharding import PartitionSpec as P

EPS = 1e-05
F32 = jnp.float32
BF16 = jnp.bfloat16
AUG = 80
KEEP = 72
UNROLL = 4
NN = (((1,), (0,)), ((), ()))
NT = (((1,), (1,)), ((), ()))
TN = (((0,), (0,)), ((), ()))
CORE = [(i, i ^ 1) for i in range(4)]
CROSS = [(i, i ^ 2) for i in range(4)]
VMEM = pl.BlockSpec(memory_space=pltpu.VMEM)
SMEM = pl.BlockSpec(memory_space=pltpu.SMEM)
FAR = pl.BlockSpec(memory_space=pltpu.HBM)
ANYWHERE = pl.BlockSpec(memory_space=pl.ANY)
SPECS = {"v": VMEM, "s": SMEM, "h": FAR, "a": ANYWHERE}


def mm(a, b, dims):
    return lax.dot_general(a, b, dims, preferred_element_type=F32)


class Staged:
    def __init__(self, far, near, sems, out):
        self.near, self.state = near, "out" if out else "in"
        self.copies, at = [], 0
        for part, sem in zip(far, sems):
            here = near if len(far) == 1 else near.at[pl.ds(at, part.shape[0])]
            pair = (here, part) if out else (part, here)
            self.copies.append(pltpu.make_async_copy(*pair, sem))
            at += part.shape[0]
        self.shape, self.dtype = near.shape, near.dtype
        if not out:
            self.start()

    def start(self):
        for copy in self.copies:
            copy.start()

    def wait(self):
        for copy in self.copies:
            copy.wait()

    def ready(self):
        if self.state == "in":
            self.wait()
            self.state = "ready"

    def flush(self):
        if self.state == "out":
            self.start()
            self.state = "flushed"

    def finish(self):
        self.ready()
        self.flush()
        if self.state == "flushed":
            self.wait()
            self.state = "done"

    def __getitem__(self, index):
        assert self.state in ("ready", "out", "flushed")
        return self.near[index]

    def __setitem__(self, index, value):
        assert self.state == "out"
        self.near[index] = value


def ready(*refs):
    for ref in refs:
        if isinstance(ref, Staged):
            ref.ready()


def flush(*refs):
    for ref in refs:
        if isinstance(ref, Staged):
            ref.flush()


def call(kernel, outs, kinds, args, name, scratch=(), out_kinds=None, limit=32, flops=1):
    out_kinds = out_kinds or "v" * len(outs)
    both = kinds + out_kinds
    groups = [a if isinstance(a, list) else [a] for a in [*args, *outs]]
    groups = [
        [p if isinstance(p, tuple) else (p, 0, p.shape[0]) for p in group] for group in groups
    ]
    operands = [(p[0], k) for group, k in zip(groups[: len(kinds)], kinds) for p in group]
    pieces = sum(len(group) for group, k in zip(groups, both) if k in "ha")
    staged = [
        pltpu.VMEM((sum(p[2] for p in group), *group[0][0].shape[1:]), group[0][0].dtype)
        for group, k in zip(groups, both) if k in "ha"
    ]

    def run(*refs):
        count = sum(len(group) for group in groups)
        extra = len(staged)
        near = refs[count : count + extra]
        sems = refs[count + extra] if extra else None
        rest = refs[count + extra + (1 if extra else 0) :]
        use, at, ref_at, sem_at = [], 0, 0, 0
        for i, (kind, group) in enumerate(zip(both, groups)):
            mine = refs[ref_at : ref_at + len(group)]
            ref_at += len(group)
            if kind in "ha":
                far = [
                    ref if ref.shape[0] == size else ref.at[pl.ds(start, size)]
                    for ref, (_, start, size) in zip(mine, group)
                ]
                own = [sems.at[sem_at + j] for j in range(len(group))]
                sem_at += len(group)
                use.append(Staged(far, near[at], own, i >= len(kinds)))
                at += 1
            else:
                use.append(mine[0])
        kernel(*use, *rest)
        for ref in use:
            if isinstance(ref, Staged):
                ref.finish()

    sems = [pltpu.SemaphoreType.DMA((pieces,))] if staged else []
    return pl.pallas_call(
        run,
        out_shape=[
            pltpu.HBM(o.shape, o.dtype) if k == "h" else o for o, k in zip(outs, out_kinds)
        ],
        in_specs=[SPECS[k] for _, k in operands],
        out_specs=[SPECS[k] for k in out_kinds],
        scratch_shapes=[*staged, *sems, *scratch],
        compiler_params=pltpu.CompilerParams(vmem_limit_bytes=limit << 20),
        cost_estimate=pl.CostEstimate(flops=flops, bytes_accessed=1, transcendentals=0),
        name=name,
    )(*[
        pltpu.with_memory_space_constraint(a, pltpu.HBM) if k == "h" else a
        for a, k in operands
    ])


def shaped(shape, dtype=F32):
    return jax.ShapeDtypeStruct(shape, dtype)


def norm_parts(v):
    center = v - jnp.mean(v, axis=-1, keepdims=True)
    scale = lax.rsqrt(jnp.mean(center * center, axis=-1, keepdims=True) + EPS)
    return center * scale, scale


def norm_back(gy, normal, scale, gain):
    a = gy * gain
    return (
        a - jnp.mean(a, axis=-1, keepdims=True)
        - normal * jnp.mean(a * normal, axis=-1, keepdims=True)
    ) * scale


def aug_rows(top, row):
    index = lax.broadcasted_iota(jnp.int32, (AUG - top.shape[0], top.shape[1]), 0)
    tail = jnp.where(index == 0, row, 0.0).astype(BF16)
    return jnp.concatenate([top, tail], axis=0)


def spread_states(total_ref, out_ref, parts, rows_per):
    for part in range(parts):
        out_ref[part] = total_ref[:, part * rows_per : (part + 1) * rows_per, :].astype(BF16)


def collect_states(in_ref, total_ref, parts, rows_per):
    for part in range(parts):
        total_ref[:, part * rows_per : (part + 1) * rows_per, :] = in_ref[part].astype(F32)


def project_rows(meta, j, w, n, pb_ref):
    line = jnp.broadcast_to(pb_ref[pl.ds(meta[j], 1), :], (128, w.shape[0])).T
    bias = jnp.concatenate([line] * (n.shape[0] // 128), axis=1)
    return (mm(w[...], n, NT) + bias).astype(BF16)


def near_kernel(meta, x_ref, p_ref, w0, w1, pb_ref, n_ref, half_ref):
    ready(x_ref)
    normal, _ = norm_parts(x_ref[...].astype(F32))
    n = (normal * p_ref[0:1] + p_ref[1:2]).astype(BF16)
    n_ref[...] = n
    flush(n_ref)
    span = w0.shape[0]
    for j, w in enumerate((w0, w1)):
        ready(w)
        start = pl.multiple_of((meta[j] & 1) * span, 64)
        half_ref[pl.ds(start, span), :] = project_rows(meta, j, w, n, pb_ref)


def far_kernel(meta, n_ref, near_ref, w2, w3, pb_ref, qkv_ref):
    span = w2.shape[0]
    ready(n_ref)
    start = pl.multiple_of((meta[0] >> 1) * 2 * span, 64)
    qkv_ref[pl.ds(start, 2 * span), :] = near_ref[...]
    for j, w in ((2, w2), (3, w3)):
        ready(w)
        start = pl.multiple_of(meta[j] * span, 64)
        qkv_ref[pl.ds(start, span), :] = project_rows(meta, j, w, n_ref[...], pb_ref)


def phi(rows_ref, base, map_ref, h):
    rows = rows_ref[pl.ds(pl.multiple_of(base + h * 64, 64), 64), :]
    logits = mm(map_ref[h], rows, TN)
    up = jnp.exp(logits - jnp.max(logits, axis=0, keepdims=True))
    down = jnp.exp(jnp.min(logits, axis=0, keepdims=True) - logits)
    p1 = up * (1.0 / jnp.sum(up, axis=0, keepdims=True))
    p2 = down * (1.0 / jnp.sum(down, axis=0, keepdims=True))
    return p1.astype(BF16), p2.astype(BF16)


def key_kernel(heads, slots, parts, meta, qkv_ref, map_ref, fk_ref, s_ref, total):
    width = heads * 64
    cols = qkv_ref.shape[1] // slots
    rows_per = s_ref.shape[2]
    total[...] = jnp.zeros_like(total)

    def head(h, carry):
        p1, p2 = phi(qkv_ref, width, map_ref, h)
        at = pl.multiple_of(h * 128, 128)
        fk_ref[pl.ds(at, 64), :] = p1
        fk_ref[pl.ds(pl.multiple_of(at + 64, 64), 64), :] = p2
        v = qkv_ref[pl.ds(pl.multiple_of(2 * width + h * 64, 64), 64), :]
        va = aug_rows(v, 1.0)
        fk = jnp.concatenate([p1, p2], axis=0)
        for s in range(slots):
            part = slice(s * cols, (s + 1) * cols)
            state = mm(va[:, part], fk[:, part], NT)
            total[s ^ meta[4], pl.ds(pl.multiple_of(h * KEEP, 8), KEEP), :] = state[:KEEP]
        return carry

    lax.fori_loop(0, heads, head, 0, unroll=UNROLL)
    flush(fk_ref)
    spread_states(total, s_ref, parts, rows_per)


def query_kernel(heads, qkv_ref, map_ref, fq_ref):
    def head(h, carry):
        p1, p2 = phi(qkv_ref, 0, map_ref, h)
        at = pl.multiple_of(h * 128, 128)
        fq_ref[pl.ds(at, 64), :] = p1
        fq_ref[pl.ds(pl.multiple_of(at + 64, 64), 64), :] = p2
        return carry

    lax.fori_loop(0, heads, head, 0, unroll=UNROLL)


def scan_kernel(nctx, backward, keep, in_ref, out_ref):
    blocks = 2 * nctx
    order = [(b, 0) if b < nctx else (blocks - 1 - b, 1) for b in range(blocks)]
    acc = jnp.zeros(in_ref.shape[2:], F32)
    for b in reversed(range(blocks)) if backward else range(blocks):
        c, lane = order[b]
        acc = acc * keep[b] + in_ref[c, lane].astype(F32)
        out_ref[c, lane] = acc.astype(BF16)


def fill_output(meta, wo_refs, wo):
    rows = wo_refs[0].shape[0]
    for j, ref in enumerate(wo_refs):
        wo[pl.ds(pl.multiple_of(meta[j] * rows, 64), rows), :] = ref[...]


def attend_kernel(
    heads, slots, parts, meta, c_ref, fq_ref, x_ref, w0, w1, w2, w3, p_ref,
    mixed_ref, den_ref, middle_ref, n2_ref, wo, total,
):
    cols = fq_ref.shape[1] // slots
    collect_states(c_ref, total, parts, c_ref.shape[2])
    ready(fq_ref)

    def head(h, carry):
        fq = fq_ref[pl.ds(pl.multiple_of(h * 128, 128), 128), :]
        for s in range(slots):
            part = slice(s * cols, (s + 1) * cols)
            c = total[s ^ meta[4], pl.ds(pl.multiple_of(h * KEEP, 8), AUG), :].astype(BF16)
            both = mm(c, fq[:, part], NN)
            den = both[64:65]
            mixed = both[:64] * (1.0 / den)
            mixed_ref[pl.ds(pl.multiple_of(h * 64, 64), 64), part] = mixed.astype(BF16)
            den_ref[pl.ds(pl.multiple_of(h * 8, 8), 8), part] = jnp.broadcast_to(den, (8, cols))
        return carry

    lax.fori_loop(0, heads, head, 0, unroll=UNROLL)
    flush(mixed_ref, den_ref)
    ready(x_ref, w0, w1, w2, w3)
    fill_output(meta, (w0, w1, w2, w3), wo)
    flush(wo)
    middle = x_ref[...].astype(F32) + mm(mixed_ref[...], wo[...], TN) + p_ref[4:5]
    middle_ref[...] = middle
    flush(middle_ref)
    normal, _ = norm_parts(middle)
    n2 = (normal * p_ref[2:3] + p_ref[3:4]).astype(BF16)
    n2_ref[...] = n2


def mlp_kernel(first, meta, n2_ref, we, n2o_ref, cot_ref, wr, coto_ref, base_ref, eb_ref, *refs):
    if first:
        out_ref, dn_ref, outo_ref, dno_ref, ge, ge_low, gr, gb_ref, act, hid = refs
    else:
        back_ref, baseo_ref, backo_ref, out_ref, dn_ref, outo_ref, dno_ref, ge, gr, gb_ref, act, hid = refs
    rows_n, width = n2_ref.shape
    line = meta[2] if first else meta[0]
    tile = we.shape[1] // 2
    ready(n2_ref, we, n2o_ref, cot_ref, wr, coto_ref)

    def step(t, carry):
        at = pl.ds(pl.multiple_of(t * tile, tile), tile)
        bias = eb_ref[pl.ds(line, 1), at]
        pre = [
            (mm(n[...], we[:, at], NN) + bias, mm(c[...], wr[at, :], NT))
            for n, c in ((n2_ref, cot_ref), (n2o_ref, coto_ref))
        ]
        actives, hiddens, sums = [], [], None
        for k, (hidden, back) in enumerate(pre):
            square = hidden * hidden
            part = 0.5 + 0.5 * jnp.tanh(
                hidden * (0.7978845608028654 + 0.035677408136300125 * square)
            )
            active = hidden * part
            slope = part + active * (1.0 - part) * (
                1.5957691216057308 + 0.21406444881780075 * square
            )
            r_hidden = back.astype(BF16).astype(F32) * slope
            actives.append(active.astype(BF16))
            hiddens.append(r_hidden.astype(BF16))
            act[k, :, at] = actives[k]
            hid[k, :, at] = hiddens[k]
            total = jnp.sum(r_hidden, axis=0, keepdims=True)
            sums = total if sums is None else sums + total
        gb_ref[:, at] = jnp.broadcast_to(sums, (8, tile))
        grad = (mm(n2_ref[...], hiddens[0], TN) + mm(n2o_ref[...], hiddens[1], TN)).astype(BF16)
        if first:
            ge[:, at] = grad[: width // 2]
            ge_low[:, at] = grad[width // 2 :]
        else:
            ge[:, at] = grad
        gr[at, :] = (
            mm(actives[0], cot_ref[...], TN) + mm(actives[1], coto_ref[...], TN)
        ).astype(BF16)
        return carry

    lax.fori_loop(0, 2, step, 0)
    flush(ge, gr)
    if first:
        flush(ge_low)
    ready(base_ref)
    out_ref[...] = base_ref[...] + mm(act[0], wr[...], NN)
    flush(out_ref)
    dn = mm(hid[0], we[...], NT)
    if first:
        dn_ref[...] = dn
        outo_ref[...] = mm(act[1], wr[...], NN).astype(BF16)
        dno_ref[...] = mm(hid[1], we[...], NT).astype(BF16)
    else:
        dn_ref[...] = back_ref[...] + dn
        flush(dn_ref)
        outo_ref[...] = (baseo_ref[...].astype(F32) + mm(act[1], wr[...], NN)).astype(BF16)
        flush(outo_ref)
        dno_ref[...] = (backo_ref[...].astype(F32) + mm(hid[1], we[...], NT)).astype(BF16)


def middle_kernel(
    heads, slots, parts, meta, dn_ref, dnin_ref, middle_ref, cot_ref, p_ref, mixed_ref, den_ref, fq_ref,
    wo, gm_ref, ratt_ref, raug_ref, g_ref, small_ref, total, rmix,
):
    cols = fq_ref.shape[1] // slots
    ready(middle_ref, dn_ref, dnin_ref, cot_ref)
    normal, scale = norm_parts(middle_ref[...])
    gy = dn_ref[...] + dnin_ref[...].astype(F32)
    cot = cot_ref[...].astype(F32)
    g_middle = cot + norm_back(gy, normal, scale, p_ref[2:3])
    gm_ref[...] = g_middle
    r_att = g_middle.astype(BF16)
    ratt_ref[...] = r_att
    flush(gm_ref, ratt_ref)
    small_ref[...] = jnp.concatenate(
        [
            jnp.sum(gy * normal, axis=0, keepdims=True),
            jnp.sum(gy, axis=0, keepdims=True),
            jnp.sum(r_att.astype(F32), axis=0, keepdims=True),
            jnp.sum(cot, axis=0, keepdims=True),
            jnp.zeros((4, gy.shape[1]), F32),
        ],
        axis=0,
    )
    ready(wo)
    rmix[...] = mm(wo[...], r_att, NT).astype(BF16)
    total[...] = jnp.zeros_like(total)
    ready(mixed_ref, den_ref, fq_ref)

    def head(h, carry):
        rows = pl.ds(pl.multiple_of(h * 64, 64), 64)
        rm = rmix[rows, :].astype(F32)
        inverse = 1.0 / den_ref[pl.ds(pl.multiple_of(h * 8, 8), 8), :][0:1]
        rn = (rm * inverse).astype(BF16)
        rd = -jnp.sum(rm * mixed_ref[rows, :].astype(F32), axis=0, keepdims=True) * inverse
        ra = aug_rows(rn, rd)
        raug_ref[pl.ds(pl.multiple_of(h * AUG, 16), AUG), :] = ra
        fq = fq_ref[pl.ds(pl.multiple_of(h * 128, 128), 128), :]
        for s in range(slots):
            part = slice(s * cols, (s + 1) * cols)
            state = mm(ra[:, part], fq[:, part], NT)
            total[s ^ meta[4], pl.ds(pl.multiple_of(h * KEEP, 8), KEEP), :] = state[:KEEP]
        return carry

    lax.fori_loop(0, heads, head, 0, unroll=UNROLL)
    spread_states(total, g_ref, parts, g_ref.shape[2])
    flush(g_ref, raug_ref)


def logits_back(p_both, g_both):
    p1, p2 = p_both[:64].astype(F32), p_both[64:].astype(F32)
    g1, g2 = g_both[:64], g_both[64:]
    s1 = jnp.sum(p1 * g1, axis=0, keepdims=True)
    s2 = jnp.sum(p2 * g2, axis=0, keepdims=True)
    return (p1 * (g1 - s1) - p2 * (g2 - s2)).astype(BF16)


def query_back_kernel(
    heads, slots, parts, meta, c_ref, raug_ref, fq_ref, qkv_ref, map_ref, mixed_ref, ratt_ref,
    rq_ref, gmap_ref, g0, g1, g2, g3, total,
):
    cols = fq_ref.shape[1] // slots
    ready(c_ref)
    collect_states(c_ref, total, parts, c_ref.shape[2])
    ready(raug_ref, fq_ref, qkv_ref)

    def head(h, carry):
        ra = raug_ref[pl.ds(pl.multiple_of(h * AUG, 16), AUG), :]
        fq = fq_ref[pl.ds(pl.multiple_of(h * 128, 128), 128), :]
        pieces = []
        for s in range(slots):
            part = slice(s * cols, (s + 1) * cols)
            c = total[s ^ meta[4], pl.ds(pl.multiple_of(h * KEEP, 8), AUG), :].astype(BF16)
            pieces.append(mm(c, ra[:, part], TN))
        r_fq = jnp.concatenate(pieces, axis=1).astype(BF16).astype(F32)
        r_l = logits_back(fq, r_fq)
        rows = pl.ds(pl.multiple_of(h * 64, 64), 64)
        rq_ref[rows, :] = mm(map_ref[h], r_l, NN).astype(BF16)
        gmap_ref[h] = mm(qkv_ref[rows, :], r_l, NT)
        return carry

    lax.fori_loop(0, heads, head, 0, unroll=UNROLL)
    flush(rq_ref, gmap_ref)
    ready(mixed_ref, ratt_ref)
    rows = g0.shape[0]
    for j, g in enumerate((g0, g1, g2, g3)):
        mixed = mixed_ref[pl.ds(pl.multiple_of(meta[j] * rows, 64), rows), :]
        g[...] = mm(mixed, ratt_ref[...], NN).astype(BF16)
        flush(g)


def key_back_kernel(
    heads, slots, parts, meta, d_ref, fk_ref, qkv_ref, map_ref, rq_ref, n_ref,
    rp_ref, gmap_ref, g1, g3, total,
):
    width = heads * 64
    cols = fk_ref.shape[1] // slots
    collect_states(d_ref, total, parts, d_ref.shape[2])
    ready(fk_ref, qkv_ref, rq_ref)
    rp_ref[0:width, :] = rq_ref[...]

    def head(h, carry):
        fk = fk_ref[pl.ds(pl.multiple_of(h * 128, 128), 128), :]
        v = qkv_ref[pl.ds(pl.multiple_of(width + h * 64, 64), 64), :]
        va = aug_rows(v, 1.0)
        pieces = []
        for s in range(slots):
            part = slice(s * cols, (s + 1) * cols)
            d = total[s ^ meta[4], pl.ds(pl.multiple_of(h * KEEP, 8), AUG), :].astype(BF16)
            pieces.append(mm(d, va[:, part], TN))
            rv = mm(d[:64], fk[:, part], NN).astype(BF16)
            rp_ref[pl.ds(pl.multiple_of(2 * width + h * 64, 64), 64), part] = rv
        r_fk = jnp.concatenate(pieces, axis=1).astype(BF16).astype(F32)
        r_l = logits_back(fk, r_fk)
        rows = pl.ds(pl.multiple_of(width + h * 64, 64), 64)
        rp_ref[rows, :] = mm(map_ref[h], r_l, NN).astype(BF16)
        keys = qkv_ref[pl.ds(pl.multiple_of(h * 64, 64), 64), :]
        gmap_ref[h] = mm(keys, r_l, NT)
        return carry

    lax.fori_loop(0, heads, head, 0, unroll=UNROLL)
    flush(rp_ref, gmap_ref)
    ready(n_ref)
    span = g1.shape[0]
    for j, g in ((1, g1), (3, g3)):
        rp = rp_ref[pl.ds(pl.multiple_of(meta[j] * span, 64), span), :]
        g[...] = mm(rp, n_ref[...], NN).astype(BF16)
        flush(g)


def project_grad_kernel(meta, rp_ref, n_ref, in0, in2, go0, go0_in, go2, go2_in, own, cross):
    span = in0.shape[0]
    ready(rp_ref, n_ref, in0, in2, go0, go0_in, go2, go2_in)
    for j, more, go, go_in, out in ((2, in2, go2, go2_in, cross), (0, in0, go0, go0_in, own)):
        rp = rp_ref[pl.ds(pl.multiple_of(meta[j] * span, 64), span), :]
        out[:span, :] = (mm(rp, n_ref[...], NN) + more[...].astype(F32)).astype(BF16)
        out[span:, :] = (go[...].astype(F32) + go_in[...].astype(F32)).astype(BF16)
        flush(out)


def input_kernel(
    heads, meta, rp_ref, x_ref, p_ref, gm_ref, out_ref, outin_ref, two_ref, ebo_ref, ebc_ref,
    mq_ref, mk_ref, w0, w1, w2, w3, dx_ref, full_ref, b0, b1, b2, b3, pack,
):
    ready(out_ref, outin_ref)
    full_ref[...] = out_ref[...] + outin_ref[...].astype(F32) + p_ref[5:6]
    flush(full_ref)
    span, width = w0.shape
    shard = width // 4
    own_heads = heads // 4
    ones = jnp.ones((8, x_ref.shape[0]), BF16)
    pack[...] = jnp.zeros_like(pack)
    gy = None
    ready(rp_ref, w0, w1, w2, w3, x_ref, gm_ref)
    for j, w in enumerate((w0, w1, w2, w3)):
        rp = rp_ref[pl.ds(pl.multiple_of(meta[j] * span, 64), span), :]
        part = mm(rp, w[...], TN)
        gy = part if gy is None else gy + part
        pack[meta[j], 8:16, :span] = mm(ones, rp, NT)
    ready(ebo_ref, ebc_ref, two_ref)
    pack[meta[0], 16:24, :] = ebo_ref[...]
    pack[meta[2], 16:24, :] = ebc_ref[...]
    normal, scale = norm_parts(x_ref[...].astype(F32))
    dx_ref[...] = gm_ref[...] + norm_back(gy, normal, scale, p_ref[0:1])
    flush(dx_ref)
    ready(mq_ref, mk_ref)
    lines = [
        jnp.sum(gy * normal, axis=0, keepdims=True),
        jnp.sum(gy, axis=0, keepdims=True),
        two_ref[0:1], two_ref[1:2], two_ref[2:3], two_ref[3:4],
    ]
    for i in range(4):
        cut = slice(i * shard, (i + 1) * shard)
        for k, line in enumerate(lines):
            pack[i, k : k + 1, :shard] = line[:, cut]
        for base, ref in ((24, mq_ref), (40, mk_ref)):
            for k in range(4):
                for h in range(own_heads):
                    at = k * shard + h * 64
                    pack[i, base : base + 16, at : at + 64] = ref[
                        i * own_heads + h, 16 * k : 16 * k + 16, :
                    ]
    for j, b in enumerate((b0, b1, b2, b3)):
        b[...] = pack[meta[j]].astype(BF16)


def unpack_kernel(rest_ref, g1, s1, g2, s2, bo, br, pb, eb, mq, mk):
    shard = g1.shape[1]
    own_heads = mq.shape[0]
    for k, ref in enumerate((g1, s1, g2, s2, bo, br)):
        ref[...] = rest_ref[k : k + 1, :shard]
    pb[...] = rest_ref[8:9, : pb.shape[1]]
    eb[...] = rest_ref[16:17, :]
    for base, ref in ((24, mq), (40, mk)):
        for k in range(4):
            for h in range(own_heads):
                at = k * shard + h * 64
                ref[h, 16 * k : 16 * k + 16, :] = rest_ref[base : base + 16, at : at + 64]


def line1(a):
    return a.reshape(-1)


def core_swap(a):
    return lax.ppermute(a, "fsdp", CORE)


def cross_swap(a):
    return lax.ppermute(a, "fsdp", CROSS)


def after(value, *others):
    return lax.optimization_barrier((value, *others))[0]


def spread(shard, cross):
    return [shard, core_swap(shard), cross, core_swap(cross)]


def add(a, b):
    return (a.astype(F32) + b.astype(F32)).astype(BF16)


def rows_sum(parts, start, size):
    out = None
    for offset, part in parts:
        if isinstance(part, tuple):
            part, offset = jnp.where(start + offset < part[0].shape[0], *part), -start
        piece = lax.dynamic_slice_in_dim(part, start + offset, size, 0).astype(F32)
        out = piece if out is None else out + piece
    return out.astype(BF16)


class Reduction:
    def __init__(self, parts, nctx, place):
        self.parts = [(0, part) for part in parts]
        self.rows, self.nctx, self.place = parts[0].shape[0], nctx, place
        self.groups = [[bit] for bit in range(nctx.bit_length() - 1)]

    def member(self, group):
        return sum(((self.place >> bit) & 1) << k for k, bit in enumerate(group))

    def send(self, value, group, other):
        flip = sum(((other >> k) & 1) << bit for k, bit in enumerate(group))
        return lax.ppermute(value, "ctx", [(i, i ^ flip) for i in range(self.nctx)])

    def scatter(self, level):
        group = self.groups[level]
        count = 1 << len(group)
        mine = self.member(group)
        self.rows //= count
        self.sent = [
            rows_sum(self.parts, (mine ^ d) * self.rows, self.rows) for d in range(1, count)
        ]
        got = [self.send(sent, group, d) for d, sent in enumerate(self.sent, 1)]
        self.parts = [
            (0, jnp.where(mine == 0, *part)) if isinstance(part, tuple)
            else (offset + mine * self.rows, part)
            for offset, part in self.parts
        ]
        self.fresh = len(got)
        self.parts += [(0, g) for g in got]
        return got

    def hold(self, *others):
        last = self.parts[-self.fresh :]
        held = lax.optimization_barrier((tuple(part for _, part in last), others))[0]
        self.parts[-self.fresh :] = [(at, part) for (at, _), part in zip(last, held)]

    def own(self):
        self.cur = rows_sum(self.parts, 0, self.rows)

    def spread(self, level):
        group = self.groups[level]
        self.others = [self.send(self.cur, group, d) for d in range(1, 1 << len(group))]
        self.level = level
        return self.others

    def join(self, *others):
        group = self.groups[self.level]
        parts = [self.cur, *self.others]
        if others:
            parts = list(lax.optimization_barrier((tuple(parts), others))[0])
        for k, bit in enumerate(group):
            swap = ((self.place >> bit) & 1) == 1
            parts = [
                jnp.where(swap, parts[j ^ (1 << k)], parts[j]) for j in range(len(parts))
            ]
        self.cur = jnp.concatenate(parts, axis=0)

    def deep(self, first):
        for level in range(first, len(self.groups)):
            self.scatter(level)
        self.own()
        for level in reversed(range(first, len(self.groups))):
            self.spread(level)
            self.join()


def straighten(parts, mine):
    a, b, c, d = parts
    odd = (mine & 1) == 1
    upper = (mine & 2) == 2
    a, b = jnp.where(odd, b, a), jnp.where(odd, a, b)
    c, d = jnp.where(odd, d, c), jnp.where(odd, c, d)
    return [
        jnp.where(upper, c, a), jnp.where(upper, d, b),
        jnp.where(upper, a, c), jnp.where(upper, b, d),
    ]


def exchange(a):
    return lax.all_to_all(a, "ctx", 0, 0, tiled=True)


def body(
    tokens, cotangent, pair_table, seq_ids, first_gain, first_shift, project_weight, project_bias,
    feature_query, feature_key, output_weight, output_bias, second_gain, second_shift,
    expand_weight, expand_bias, reduce_weight, reduce_bias,
):
    x = tokens[0]
    cot = cotangent[0]
    rows_n, width = x.shape
    heads = width // feature_query.shape[1]
    own_heads = feature_query.shape[0]
    slots = pair_table.shape[2]
    nctx = lax.axis_size("ctx")
    place = lax.axis_index("ctx")
    mine = lax.axis_index("fsdp")
    span = project_weight.shape[1]
    hidden_own = expand_weight.shape[1]
    shard = width // 4
    wide = heads * 128

    project_t = project_weight.T
    cross_project = cross_swap(project_t)
    vector = jnp.concatenate(
        [first_gain, first_shift, second_gain, second_shift, output_bias, reduce_bias,
         project_bias, expand_bias]
    )
    room = -vector.shape[0] % 1024
    vector = jnp.concatenate([vector, jnp.zeros((room,), BF16)]).reshape(-1, 64)
    map_rows = own_heads * 64
    pack = jnp.concatenate(
        [feature_query.reshape(-1, 64), feature_key.reshape(-1, 64), vector]
    )
    packs = spread(pack, cross_swap(pack))
    ordered = straighten(packs, mine)
    query_map = jnp.concatenate([p[:map_rows] for p in ordered]).reshape(heads, 64, 64)
    key_map = jnp.concatenate([p[map_rows : 2 * map_rows] for p in ordered]).reshape(heads, 64, 64)
    vectors = jnp.stack([p[2 * map_rows :] for p in ordered]).reshape(4, -1).astype(F32)
    params = vectors[:, : 6 * shard].reshape(4, 6, shard).transpose(1, 0, 2).reshape(6, width)
    project_line = vectors[:, 6 * shard : 6 * shard + span]
    expand_line = vectors[:, 6 * shard + span : 6 * shard + span + hidden_own]
    project_core = core_swap(project_t)
    project_far = core_swap(cross_project)
    projects = [project_t, project_core, cross_project, project_far]
    near_first = jnp.concatenate([expand_weight, output_weight])
    cross_first = cross_swap(after(near_first, cross_project))
    core_output = core_swap(output_weight)
    cross_reduce = cross_swap(after(reduce_weight, cross_first))
    cot_other = core_swap(cot)

    positions = pair_table[0, 0]
    swap = (positions[0] > positions[1]).astype(jnp.int32)
    meta = jnp.stack([mine, mine ^ 1, mine ^ 2, mine ^ 3, swap]).astype(jnp.int32)
    ids = seq_ids[0]
    same = (ids[1:] == ids[:-1]).astype(F32)
    none = jnp.zeros((1,), F32)
    keep = jnp.concatenate([none, same])
    keep_next = jnp.concatenate([same, none])

    rows_per = -(-(heads * KEEP) // (nctx * 16)) * 16
    state_shape = shaped((nctx, slots, rows_per, 128), BF16)
    total = pltpu.VMEM((slots, nctx * rows_per, 128), F32)
    wo_scratch = pltpu.VMEM((width, width), BF16)
    low = shaped((rows_n, width), BF16)
    full = shaped((rows_n, width))
    table = shaped((width, rows_n), BF16)
    square = shaped((heads, 64, 64))

    n1, near = call(
        near_kernel, [low, shaped((2 * span, rows_n), BF16)], "shvaav",
        [meta, x, params, projects[0], projects[1], project_line], "project_near", (), "hv",
    )
    (qkv,) = call(
        far_kernel, [shaped((3 * width, rows_n), BF16)], "shvaav",
        [meta, n1, near, projects[2], projects[3], project_line], "project_far",
    )
    fk, states = call(
        functools.partial(key_kernel, heads, slots, nctx),
        [shaped((wide, rows_n), BF16), state_shape], "svv",
        [meta, qkv, key_map], "keys", [total], "hh",
    )
    arrived = exchange(states)
    (fq,) = call(
        functools.partial(query_kernel, heads), [shaped((wide, rows_n), BF16)], "vv",
        [after(qkv, states), query_map], "queries", (), "h", flops=10**12,
    )
    (running,) = call(
        functools.partial(scan_kernel, nctx, False), [state_shape], "sv",
        [keep, after(arrived, cross_first)], "scan", (), "h",
    )
    carried = exchange(running)
    far_output = core_swap(after(cross_first, running)[width : width + shard])
    outputs = [output_weight, core_output, (cross_first, width, shard), far_output]
    mixed, den, middle, n2, wo = call(
        functools.partial(attend_kernel, heads, slots, nctx),
        [table, shaped((heads * 8, rows_n)), full, low, shaped((width, width), BF16)],
        "svhhhvavv", [meta, carried, fq, x, *outputs, params], "attend",
        [total], "hhhvh",
    )
    n2_other = core_swap(n2)

    def mlp(first, base, w_in, w_out, more, name):
        half = shaped((width // 2, hidden_own), BF16)
        grads = [half, half] if first else [shaped((width, hidden_own), BF16)]
        return call(
            functools.partial(mlp_kernel, first),
            [full, full, low, low, *grads, shaped((hidden_own, width), BF16),
             shaped((8, hidden_own))],
            "saaaaaa" + ("h" if first else "v") + "v" + "v" * len(more),
            [meta, n2, w_in, n2_other, cot, w_out, cot_other, base, expand_line, *more], name,
            [pltpu.VMEM((2, rows_n, hidden_own), BF16)] * 2,
            "vvvvhhhv" if first else "hhhvhhv", 48,
        )

    out1, dn1, out1_o, dn1_o, ge_top, ge_low, gr_cross, gb_cross = mlp(
        True, middle, (cross_first, 0, width), cross_reduce, [], "mlp_far"
    )
    top_in = cross_swap(ge_top)
    low_in = cross_swap(after(ge_low, top_in))
    out2, dn2, out2_o, dn2_o, ge_own, gr_own, gb_own = mlp(
        False, out1, expand_weight, reduce_weight, [dn1, out1_o, dn1_o], "mlp_near"
    )
    dn2_in = core_swap(after(dn2_o, top_in))

    g_middle, r_att, raug, g_states, small_two = call(
        functools.partial(middle_kernel, heads, slots, nctx),
        [full, low, shaped((heads * AUG, rows_n), BF16), state_shape, shaped((8, width))],
        "shahavhhhh",
        [meta, dn2, dn2_in, middle, cot, params, mixed, den, fq, wo], "middle",
        [total, pltpu.VMEM((width, rows_n), BF16)], "hhhhv",
    )
    g_arrived = exchange(g_states)
    gr_in = cross_swap(after(gr_cross, low_in))
    out2_in = core_swap(after(out2_o, g_states))
    rq, g_query_map, *go = call(
        functools.partial(query_back_kernel, heads, slots, nctx),
        [table, square] + [shaped((shard, width), BF16)] * 4,
        "sahhavhh", [meta, carried, raug, fq, (qkv, 0, width), query_map, mixed, r_att], "query_back",
        [total], "hhhhhh",
    )
    (g_running,) = call(
        functools.partial(scan_kernel, nctx, True), [state_shape], "sv",
        [keep_next, after(g_arrived, rq, low_in)], "scan_back", (), "h",
    )
    g_carried = exchange(g_running)
    top_in, low_in = lax.optimization_barrier((top_in, low_in, g_running))[:2]
    sum_e = Reduction([ge_own, (top_in, low_in)], nctx, place)
    e_got = sum_e.scatter(0)
    sum_r = Reduction([gr_own, after(gr_in, g_running)], nctx, place)
    r_got = sum_r.scatter(0)
    go_far, go_core = core_swap(after(go[3], g_running)), core_swap(after(go[1], g_running))
    rp, g_key_map, gp1, gp3 = call(
        functools.partial(key_back_kernel, heads, slots, nctx),
        [shaped((3 * width, rows_n), BF16), square] + [shaped((span, width), BF16)] * 2,
        "svhavhh", [meta, after(g_carried, sum_e.sent, sum_r.sent), fk, (qkv, width, 2 * width), key_map, rq, n1],
        "key_back", [total], "hhhh",
    )
    gp3_in, gp1_in = core_swap(after(gp3, e_got)), core_swap(after(gp1, e_got))
    p_own, p_cross = call(
        project_grad_kernel, [shaped((width, width), BF16)] * 2, "shhaahaha",
        [meta, rp, n1, gp1_in, gp3_in, go[0], go_core, go[2], go_far], "project_grad", (), "hh",
    )
    p_in = cross_swap(p_cross)
    sum_e.hold(p_own)
    sum_e.scatter(1)
    small = shaped((64, width), BF16)
    dx, layer_out, own_s, core_s, cross_s, far_s = call(
        functools.partial(input_kernel, heads), [full, full, small, small, small, small],
        "shhvhhaaaahhaaaa",
        [meta, rp, after(x, p_own, sum_e.sent), params, g_middle, out2, out2_in, small_two,
         gb_own, gb_cross, g_query_map, g_key_map, *projects],
        "input", [pltpu.VMEM((4, 64, width), F32)], "hhvvvv",
    )
    far_in, core_in = core_swap(far_s), core_swap(core_s)
    cross_in = cross_swap(add(cross_s, far_in))
    small_own = add(own_s, core_in)
    sum_e.hold(far_in, core_in)
    e_got = sum_e.scatter(2)
    sum_r.hold(far_in, core_in)
    r_got = sum_r.scatter(1)
    sum_p = Reduction([p_own, p_in], nctx, place)
    p_got = sum_p.scatter(0)
    sum_e.hold(sum_p.sent)
    sum_r.hold(sum_p.sent)
    sum_e.deep(3)
    e_got = sum_e.spread(2)
    r_got = sum_r.scatter(2)
    sum_p.hold(e_got, r_got)
    sum_p.scatter(1)
    sum_e.join(sum_p.sent)
    e_got = sum_e.spread(1)
    sum_r.hold(sum_p.sent)
    sum_r.deep(3)
    r_got = sum_r.spread(2)
    sum_p.hold(e_got, r_got)
    sum_p.scatter(2)
    sum_e.join(sum_p.sent)
    e_got = sum_e.spread(0)
    sum_r.join(sum_p.sent)
    r_got = sum_r.spread(1)
    sum_p.deep(3)
    sum_r.join(sum_p.cur)
    r_got = sum_r.spread(0)
    sum_p.spread(2)
    sum_p.join(e_got)
    sum_p.spread(1)
    sum_p.join(r_got)
    sum_p.spread(0)
    sum_p.join()
    sum_e.join()
    sum_r.join()
    g_expand, g_reduce, g_project = sum_e.cur, sum_r.cur, sum_p.cur
    rest = small_own.astype(F32) + cross_in.astype(F32)
    for level in range(len(sum_p.groups)):
        low_rest = rest.astype(BF16)
        rest = low_rest.astype(F32) + sum_p.send(low_rest, sum_p.groups[level], 1).astype(F32)
    g_output = g_project[span : span + shard]
    line = shaped((1, shard))
    g1, s1, g2, s2, bo, br, pb, eb, mq, mk = call(
        unpack_kernel,
        [line] * 6 + [shaped((1, span)), shaped((1, hidden_own))]
        + [shaped((own_heads, 64, 64))] * 2, "v", [rest], "unpack",
    )
    return (
        layer_out[None], dx[None], line1(g1), line1(s1), g_project[:span].T.astype(F32), line1(pb), mq, mk,
        g_output.astype(F32), line1(bo), line1(g2), line1(s2), g_expand.astype(F32), line1(eb),
        g_reduce.astype(F32), line1(br),
    )


def solution(mesh):
    row = P("fsdp", "ctx", None)
    vec = P("fsdp")
    maps = P("fsdp", None, None)
    in_specs = (
        row, row, row, P("fsdp", None), vec, vec, P(None, "fsdp"), vec, maps, maps,
        P("fsdp", None), vec, vec, vec, P(None, "fsdp"), vec, P("fsdp", None), vec,
    )
    out_specs = (
        row, row, vec, vec, P(None, "fsdp"), vec, maps, maps, P("fsdp", None), vec, vec, vec,
        P(None, "fsdp"), vec, P("fsdp", None), vec,
    )
    return jax.shard_map(body, mesh=mesh, in_specs=in_specs, out_specs=out_specs, check_vma=False)
```

```python
import functools

import jax
import jax.numpy as jnp
from jax import lax
from jax.experimental import pallas as pl
from jax.experimental.pallas import tpu as pltpu
from jax.sharding import PartitionSpec as P

EPS = 1e-05
F32 = jnp.float32
BF16 = jnp.bfloat16
AUG = 80
KEEP = 72
UNROLL = 6
NN = (((1,), (0,)), ((), ()))
NT = (((1,), (1,)), ((), ()))
TN = (((0,), (0,)), ((), ()))
CORE = [(i, i ^ 1) for i in range(4)]
CROSS = [(i, i ^ 2) for i in range(4)]
VMEM = pl.BlockSpec(memory_space=pltpu.VMEM)
SMEM = pl.BlockSpec(memory_space=pltpu.SMEM)
FAR = pl.BlockSpec(memory_space=pltpu.HBM)
ANYWHERE = pl.BlockSpec(memory_space=pl.ANY)
SPECS = {"v": VMEM, "s": SMEM, "h": FAR, "a": ANYWHERE}


def mm(a, b, dims):
    return lax.dot_general(a, b, dims, preferred_element_type=F32)


class Staged:
    def __init__(self, far, near, sems, out):
        self.near, self.state = near, "out" if out else "in"
        self.copies, at = [], 0
        for part, sem in zip(far, sems):
            here = near if len(far) == 1 else near.at[pl.ds(at, part.shape[0])]
            pair = (here, part) if out else (part, here)
            self.copies.append(pltpu.make_async_copy(*pair, sem))
            at += part.shape[0]
        self.shape, self.dtype = near.shape, near.dtype
        if not out:
            self.start()

    def start(self):
        for copy in self.copies:
            copy.start()

    def wait(self):
        for copy in self.copies:
            copy.wait()

    def ready(self):
        if self.state == "in":
            self.wait()
            self.state = "ready"

    def flush(self):
        if self.state == "out":
            self.start()
            self.state = "flushed"

    def finish(self):
        self.ready()
        self.flush()
        if self.state == "flushed":
            self.wait()
            self.state = "done"

    def __getitem__(self, index):
        assert self.state in ("ready", "out", "flushed")
        return self.near[index]

    def __setitem__(self, index, value):
        assert self.state == "out"
        self.near[index] = value


def ready(*refs):
    for ref in refs:
        if isinstance(ref, Staged):
            ref.ready()


def flush(*refs):
    for ref in refs:
        if isinstance(ref, Staged):
            ref.flush()


def call(kernel, outs, kinds, args, name, scratch=(), out_kinds=None, limit=32, flops=1):
    out_kinds = out_kinds or "v" * len(outs)
    both = kinds + out_kinds
    groups = [a if isinstance(a, list) else [a] for a in [*args, *outs]]
    groups = [
        [p if isinstance(p, tuple) else (p, 0, p.shape[0]) for p in group] for group in groups
    ]
    operands = [(p[0], k) for group, k in zip(groups[: len(kinds)], kinds) for p in group]
    pieces = sum(len(group) for group, k in zip(groups, both) if k in "ha")
    staged = [
        pltpu.VMEM((sum(p[2] for p in group), *group[0][0].shape[1:]), group[0][0].dtype)
        for group, k in zip(groups, both) if k in "ha"
    ]

    def run(*refs):
        count = sum(len(group) for group in groups)
        extra = len(staged)
        near = refs[count : count + extra]
        sems = refs[count + extra] if extra else None
        rest = refs[count + extra + (1 if extra else 0) :]
        use, at, ref_at, sem_at = [], 0, 0, 0
        for i, (kind, group) in enumerate(zip(both, groups)):
            mine = refs[ref_at : ref_at + len(group)]
            ref_at += len(group)
            if kind in "ha":
                far = [
                    ref if ref.shape[0] == size else ref.at[pl.ds(start, size)]
                    for ref, (_, start, size) in zip(mine, group)
                ]
                own = [sems.at[sem_at + j] for j in range(len(group))]
                sem_at += len(group)
                use.append(Staged(far, near[at], own, i >= len(kinds)))
                at += 1
            else:
                use.append(mine[0])
        kernel(*use, *rest)
        for ref in use:
            if isinstance(ref, Staged):
                ref.finish()

    sems = [pltpu.SemaphoreType.DMA((pieces,))] if staged else []
    return pl.pallas_call(
        run,
        out_shape=[
            pltpu.HBM(o.shape, o.dtype) if k == "h" else o for o, k in zip(outs, out_kinds)
        ],
        in_specs=[SPECS[k] for _, k in operands],
        out_specs=[SPECS[k] for k in out_kinds],
        scratch_shapes=[*staged, *sems, *scratch],
        compiler_params=pltpu.CompilerParams(vmem_limit_bytes=limit << 20),
        cost_estimate=pl.CostEstimate(flops=flops, bytes_accessed=1, transcendentals=0),
        name=name,
    )(*[
        pltpu.with_memory_space_constraint(a, pltpu.HBM) if k == "h" else a
        for a, k in operands
    ])


def shaped(shape, dtype=F32):
    return jax.ShapeDtypeStruct(shape, dtype)


def norm_parts(v):
    center = v - jnp.mean(v, axis=-1, keepdims=True)
    scale = lax.rsqrt(jnp.mean(center * center, axis=-1, keepdims=True) + EPS)
    return center * scale, scale


def norm_back(gy, normal, scale, gain):
    a = gy * gain
    return (
        a - jnp.mean(a, axis=-1, keepdims=True)
        - normal * jnp.mean(a * normal, axis=-1, keepdims=True)
    ) * scale


def aug_rows(top, row):
    index = lax.broadcasted_iota(jnp.int32, (AUG - top.shape[0], top.shape[1]), 0)
    tail = jnp.where(index == 0, row, 0.0).astype(BF16)
    return jnp.concatenate([top, tail], axis=0)


def spread_states(total_ref, out_ref, parts, rows_per):
    for part in range(parts):
        out_ref[part] = total_ref[:, part * rows_per : (part + 1) * rows_per, :].astype(BF16)


def collect_states(in_ref, total_ref, parts, rows_per):
    for part in range(parts):
        total_ref[:, part * rows_per : (part + 1) * rows_per, :] = in_ref[part].astype(F32)


def project_rows(meta, j, w, n, pb_ref):
    line = jnp.broadcast_to(pb_ref[pl.ds(meta[j], 1), :], (128, w.shape[0])).T
    bias = jnp.concatenate([line] * (n.shape[0] // 128), axis=1)
    return (mm(w[...], n, NT) + bias).astype(BF16)


def near_kernel(meta, x_ref, p_ref, w0, w1, pb_ref, n_ref, half_ref):
    ready(x_ref)
    normal, _ = norm_parts(x_ref[...].astype(F32))
    n = (normal * p_ref[0:1] + p_ref[1:2]).astype(BF16)
    n_ref[...] = n
    flush(n_ref)
    span = w0.shape[0]
    for j, w in enumerate((w0, w1)):
        ready(w)
        start = pl.multiple_of((meta[j] & 1) * span, 64)
        half_ref[pl.ds(start, span), :] = project_rows(meta, j, w, n, pb_ref)


def far_kernel(meta, n_ref, near_ref, w2, w3, pb_ref, qkv_ref):
    span = w2.shape[0]
    ready(n_ref)
    start = pl.multiple_of((meta[0] >> 1) * 2 * span, 64)
    qkv_ref[pl.ds(start, 2 * span), :] = near_ref[...]
    for j, w in ((2, w2), (3, w3)):
        ready(w)
        start = pl.multiple_of(meta[j] * span, 64)
        qkv_ref[pl.ds(start, span), :] = project_rows(meta, j, w, n_ref[...], pb_ref)


def phi(rows_ref, base, map_ref, h):
    rows = rows_ref[pl.ds(pl.multiple_of(base + h * 64, 64), 64), :]
    logits = mm(map_ref[h], rows, TN)
    up = jnp.exp(logits - jnp.max(logits, axis=0, keepdims=True))
    down = jnp.exp(jnp.min(logits, axis=0, keepdims=True) - logits)
    p1 = up * (1.0 / jnp.sum(up, axis=0, keepdims=True))
    p2 = down * (1.0 / jnp.sum(down, axis=0, keepdims=True))
    return p1.astype(BF16), p2.astype(BF16)


def key_kernel(heads, slots, parts, meta, qkv_ref, map_ref, fk_ref, s_ref, total):
    width = heads * 64
    cols = qkv_ref.shape[1] // slots
    rows_per = s_ref.shape[2]
    total[...] = jnp.zeros_like(total)

    def head(h, carry):
        p1, p2 = phi(qkv_ref, width, map_ref, h)
        at = pl.multiple_of(h * 128, 128)
        fk_ref[pl.ds(at, 64), :] = p1
        fk_ref[pl.ds(pl.multiple_of(at + 64, 64), 64), :] = p2
        v = qkv_ref[pl.ds(pl.multiple_of(2 * width + h * 64, 64), 64), :]
        va = aug_rows(v, 1.0)
        fk = jnp.concatenate([p1, p2], axis=0)
        for s in range(slots):
            part = slice(s * cols, (s + 1) * cols)
            state = mm(va[:, part], fk[:, part], NT)
            total[s ^ meta[4], pl.ds(pl.multiple_of(h * KEEP, 8), KEEP), :] = state[:KEEP]
        return carry

    lax.fori_loop(0, heads, head, 0, unroll=UNROLL)
    flush(fk_ref)
    spread_states(total, s_ref, parts, rows_per)


def query_kernel(heads, qkv_ref, map_ref, fq_ref):
    def head(h, carry):
        p1, p2 = phi(qkv_ref, 0, map_ref, h)
        at = pl.multiple_of(h * 128, 128)
        fq_ref[pl.ds(at, 64), :] = p1
        fq_ref[pl.ds(pl.multiple_of(at + 64, 64), 64), :] = p2
        return carry

    lax.fori_loop(0, heads, head, 0, unroll=UNROLL)


def scan_kernel(nctx, backward, keep, in_ref, out_ref):
    blocks = 2 * nctx
    order = [(b, 0) if b < nctx else (blocks - 1 - b, 1) for b in range(blocks)]
    acc = jnp.zeros(in_ref.shape[2:], F32)
    for b in reversed(range(blocks)) if backward else range(blocks):
        c, lane = order[b]
        acc = acc * keep[b] + in_ref[c, lane].astype(F32)
        out_ref[c, lane] = acc.astype(BF16)


def fill_output(meta, wo_refs, wo):
    rows = wo_refs[0].shape[0]
    for j, ref in enumerate(wo_refs):
        wo[pl.ds(pl.multiple_of(meta[j] * rows, 64), rows), :] = ref[...]


def attend_kernel(
    heads, slots, parts, meta, c_ref, fq_ref, x_ref, w0, w1, w2, w3, p_ref,
    mixed_ref, den_ref, middle_ref, n2_ref, wo, total,
):
    cols = fq_ref.shape[1] // slots
    collect_states(c_ref, total, parts, c_ref.shape[2])
    ready(fq_ref)

    def head(h, carry):
        fq = fq_ref[pl.ds(pl.multiple_of(h * 128, 128), 128), :]
        for s in range(slots):
            part = slice(s * cols, (s + 1) * cols)
            c = total[s ^ meta[4], pl.ds(pl.multiple_of(h * KEEP, 8), AUG), :].astype(BF16)
            both = mm(c, fq[:, part], NN)
            den = both[64:65]
            mixed = both[:64] * (1.0 / den)
            mixed_ref[pl.ds(pl.multiple_of(h * 64, 64), 64), part] = mixed.astype(BF16)
            den_ref[pl.ds(pl.multiple_of(h * 8, 8), 8), part] = jnp.broadcast_to(den, (8, cols))
        return carry

    lax.fori_loop(0, heads, head, 0, unroll=UNROLL)
    flush(mixed_ref, den_ref)
    ready(x_ref, w0, w1, w2, w3)
    fill_output(meta, (w0, w1, w2, w3), wo)
    flush(wo)
    middle = x_ref[...].astype(F32) + mm(mixed_ref[...], wo[...], TN) + p_ref[4:5]
    middle_ref[...] = middle
    flush(middle_ref)
    normal, _ = norm_parts(middle)
    n2 = (normal * p_ref[2:3] + p_ref[3:4]).astype(BF16)
    n2_ref[...] = n2


def mlp_kernel(first, meta, n2_ref, we, n2o_ref, cot_ref, wr, coto_ref, base_ref, eb_ref, *refs):
    if first:
        out_ref, dn_ref, outo_ref, dno_ref, ge, ge_low, gr, gb_ref, act, hid = refs
    else:
        back_ref, baseo_ref, backo_ref, out_ref, dn_ref, outo_ref, dno_ref, ge, gr, gb_ref, act, hid = refs
    rows_n, width = n2_ref.shape
    line = meta[2] if first else meta[0]
    tile = we.shape[1] // 2
    ready(n2_ref, we, n2o_ref, cot_ref, wr, coto_ref)

    def step(t, carry):
        at = pl.ds(pl.multiple_of(t * tile, tile), tile)
        bias = eb_ref[pl.ds(line, 1), at]
        pre = [
            (mm(n[...], we[:, at], NN) + bias, mm(c[...], wr[at, :], NT))
            for n, c in ((n2_ref, cot_ref), (n2o_ref, coto_ref))
        ]
        actives, hiddens, sums = [], [], None
        for k, (hidden, back) in enumerate(pre):
            square = hidden * hidden
            part = 0.5 + 0.5 * jnp.tanh(
                hidden * (0.7978845608028654 + 0.035677408136300125 * square)
            )
            active = hidden * part
            slope = part + active * (1.0 - part) * (
                1.5957691216057308 + 0.21406444881780075 * square
            )
            r_hidden = back.astype(BF16).astype(F32) * slope
            actives.append(active.astype(BF16))
            hiddens.append(r_hidden.astype(BF16))
            act[k, :, at] = actives[k]
            hid[k, :, at] = hiddens[k]
            total = jnp.sum(r_hidden, axis=0, keepdims=True)
            sums = total if sums is None else sums + total
        gb_ref[:, at] = jnp.broadcast_to(sums, (8, tile))
        grad = (mm(n2_ref[...], hiddens[0], TN) + mm(n2o_ref[...], hiddens[1], TN)).astype(BF16)
        if first:
            ge[:, at] = grad[: width // 2]
            ge_low[:, at] = grad[width // 2 :]
        else:
            ge[:, at] = grad
        gr[at, :] = (
            mm(actives[0], cot_ref[...], TN) + mm(actives[1], coto_ref[...], TN)
        ).astype(BF16)
        return carry

    lax.fori_loop(0, 2, step, 0)
    flush(ge, gr)
    if first:
        flush(ge_low)
    ready(base_ref)
    out_ref[...] = base_ref[...] + mm(act[0], wr[...], NN)
    flush(out_ref)
    dn = mm(hid[0], we[...], NT)
    if first:
        dn_ref[...] = dn
        outo_ref[...] = mm(act[1], wr[...], NN).astype(BF16)
        dno_ref[...] = mm(hid[1], we[...], NT).astype(BF16)
    else:
        dn_ref[...] = back_ref[...] + dn
        flush(dn_ref)
        outo_ref[...] = (baseo_ref[...].astype(F32) + mm(act[1], wr[...], NN)).astype(BF16)
        flush(outo_ref)
        dno_ref[...] = (backo_ref[...].astype(F32) + mm(hid[1], we[...], NT)).astype(BF16)


def middle_kernel(
    heads, slots, parts, meta, dn_ref, dnin_ref, middle_ref, cot_ref, p_ref, mixed_ref, den_ref, fq_ref,
    wo, gm_ref, ratt_ref, raug_ref, g_ref, small_ref, total, rmix,
):
    cols = fq_ref.shape[1] // slots
    ready(middle_ref, dn_ref, dnin_ref, cot_ref)
    normal, scale = norm_parts(middle_ref[...])
    gy = dn_ref[...] + dnin_ref[...].astype(F32)
    cot = cot_ref[...].astype(F32)
    g_middle = cot + norm_back(gy, normal, scale, p_ref[2:3])
    gm_ref[...] = g_middle
    r_att = g_middle.astype(BF16)
    ratt_ref[...] = r_att
    flush(gm_ref, ratt_ref)
    small_ref[...] = jnp.concatenate(
        [
            jnp.sum(gy * normal, axis=0, keepdims=True),
            jnp.sum(gy, axis=0, keepdims=True),
            jnp.sum(r_att.astype(F32), axis=0, keepdims=True),
            jnp.sum(cot, axis=0, keepdims=True),
            jnp.zeros((4, gy.shape[1]), F32),
        ],
        axis=0,
    )
    ready(wo)
    rmix[...] = mm(wo[...], r_att, NT).astype(BF16)
    total[...] = jnp.zeros_like(total)
    ready(mixed_ref, den_ref, fq_ref)

    def head(h, carry):
        rows = pl.ds(pl.multiple_of(h * 64, 64), 64)
        rm = rmix[rows, :].astype(F32)
        inverse = 1.0 / den_ref[pl.ds(pl.multiple_of(h * 8, 8), 8), :][0:1]
        rn = (rm * inverse).astype(BF16)
        rd = -jnp.sum(rm * mixed_ref[rows, :].astype(F32), axis=0, keepdims=True) * inverse
        ra = aug_rows(rn, rd)
        raug_ref[pl.ds(pl.multiple_of(h * AUG, 16), AUG), :] = ra
        fq = fq_ref[pl.ds(pl.multiple_of(h * 128, 128), 128), :]
        for s in range(slots):
            part = slice(s * cols, (s + 1) * cols)
            state = mm(ra[:, part], fq[:, part], NT)
            total[s ^ meta[4], pl.ds(pl.multiple_of(h * KEEP, 8), KEEP), :] = state[:KEEP]
        return carry

    lax.fori_loop(0, heads, head, 0, unroll=UNROLL)
    spread_states(total, g_ref, parts, g_ref.shape[2])
    flush(g_ref, raug_ref)


def logits_back(p_both, g_both):
    p1, p2 = p_both[:64].astype(F32), p_both[64:].astype(F32)
    g1, g2 = g_both[:64], g_both[64:]
    s1 = jnp.sum(p1 * g1, axis=0, keepdims=True)
    s2 = jnp.sum(p2 * g2, axis=0, keepdims=True)
    return (p1 * (g1 - s1) - p2 * (g2 - s2)).astype(BF16)


def query_back_kernel(
    heads, slots, parts, meta, c_ref, raug_ref, fq_ref, qkv_ref, map_ref, mixed_ref, ratt_ref,
    rq_ref, gmap_ref, g0, g1, g2, g3, total,
):
    cols = fq_ref.shape[1] // slots
    ready(c_ref)
    collect_states(c_ref, total, parts, c_ref.shape[2])
    ready(raug_ref, fq_ref, qkv_ref)

    def head(h, carry):
        ra = raug_ref[pl.ds(pl.multiple_of(h * AUG, 16), AUG), :]
        fq = fq_ref[pl.ds(pl.multiple_of(h * 128, 128), 128), :]
        pieces = []
        for s in range(slots):
            part = slice(s * cols, (s + 1) * cols)
            c = total[s ^ meta[4], pl.ds(pl.multiple_of(h * KEEP, 8), AUG), :].astype(BF16)
            pieces.append(mm(c, ra[:, part], TN))
        r_fq = jnp.concatenate(pieces, axis=1).astype(BF16).astype(F32)
        r_l = logits_back(fq, r_fq)
        rows = pl.ds(pl.multiple_of(h * 64, 64), 64)
        rq_ref[rows, :] = mm(map_ref[h], r_l, NN).astype(BF16)
        gmap_ref[h] = mm(qkv_ref[rows, :], r_l, NT)
        return carry

    lax.fori_loop(0, heads, head, 0, unroll=UNROLL)
    flush(rq_ref, gmap_ref)
    ready(mixed_ref, ratt_ref)
    rows = g0.shape[0]
    for j, g in enumerate((g0, g1, g2, g3)):
        mixed = mixed_ref[pl.ds(pl.multiple_of(meta[j] * rows, 64), rows), :]
        g[...] = mm(mixed, ratt_ref[...], NN).astype(BF16)
        flush(g)


def key_back_kernel(
    heads, slots, parts, meta, d_ref, fk_ref, qkv_ref, map_ref, rq_ref, n_ref,
    rp_ref, gmap_ref, g1, g3, total,
):
    width = heads * 64
    cols = fk_ref.shape[1] // slots
    collect_states(d_ref, total, parts, d_ref.shape[2])
    ready(fk_ref, qkv_ref, rq_ref)
    rp_ref[0:width, :] = rq_ref[...]

    def head(h, carry):
        fk = fk_ref[pl.ds(pl.multiple_of(h * 128, 128), 128), :]
        v = qkv_ref[pl.ds(pl.multiple_of(width + h * 64, 64), 64), :]
        va = aug_rows(v, 1.0)
        pieces = []
        for s in range(slots):
            part = slice(s * cols, (s + 1) * cols)
            d = total[s ^ meta[4], pl.ds(pl.multiple_of(h * KEEP, 8), AUG), :].astype(BF16)
            pieces.append(mm(d, va[:, part], TN))
            rv = mm(d[:64], fk[:, part], NN).astype(BF16)
            rp_ref[pl.ds(pl.multiple_of(2 * width + h * 64, 64), 64), part] = rv
        r_fk = jnp.concatenate(pieces, axis=1).astype(BF16).astype(F32)
        r_l = logits_back(fk, r_fk)
        rows = pl.ds(pl.multiple_of(width + h * 64, 64), 64)
        rp_ref[rows, :] = mm(map_ref[h], r_l, NN).astype(BF16)
        keys = qkv_ref[pl.ds(pl.multiple_of(h * 64, 64), 64), :]
        gmap_ref[h] = mm(keys, r_l, NT)
        return carry

    lax.fori_loop(0, heads, head, 0, unroll=UNROLL)
    flush(rp_ref, gmap_ref)
    ready(n_ref)
    span = g1.shape[0]
    for j, g in ((1, g1), (3, g3)):
        rp = rp_ref[pl.ds(pl.multiple_of(meta[j] * span, 64), span), :]
        g[...] = mm(rp, n_ref[...], NN).astype(BF16)
        flush(g)


def project_grad_kernel(meta, rp_ref, n_ref, in0, in2, go0, go0_in, go2, go2_in, own, cross):
    span = in0.shape[0]
    ready(rp_ref, n_ref, in0, in2, go0, go0_in, go2, go2_in)
    for j, more, go, go_in, out in ((2, in2, go2, go2_in, cross), (0, in0, go0, go0_in, own)):
        rp = rp_ref[pl.ds(pl.multiple_of(meta[j] * span, 64), span), :]
        out[:span, :] = (mm(rp, n_ref[...], NN) + more[...].astype(F32)).astype(BF16)
        out[span:, :] = (go[...].astype(F32) + go_in[...].astype(F32)).astype(BF16)
        flush(out)


def input_kernel(
    heads, meta, rp_ref, x_ref, p_ref, gm_ref, out_ref, outin_ref, two_ref, ebo_ref, ebc_ref,
    mq_ref, mk_ref, w0, w1, w2, w3, dx_ref, full_ref, b0, b1, b2, b3, pack,
):
    ready(out_ref, outin_ref)
    full_ref[...] = out_ref[...] + outin_ref[...].astype(F32) + p_ref[5:6]
    flush(full_ref)
    span, width = w0.shape
    shard = width // 4
    own_heads = heads // 4
    ones = jnp.ones((8, x_ref.shape[0]), BF16)
    pack[...] = jnp.zeros_like(pack)
    gy = None
    ready(rp_ref, w0, w1, w2, w3, x_ref, gm_ref)
    for j, w in enumerate((w0, w1, w2, w3)):
        rp = rp_ref[pl.ds(pl.multiple_of(meta[j] * span, 64), span), :]
        part = mm(rp, w[...], TN)
        gy = part if gy is None else gy + part
        pack[meta[j], 8:16, :span] = mm(ones, rp, NT)
    ready(ebo_ref, ebc_ref, two_ref)
    pack[meta[0], 16:24, :] = ebo_ref[...]
    pack[meta[2], 16:24, :] = ebc_ref[...]
    normal, scale = norm_parts(x_ref[...].astype(F32))
    dx_ref[...] = gm_ref[...] + norm_back(gy, normal, scale, p_ref[0:1])
    flush(dx_ref)
    ready(mq_ref, mk_ref)
    lines = [
        jnp.sum(gy * normal, axis=0, keepdims=True),
        jnp.sum(gy, axis=0, keepdims=True),
        two_ref[0:1], two_ref[1:2], two_ref[2:3], two_ref[3:4],
    ]
    for i in range(4):
        cut = slice(i * shard, (i + 1) * shard)
        for k, line in enumerate(lines):
            pack[i, k : k + 1, :shard] = line[:, cut]
        for base, ref in ((24, mq_ref), (40, mk_ref)):
            for k in range(4):
                for h in range(own_heads):
                    at = k * shard + h * 64
                    pack[i, base : base + 16, at : at + 64] = ref[
                        i * own_heads + h, 16 * k : 16 * k + 16, :
                    ]
    for j, b in enumerate((b0, b1, b2, b3)):
        b[...] = pack[meta[j]].astype(BF16)


def unpack_kernel(rest_ref, g1, s1, g2, s2, bo, br, pb, eb, mq, mk):
    shard = g1.shape[1]
    own_heads = mq.shape[0]
    for k, ref in enumerate((g1, s1, g2, s2, bo, br)):
        ref[...] = rest_ref[k : k + 1, :shard]
    pb[...] = rest_ref[8:9, : pb.shape[1]]
    eb[...] = rest_ref[16:17, :]
    for base, ref in ((24, mq), (40, mk)):
        for k in range(4):
            for h in range(own_heads):
                at = k * shard + h * 64
                ref[h, 16 * k : 16 * k + 16, :] = rest_ref[base : base + 16, at : at + 64]


def line1(a):
    return a.reshape(-1)


def core_swap(a):
    return lax.ppermute(a, "fsdp", CORE)


def cross_swap(a):
    return lax.ppermute(a, "fsdp", CROSS)


def after(value, *others):
    return lax.optimization_barrier((value, *others))[0]


def spread(shard, cross):
    return [shard, core_swap(shard), cross, core_swap(cross)]


def add(a, b):
    return (a.astype(F32) + b.astype(F32)).astype(BF16)


def rows_sum(parts, start, size):
    out = None
    for offset, part in parts:
        if isinstance(part, tuple):
            part, offset = jnp.where(start + offset < part[0].shape[0], *part), -start
        piece = lax.dynamic_slice_in_dim(part, start + offset, size, 0).astype(F32)
        out = piece if out is None else out + piece
    return out.astype(BF16)


class Reduction:
    def __init__(self, parts, nctx, place):
        self.parts = [(0, part) for part in parts]
        self.rows, self.nctx, self.place = parts[0].shape[0], nctx, place
        self.groups = [[bit] for bit in range(nctx.bit_length() - 1)]

    def member(self, group):
        return sum(((self.place >> bit) & 1) << k for k, bit in enumerate(group))

    def send(self, value, group, other):
        flip = sum(((other >> k) & 1) << bit for k, bit in enumerate(group))
        return lax.ppermute(value, "ctx", [(i, i ^ flip) for i in range(self.nctx)])

    def scatter(self, level):
        group = self.groups[level]
        count = 1 << len(group)
        mine = self.member(group)
        self.rows //= count
        self.sent = [
            rows_sum(self.parts, (mine ^ d) * self.rows, self.rows) for d in range(1, count)
        ]
        got = [self.send(sent, group, d) for d, sent in enumerate(self.sent, 1)]
        self.parts = [
            (0, jnp.where(mine == 0, *part)) if isinstance(part, tuple)
            else (offset + mine * self.rows, part)
            for offset, part in self.parts
        ]
        self.fresh = len(got)
        self.parts += [(0, g) for g in got]
        return got

    def hold(self, *others):
        last = self.parts[-self.fresh :]
        held = lax.optimization_barrier((tuple(part for _, part in last), others))[0]
        self.parts[-self.fresh :] = [(at, part) for (at, _), part in zip(last, held)]

    def own(self):
        self.cur = rows_sum(self.parts, 0, self.rows)

    def spread(self, level):
        group = self.groups[level]
        self.others = [self.send(self.cur, group, d) for d in range(1, 1 << len(group))]
        self.level = level
        return self.others

    def join(self, *others):
        group = self.groups[self.level]
        parts = [self.cur, *self.others]
        if others:
            parts = list(lax.optimization_barrier((tuple(parts), others))[0])
        for k, bit in enumerate(group):
            swap = ((self.place >> bit) & 1) == 1
            parts = [
                jnp.where(swap, parts[j ^ (1 << k)], parts[j]) for j in range(len(parts))
            ]
        self.cur = jnp.concatenate(parts, axis=0)

    def deep(self, first):
        for level in range(first, len(self.groups)):
            self.scatter(level)
        self.own()
        for level in reversed(range(first, len(self.groups))):
            self.spread(level)
            self.join()


def straighten(parts, mine):
    a, b, c, d = parts
    odd = (mine & 1) == 1
    upper = (mine & 2) == 2
    a, b = jnp.where(odd, b, a), jnp.where(odd, a, b)
    c, d = jnp.where(odd, d, c), jnp.where(odd, c, d)
    return [
        jnp.where(upper, c, a), jnp.where(upper, d, b),
        jnp.where(upper, a, c), jnp.where(upper, b, d),
    ]


def exchange(a):
    return lax.all_to_all(a, "ctx", 0, 0, tiled=True)


def body(
    tokens, cotangent, pair_table, seq_ids, first_gain, first_shift, project_weight, project_bias,
    feature_query, feature_key, output_weight, output_bias, second_gain, second_shift,
    expand_weight, expand_bias, reduce_weight, reduce_bias,
):
    x = tokens[0]
    cot = cotangent[0]
    rows_n, width = x.shape
    heads = width // feature_query.shape[1]
    own_heads = feature_query.shape[0]
    slots = pair_table.shape[2]
    nctx = lax.axis_size("ctx")
    place = lax.axis_index("ctx")
    mine = lax.axis_index("fsdp")
    span = project_weight.shape[1]
    hidden_own = expand_weight.shape[1]
    shard = width // 4
    wide = heads * 128

    project_t = project_weight.T
    cross_project = cross_swap(project_t)
    vector = jnp.concatenate(
        [first_gain, first_shift, second_gain, second_shift, output_bias, reduce_bias,
         project_bias, expand_bias]
    )
    room = -vector.shape[0] % 1024
    vector = jnp.concatenate([vector, jnp.zeros((room,), BF16)]).reshape(-1, 64)
    map_rows = own_heads * 64
    pack = jnp.concatenate(
        [feature_query.reshape(-1, 64), feature_key.reshape(-1, 64), vector]
    )
    packs = spread(pack, cross_swap(pack))
    ordered = straighten(packs, mine)
    query_map = jnp.concatenate([p[:map_rows] for p in ordered]).reshape(heads, 64, 64)
    key_map = jnp.concatenate([p[map_rows : 2 * map_rows] for p in ordered]).reshape(heads, 64, 64)
    vectors = jnp.stack([p[2 * map_rows :] for p in ordered]).reshape(4, -1).astype(F32)
    params = vectors[:, : 6 * shard].reshape(4, 6, shard).transpose(1, 0, 2).reshape(6, width)
    project_line = vectors[:, 6 * shard : 6 * shard + span]
    expand_line = vectors[:, 6 * shard + span : 6 * shard + span + hidden_own]
    project_core = core_swap(project_t)
    project_far = core_swap(cross_project)
    projects = [project_t, project_core, cross_project, project_far]
    near_first = jnp.concatenate([expand_weight, output_weight])
    cross_first = cross_swap(after(near_first, cross_project))
    core_output = core_swap(output_weight)
    cross_reduce = cross_swap(after(reduce_weight, cross_first))
    cot_other = core_swap(cot)

    positions = pair_table[0, 0]
    swap = (positions[0] > positions[1]).astype(jnp.int32)
    meta = jnp.stack([mine, mine ^ 1, mine ^ 2, mine ^ 3, swap]).astype(jnp.int32)
    ids = seq_ids[0]
    same = (ids[1:] == ids[:-1]).astype(F32)
    none = jnp.zeros((1,), F32)
    keep = jnp.concatenate([none, same])
    keep_next = jnp.concatenate([same, none])

    rows_per = -(-(heads * KEEP) // (nctx * 16)) * 16
    state_shape = shaped((nctx, slots, rows_per, 128), BF16)
    total = pltpu.VMEM((slots, nctx * rows_per, 128), F32)
    wo_scratch = pltpu.VMEM((width, width), BF16)
    low = shaped((rows_n, width), BF16)
    full = shaped((rows_n, width))
    table = shaped((width, rows_n), BF16)
    square = shaped((heads, 64, 64))

    n1, near = call(
        near_kernel, [low, shaped((2 * span, rows_n), BF16)], "shvaav",
        [meta, x, params, projects[0], projects[1], project_line], "project_near", (), "hv",
    )
    (qkv,) = call(
        far_kernel, [shaped((3 * width, rows_n), BF16)], "shvaav",
        [meta, n1, near, projects[2], projects[3], project_line], "project_far",
    )
    fk, states = call(
        functools.partial(key_kernel, heads, slots, nctx),
        [shaped((wide, rows_n), BF16), state_shape], "svv",
        [meta, qkv, key_map], "keys", [total], "hh",
    )
    arrived = exchange(states)
    (fq,) = call(
        functools.partial(query_kernel, heads), [shaped((wide, rows_n), BF16)], "vv",
        [after(qkv, states), query_map], "queries", (), "h", flops=10**12,
    )
    (running,) = call(
        functools.partial(scan_kernel, nctx, False), [state_shape], "sv",
        [keep, after(arrived, cross_first)], "scan", (), "h",
    )
    carried = exchange(running)
    far_output = core_swap(after(cross_first, running)[width : width + shard])
    outputs = [output_weight, core_output, (cross_first, width, shard), far_output]
    mixed, den, middle, n2, wo = call(
        functools.partial(attend_kernel, heads, slots, nctx),
        [table, shaped((heads * 8, rows_n)), full, low, shaped((width, width), BF16)],
        "svhhhvavv", [meta, carried, fq, x, *outputs, params], "attend",
        [total], "hhhvh",
    )
    n2_other = core_swap(n2)

    def mlp(first, base, w_in, w_out, more, name):
        half = shaped((width // 2, hidden_own), BF16)
        grads = [half, half] if first else [shaped((width, hidden_own), BF16)]
        return call(
            functools.partial(mlp_kernel, first),
            [full, full, low, low, *grads, shaped((hidden_own, width), BF16),
             shaped((8, hidden_own))],
            "saaaaaa" + ("h" if first else "v") + "v" + "v" * len(more),
            [meta, n2, w_in, n2_other, cot, w_out, cot_other, base, expand_line, *more], name,
            [pltpu.VMEM((2, rows_n, hidden_own), BF16)] * 2,
            "vvvvhhhv" if first else "hhhvhhv", 48,
        )

    out1, dn1, out1_o, dn1_o, ge_top, ge_low, gr_cross, gb_cross = mlp(
        True, middle, (cross_first, 0, width), cross_reduce, [], "mlp_far"
    )
    top_in = cross_swap(ge_top)
    low_in = cross_swap(after(ge_low, top_in))
    out2, dn2, out2_o, dn2_o, ge_own, gr_own, gb_own = mlp(
        False, out1, expand_weight, reduce_weight, [dn1, out1_o, dn1_o], "mlp_near"
    )
    dn2_in = core_swap(after(dn2_o, top_in))

    g_middle, r_att, raug, g_states, small_two = call(
        functools.partial(middle_kernel, heads, slots, nctx),
        [full, low, shaped((heads * AUG, rows_n), BF16), state_shape, shaped((8, width))],
        "shahavhhhh",
        [meta, dn2, dn2_in, middle, cot, params, mixed, den, fq, wo], "middle",
        [total, pltpu.VMEM((width, rows_n), BF16)], "hhhhv",
    )
    g_arrived = exchange(g_states)
    gr_in = cross_swap(after(gr_cross, low_in))
    out2_in = core_swap(after(out2_o, g_states))
    rq, g_query_map, *go = call(
        functools.partial(query_back_kernel, heads, slots, nctx),
        [table, square] + [shaped((shard, width), BF16)] * 4,
        "sahhavhh", [meta, carried, raug, fq, (qkv, 0, width), query_map, mixed, r_att], "query_back",
        [total], "hhhhhh",
    )
    (g_running,) = call(
        functools.partial(scan_kernel, nctx, True), [state_shape], "sv",
        [keep_next, after(g_arrived, rq, low_in)], "scan_back", (), "h",
    )
    g_carried = exchange(g_running)
    top_in, low_in = lax.optimization_barrier((top_in, low_in, g_running))[:2]
    sum_e = Reduction([ge_own, (top_in, low_in)], nctx, place)
    e_got = sum_e.scatter(0)
    sum_r = Reduction([gr_own, after(gr_in, g_running)], nctx, place)
    r_got = sum_r.scatter(0)
    go_far, go_core = core_swap(after(go[3], g_running)), core_swap(after(go[1], g_running))
    rp, g_key_map, gp1, gp3 = call(
        functools.partial(key_back_kernel, heads, slots, nctx),
        [shaped((3 * width, rows_n), BF16), square] + [shaped((span, width), BF16)] * 2,
        "svhavhh", [meta, after(g_carried, sum_e.sent, sum_r.sent), fk, (qkv, width, 2 * width), key_map, rq, n1],
        "key_back", [total], "hhhh",
    )
    gp3_in, gp1_in = core_swap(after(gp3, e_got)), core_swap(after(gp1, e_got))
    p_own, p_cross = call(
        project_grad_kernel, [shaped((width, width), BF16)] * 2, "shhaahaha",
        [meta, rp, n1, gp1_in, gp3_in, go[0], go_core, go[2], go_far], "project_grad", (), "hh",
    )
    p_in = cross_swap(p_cross)
    sum_e.hold(p_own)
    sum_e.scatter(1)
    small = shaped((64, width), BF16)
    dx, layer_out, own_s, core_s, cross_s, far_s = call(
        functools.partial(input_kernel, heads), [full, full, small, small, small, small],
        "shhvhhaaaahhaaaa",
        [meta, rp, after(x, p_own, sum_e.sent), params, g_middle, out2, out2_in, small_two,
         gb_own, gb_cross, g_query_map, g_key_map, *projects],
        "input", [pltpu.VMEM((4, 64, width), F32)], "hhvvvv",
    )
    far_in, core_in = core_swap(far_s), core_swap(core_s)
    cross_in = cross_swap(add(cross_s, far_in))
    small_own = add(own_s, core_in)
    sum_e.hold(far_in, core_in)
    e_got = sum_e.scatter(2)
    sum_r.hold(far_in, core_in)
    r_got = sum_r.scatter(1)
    sum_p = Reduction([p_own, p_in], nctx, place)
    p_got = sum_p.scatter(0)
    sum_e.hold(sum_p.sent)
    sum_r.hold(sum_p.sent)
    sum_e.deep(3)
    e_got = sum_e.spread(2)
    r_got = sum_r.scatter(2)
    sum_p.hold(e_got, r_got)
    sum_p.scatter(1)
    sum_e.join(sum_p.sent)
    e_got = sum_e.spread(1)
    sum_r.hold(sum_p.sent)
    sum_r.deep(3)
    r_got = sum_r.spread(2)
    sum_p.hold(e_got, r_got)
    sum_p.scatter(2)
    sum_e.join(sum_p.sent)
    e_got = sum_e.spread(0)
    sum_r.join(sum_p.sent)
    r_got = sum_r.spread(1)
    sum_p.deep(3)
    sum_r.join(sum_p.cur)
    r_got = sum_r.spread(0)
    sum_p.spread(2)
    sum_p.join(e_got)
    sum_p.spread(1)
    sum_p.join(r_got)
    sum_p.spread(0)
    sum_p.join()
    sum_e.join()
    sum_r.join()
    g_expand, g_reduce, g_project = sum_e.cur, sum_r.cur, sum_p.cur
    rest = small_own.astype(F32) + cross_in.astype(F32)
    for level in range(len(sum_p.groups)):
        low_rest = rest.astype(BF16)
        rest = low_rest.astype(F32) + sum_p.send(low_rest, sum_p.groups[level], 1).astype(F32)
    g_output = g_project[span : span + shard]
    line = shaped((1, shard))
    g1, s1, g2, s2, bo, br, pb, eb, mq, mk = call(
        unpack_kernel,
        [line] * 6 + [shaped((1, span)), shaped((1, hidden_own))]
        + [shaped((own_heads, 64, 64))] * 2, "v", [rest], "unpack",
    )
    return (
        layer_out[None], dx[None], line1(g1), line1(s1), g_project[:span].T.astype(F32), line1(pb), mq, mk,
        g_output.astype(F32), line1(bo), line1(g2), line1(s2), g_expand.astype(F32), line1(eb),
        g_reduce.astype(F32), line1(br),
    )


def solution(mesh):
    row = P("fsdp", "ctx", None)
    vec = P("fsdp")
    maps = P("fsdp", None, None)
    in_specs = (
        row, row, row, P("fsdp", None), vec, vec, P(None, "fsdp"), vec, maps, maps,
        P("fsdp", None), vec, vec, vec, P(None, "fsdp"), vec, P("fsdp", None), vec,
    )
    out_specs = (
        row, row, vec, vec, P(None, "fsdp"), vec, maps, maps, P("fsdp", None), vec, vec, vec,
        P(None, "fsdp"), vec, P("fsdp", None), vec,
    )
    return jax.shard_map(body, mesh=mesh, in_specs=in_specs, out_specs=out_specs, check_vma=False)
```
